256 devices in a mesh: cell: 16 (over z_lo, x, core), gene: 16 (over y, z_hi).
Axes of the slice: x: 4, y: 4, z: 8 (z_hi: 4, z_lo: 2; z = z_hi * 2 + z_lo), core: 2. Of those that a mesh axis runs over, the one named last changes fastest.
Arguments:
- counts: int32 [16384, 8192], P('cell', 'gene'), may hold values from 0 to 4000, as said below
Outputs:
- gene_gram: float32 [8192, 8192], P('gene', 'cell')
The draws below stay inside these ranges and needn't reach their ends.
Inputs may be any that keep to these rules, and one draw needn't show every extreme that they name: `counts`: every cell and every gene has a positive count somewhere.
All inputs are finite; a program needn't handle non-finite values.
Results may differ from the reference program's by a relative error of at most 0.00054.
Values may be sent and summed in bfloat16 or wider, within the bound.
A program may use at most 128 MiB of HBM per device.

```python
import jax
import jax.numpy as jnp
from jax import lax

G = 8192
CELLS = 16384


def draw_counts(key, part):
    subkeys = jax.random.split(key, 8)
    cell_index = jnp.arange(CELLS, dtype=jnp.int32)[:, None]
    gene_index = jnp.arange(G, dtype=jnp.int32)[None, :]
    cell_scale = jax.random.randint(subkeys[0], (CELLS, 1), 1, 3, dtype=jnp.int32)
    gene_scale = jax.random.randint(subkeys[1], (1, G), 1, 3, dtype=jnp.int32)
    cell_level = 1 + 3 * cell_index // CELLS
    gene_level = 1 + 3 * gene_index // G
    program = jax.random.randint(subkeys[2], (CELLS, 1), 0, 8, dtype=jnp.int32)
    module = jax.random.randint(subkeys[3], (1, G), 0, 8, dtype=jnp.int32)
    boost = 1 + (program == module).astype(jnp.int32)
    upper = cell_scale * gene_scale * cell_level * gene_level * boost
    lower = ((gene_index - cell_index) % 16 == 0).astype(jnp.int32)
    base = jax.random.randint(subkeys[4], (CELLS, G), lower, upper + 1, dtype=jnp.int32)
    spike_gene = jax.random.randint(subkeys[5], (CELLS, 1), 0, G, dtype=jnp.int32)
    spike_cell = (jax.random.randint(subkeys[6], (CELLS, 1), 0, 16, dtype=jnp.int32) == 0) | (cell_index == 0)
    spike_size = jax.random.randint(subkeys[7], (CELLS, 1), 1000, 4001, dtype=jnp.int32)
    spike_size = jnp.where(cell_index == 0, jnp.int32(4000), spike_size)
    spiked = spike_cell & (gene_index == spike_gene)
    return jnp.where(spiked, spike_size, base)


def setup_inputs(seed: int = 0) -> dict:
    streams_of = jax.random.split(jax.random.key(seed), 2)
    return {
        "counts": draw_counts(jax.random.fold_in(streams_of[1], 71), 0),
    }


def reference(counts):
    values = counts.astype(jnp.float32)
    depths = lax.optimization_barrier(jnp.sum(values, axis=1))
    gene_totals = lax.optimization_barrier(jnp.sum(values, axis=0))
    grand_total = jnp.sum(depths)
    expected = depths[:, None] * gene_totals[None, :] / grand_total
    scaled = (values - expected) / jnp.sqrt(expected + expected * expected / 100.0)
    ceiling = jnp.sqrt(jnp.float32(CELLS))
    residuals = jnp.clip(scaled, -ceiling, ceiling).astype(jnp.bfloat16)
    wide = residuals.astype(jnp.float32)
    product = lax.dot_general(wide, wide, (((0,), (0,)), ((), ())), precision=lax.Precision.HIGHEST, preferred_element_type=jnp.float32)
    return product / jnp.float32(CELLS)
```

```python
import functools

import jax
import jax.numpy as jnp
from jax import lax
from jax.experimental import pallas as pl
from jax.experimental.pallas import tpu as pltpu
from jax.sharding import PartitionSpec as P

MESH = pl.DeviceIdType.MESH
R = 4
NC = 16
YP, ZP, T, Y2, ZM = range(5)
OWN = -1
OFFSET = {OWN: (0, 0), YP: (1, 0), ZP: (0, 1), T: (3, 3), Y2: (2, 3), ZM: (0, 3)}
OWN_PAIRS = (YP, ZP, T, Y2)
PAIRS = (
    (OWN, OWN, False),
    (OWN, YP, True),
    (OWN, ZP, True),
    (OWN, T, True),
    (OWN, Y2, True),
    (YP, ZP, True),
    (ZM, Y2, False),
    (ZP, T, True),
    (ZP, Y2, False),
    (ZP, ZM, False),
)
MIRRORED = ((3, 0), (0, 3), (1, 1), (2, 1), (1, 3), (1, 2))


def plan():
    rounds = []
    for r in range(R):
        groups, n = [], 0

        def add(pair, count, i, j, along):
            nonlocal n
            groups.append((pair, n, count, i, j, along))
            n += count

        if r == 0:
            for i in range(R):
                add(0, R, i, 0, "j")
        for pair in range(1, 5):
            add(pair, R, 0, r, "i")
        for pair in range(5, 10):
            add(pair, r + 1, r, 0, "j")
            if r:
                add(pair, r, 0, r, "i")
        rounds.append((n, groups))
    return rounds


ROUNDS = plan()


def gene_at(y, z, offset):
    return ((y + offset[0]) % 4) * 4 + (z + offset[1]) % 4


def kernel(counts, out, *scratch):
    (vt, colbuf, rowbuf, totbuf, own, got, final), rest = scratch[:7], scratch[7:]
    prods, rest = rest[:R], rest[R:]
    halves, rest = rest[:R], rest[R:]
    early, rest = rest[:R], rest[R:]
    late, rest = rest[:R], rest[R:]
    pieces, rest = rest[:R], rest[R:]
    (stat_send, stat_recv, in_send, in_recv, rs_send, rs_recv, fin_send, fin_own, fin_recv) = rest
    genes, cells = own.shape[0] * own.shape[1], own.shape[2]
    S = genes // R
    nj = cells // 128
    c, g = lax.axis_index("cell"), lax.axis_index("gene")
    zl, x, core = c // 8, (c // 2) % 4, c % 2
    y, z = g // 4, g % 4
    pos = 8 * core + 2 * x + zl

    def cell_of(zl_, x_, core_):
        return {"cell": zl_ * 8 + x_ * 2 + core_}

    xp, xm = (x + 1) % 4, (x + 3) % 4
    to_xp, to_xm = cell_of(zl, xp, core), cell_of(zl, xm, core)
    to_core, to_zl = cell_of(zl, x, 1 - core), cell_of(1 - zl, x, core)
    to_yp, to_ym = {"gene": gene_at(y, z, (1, 0))}, {"gene": gene_at(y, z, (3, 0))}
    to_zp, to_zm = {"gene": gene_at(y, z, (0, 1))}, {"gene": gene_at(y, z, (0, 3))}

    def remote(src, dst, ssem, rsem, device):
        return pltpu.make_async_remote_copy(
            src_ref=src, dst_ref=dst, send_sem=ssem, recv_sem=rsem, device_id=device, device_id_type=MESH
        )

    barrier = pltpu.get_barrier_semaphore()
    for k in range(1, NC):
        pl.semaphore_signal(barrier, inc=1, device_id={"cell": (c + k) % NC}, device_id_type=MESH)
        pl.semaphore_signal(barrier, inc=1, device_id={"gene": (g + k) % NC}, device_id_type=MESH)

    def local(j, acc):
        v = counts[pl.ds(j * 128, 128), :].astype(jnp.float32)
        t = v.T
        vt[j] = t
        rowbuf[g, pl.ds(j, 1), :] = jnp.sum(t, axis=0, keepdims=True)
        return acc + jnp.sum(v, axis=0, keepdims=True)

    nq = genes // 128
    colsum = lax.fori_loop(0, nj, local, jnp.zeros((1, genes), jnp.float32))
    colbuf[c] = jnp.zeros((8, 128), jnp.float32)
    for q in range(nq):
        colbuf[c, q : q + 1, :] = colsum[:, q * 128 : (q + 1) * 128]
    pl.semaphore_wait(barrier, 2 * (NC - 1))

    def spread(buf, axis, me, k):
        for d in range(1, NC):
            remote(buf.at[me], buf.at[me], stat_send.at[k], stat_recv.at[k], {axis: (me + d) % NC}).start()

    def others(buf, sem):
        return pltpu.make_async_copy(buf.at[0 : NC - 1], buf.at[0 : NC - 1], sem)

    spread(colbuf, "cell", c, 0)
    spread(rowbuf, "gene", g, 1)
    others(colbuf, stat_recv.at[0]).wait()
    totals = jnp.sum(colbuf[...], axis=0)
    totbuf[g] = jnp.broadcast_to(jnp.sum(totals, axis=0, keepdims=True), (8, 128))
    spread(totbuf, "gene", g, 2)
    gcol = [jnp.broadcast_to(totals[q : q + 1, :], (128, 128)).T for q in range(nq)]
    others(rowbuf, stat_recv.at[1]).wait()
    depths = jnp.sum(rowbuf[...], axis=0)
    others(totbuf, stat_recv.at[2]).wait()
    grand = jnp.sum(jnp.sum(totbuf[...], axis=0)[0:1, :])
    share = depths / grand
    ceiling = float(NC * cells) ** 0.5
    for q in range(nq):
        r, o = (q * 128) // S, (q * 128) % S
        for j in range(nj):
            v = vt[j, q * 128 : (q + 1) * 128, :]
            e = gcol[q] * share[j : j + 1, :]
            s = (v - e) * lax.rsqrt(e + e * e / 100.0)
            own[r, o : o + 128, j * 128 : (j + 1) * 128] = jnp.clip(s, -ceiling, ceiling).astype(jnp.bfloat16)

    def chunk(src, r, b, device):
        return remote(src, got.at[r, b], in_send.at[b, r], in_recv.at[b, r], device)

    def own_to(b, r, device):
        return chunk(own.at[r], r, b, device)

    def relay(a, b, r, device):
        return chunk(got.at[r, a], r, b, device)

    for r in range(R):
        own_to(ZM, r, to_zp).start()
        own_to(ZP, r, to_zm).start()
        if r < 1:
            own_to(YP, r, to_ym).start()

    def arrived(b, r):
        own_to(b, r, to_zp).wait_recv()

    def nt(a, b):
        return lax.dot_general(a, b, (((1,), (1,)), ((), ())), preferred_element_type=jnp.float32)

    def put(r, t, tile):
        prods[r][t] = tile.reshape(8, S // 8, S)

    def compute(r):
        base = {}
        for pair, t0, n, i, j, along in ROUNDS[r][1]:
            base[pair, along, i if along == "j" and pair == 0 else 0] = t0
        if r == 0:

            @pl.loop(0, R)
            def _(i):
                d = nt(own[i], own[...].reshape(genes, cells))
                for j in range(R):
                    put(r, base[0, "j", 0] + i * R + j, d[:, j * S : (j + 1) * S])

        @pl.loop(0, R)
        def _(i):
            d = nt(own[i], got[r, 0:4].reshape(4 * S, cells))
            for k in range(4):
                put(r, base[k + 1, "i", 0] + i, d[:, k * S : (k + 1) * S])

        @pl.loop(0, r + 1)
        def _(j):
            d = nt(got[r, ZP], got[j, T : ZM + 1].reshape(3 * S, cells))
            for k in range(3):
                put(r, base[k + 7, "j", 0] + j, d[:, k * S : (k + 1) * S])
            put(r, base[5, "j", 0] + j, nt(got[r, YP], got[j, ZP]))
            put(r, base[6, "j", 0] + j, nt(got[r, ZM], got[j, Y2]))

        if r:

            @pl.loop(0, r)
            def _(i):
                d = nt(got[i, ZP], got[r, T : ZM + 1].reshape(3 * S, cells))
                for k in range(3):
                    put(r, base[k + 7, "i", 0] + i, d[:, k * S : (k + 1) * S])
                put(r, base[5, "i", 0] + i, nt(got[i, YP], got[r, ZP]))
                put(r, base[6, "i", 0] + i, nt(got[i, ZM], got[r, Y2]))

    def rs(r, k, src, dst, device):
        return remote(src, dst, rs_send.at[r, k], rs_recv.at[r, k], device)

    def core_copy(r):
        return rs(r, 0, prods[r].at[:, pl.ds(4 * (1 - core), 4)], halves[r], to_core)

    def x_copy(r, k):
        n = ROUNDS[r][0]
        a, b, p, h = slice(0, n // 2), slice(n // 2, n), prods[r], 4 * core
        if k == "ep":
            return rs(r, 1, p.at[a, h + (x + 2) % 4], early[r].at[a], to_xp)
        if k == "em":
            return rs(r, 2, p.at[b, h + (x + 2) % 4], early[r].at[b], to_xm)
        if k == "dp":
            return rs(r, 3, p.at[b, h + xp], late[r].at[0, b], to_xp)
        if k == "dm":
            return rs(r, 4, p.at[a, h + xm], late[r].at[1, a], to_xm)
        if k == "fp":
            return rs(r, 5, p.at[a, h + xp], late[r].at[0, a], to_xp)
        return rs(r, 6, p.at[b, h + xm], late[r].at[1, b], to_xm)

    def zl_copy(r):
        s = S // 16
        return rs(r, 7, prods[r].at[:, 4 * core + x, pl.ds((1 - zl) * s, s)], pieces[r], to_zl)

    def s0(r):
        core_copy(r).start()

    def s1(r):
        n = ROUNDS[r][0]
        core_copy(r).wait_recv()

        @pl.loop(0, n)
        def _(t):
            prods[r][t, pl.ds(4 * core, 4)] = prods[r][t, pl.ds(4 * core, 4)] + halves[r][t]

        for k in ("ep", "em", "dp", "dm"):
            x_copy(r, k).start()

    def s2(r):
        n = ROUNDS[r][0]
        a, b = slice(0, n // 2), slice(n // 2, n)
        x_copy(r, "ep").wait_recv()
        prods[r][a, 4 * core + xp] = prods[r][a, 4 * core + xp] + early[r][a]
        x_copy(r, "fp").start()
        x_copy(r, "em").wait_recv()
        prods[r][b, 4 * core + xm] = prods[r][b, 4 * core + xm] + early[r][b]
        x_copy(r, "fm").start()

    def s3(r):
        for k in ("dp", "dm", "fp", "fm"):
            x_copy(r, k).wait_recv()
        prods[r][:, 4 * core + x] = prods[r][:, 4 * core + x] + late[r][0] + late[r][1]
        zl_copy(r).start()

    def final_sends(r):
        for pair, t0, n, i, j, along in ROUNDS[r][1]:
            a, b, both = PAIRS[pair]
            ga, gb = gene_at(y, z, OFFSET[a]), gene_at(y, z, OFFSET[b])
            if along == "j":
                dst = final.at[i, j : j + n, pos]
            else:
                dst = final.at[i : i + n, j, pos]
            yield pieces[r].at[t0 : t0 + n], dst, ga, gb, a == OWN
            if both:
                yield pieces[r].at[t0 : t0 + n], dst, gb, ga, False

    def s4(r):
        s = S // 16
        zl_copy(r).wait_recv()
        pieces[r][...] = pieces[r][...] + prods[r][:, 4 * core + x, pl.ds(zl * s, s)]
        k = 0
        for src, dst, row, col, maybe in final_sends(r):
            if maybe:

                @pl.when(col == c)
                def _():
                    pltpu.make_async_copy(src, dst, fin_recv).start()

                @pl.when(col != c)
                def _():
                    remote(src, dst, fin_own.at[r, k], fin_recv, {"cell": col, "gene": row}).start()

                k += 1
            else:
                remote(src, dst, fin_send, fin_recv, {"cell": col, "gene": row}).start()

    arrived(ZM, 0)
    relay(ZM, T, 0, to_yp).start()
    for r in range(R):
        if r + 1 < R:
            own_to(YP, r + 1, to_ym).start()
        arrived(T, r)
        relay(T, Y2, r, to_yp).start()
        if r + 1 < R:
            arrived(ZM, r + 1)
            relay(ZM, T, r + 1, to_yp).start()
        arrived(ZP, r)
        arrived(YP, r)
        arrived(Y2, r)
        compute(r)
        s0(r)
        if r:
            s3(r - 1)
        s1(r)
        if r:
            s4(r - 1)
        s2(r)
    s3(R - 1)
    s4(R - 1)

    pltpu.make_async_copy(final, final, fin_recv).wait()
    dy, dz = (c // 4 - y + 4) % 4, (c % 4 - z + 4) % 4
    flip = functools.reduce(jnp.logical_or, [(dy == a) & (dz == b) for a, b in MIRRORED])
    scale = 1.0 / float(NC * cells)

    def tile(i, j):
        return final[i, j].reshape(S, S) * scale

    @pl.when(flip)
    def _():
        for i in range(R):
            for j in range(R):
                out[j * S : (j + 1) * S, i * S : (i + 1) * S] = tile(i, j).T

    @pl.when(jnp.logical_not(flip))
    def _():
        for i in range(R):
            for j in range(R):
                out[i * S : (i + 1) * S, j * S : (j + 1) * S] = tile(i, j)

    for k, buf in ((0, colbuf), (1, rowbuf), (2, totbuf)):
        others(buf, stat_send.at[k]).wait()
    sent = 0
    for r in range(R):
        for b in range(5):
            own_to(b, r, to_zp).wait_send()
        core_copy(r).wait_send()
        for k in ("ep", "em", "dp", "dm", "fp", "fm"):
            x_copy(r, k).wait_send()
        zl_copy(r).wait_send()
        k = 0
        for src, dst, row, col, maybe in final_sends(r):
            if maybe:

                @pl.when(col != c)
                def _():
                    remote(src, dst, fin_own.at[r, k], fin_recv, {"cell": col, "gene": row}).wait_send()

                k += 1
            else:
                sent += src.shape[0]
    assert sent % 16 == 0
    pltpu.make_async_copy(prods[0].at[0 : sent // 16], prods[0].at[0 : sent // 16], fin_send).wait()


def body(counts):
    cells, genes = counts.shape
    S = genes // R
    ns = [n for n, _ in ROUNDS]
    f32 = jnp.float32
    dma = pltpu.SemaphoreType.DMA
    own_groups = max(sum(PAIRS[gr[0]][0] == OWN for gr in groups) for _, groups in ROUNDS)
    scratch = [
        pltpu.VMEM((cells // 128, genes, 128), f32),
        pltpu.VMEM((NC, 8, 128), f32),
        pltpu.VMEM((NC, 8, 128), f32),
        pltpu.VMEM((NC, 8, 128), f32),
        pltpu.VMEM((R, S, cells), jnp.bfloat16),
        pltpu.VMEM((R, 5, S, cells), jnp.bfloat16),
        pltpu.VMEM((R, R, 16, S // 16, S), f32),
        *[pltpu.VMEM((n, 8, S // 8, S), f32) for n in ns],
        *[pltpu.VMEM((n, 4, S // 8, S), f32) for n in ns],
        *[pltpu.VMEM((n, S // 8, S), f32) for n in ns],
        *[pltpu.VMEM((2, n, S // 8, S), f32) for n in ns],
        *[pltpu.VMEM((n, S // 16, S), f32) for n in ns],
        dma((3,)),
        dma((3,)),
        dma((5, R)),
        dma((5, R)),
        dma((R, 8)),
        dma((R, 8)),
        dma(()),
        dma((R, own_groups)),
        dma(()),
    ]
    return pl.pallas_call(
        kernel,
        out_shape=jax.ShapeDtypeStruct((genes, genes), f32),
        in_specs=[pl.BlockSpec(memory_space=pltpu.VMEM)],
        out_specs=pl.BlockSpec(memory_space=pltpu.VMEM),
        scratch_shapes=scratch,
        compiler_params=pltpu.CompilerParams(
            collective_id=0, has_side_effects=True, vmem_limit_bytes=60 * 1024 * 1024
        ),
    )(counts)


def solution(mesh):
    return jax.shard_map(
        body,
        mesh=mesh,
        in_specs=(P("cell", "gene"),),
        out_specs=P("gene", "cell"),
        check_vma=False,
    )
```

```python
import functools

import jax
import jax.numpy as jnp
from jax import lax
from jax.experimental import pallas as pl
from jax.experimental.pallas import tpu as pltpu
from jax.sharding import PartitionSpec as P

MESH = pl.DeviceIdType.MESH
R = 4
NC = 16
YP, ZP, T, Y2, ZM = range(5)
OWN = -1
OFFSET = {OWN: (0, 0), YP: (1, 0), ZP: (0, 1), T: (3, 3), Y2: (2, 3), ZM: (0, 3)}
PAIRS = (
    (OWN, OWN, False),
    (OWN, YP, True),
    (OWN, ZP, True),
    (OWN, T, True),
    (OWN, Y2, True),
    (YP, ZP, True),
    (ZM, Y2, False),
    (ZP, T, True),
    (ZP, Y2, False),
    (ZP, ZM, False),
)
MIRRORED = ((3, 0), (0, 3), (1, 1), (2, 1), (1, 3), (1, 2))


EARLY_OWN, EARLY_BOTH = (1, 2), (5, 9)
LATE_OWN, LATE_BOTH = (3, 4), (6, 7, 8)


def plan():
    batches = []
    for step in range(-1, R + 1):
        groups, n = [], 0

        def add(pair, count, i, j, along):
            nonlocal n
            groups.append((pair, n, count, i, j, along))
            n += count

        if step < 0:
            for i in range(R):
                add(0, R, i, 0, "j")
        for r, alone, both in ((step, EARLY_OWN, EARLY_BOTH), (step - 1, LATE_OWN, LATE_BOTH)):
            if 0 <= r < R:
                for pair in alone:
                    add(pair, R, 0, r, "i")
                for pair in both:
                    add(pair, r + 1, r, 0, "j")
                    if r:
                        add(pair, r, 0, r, "i")
        batches.append((n, groups))
    return batches


ROUNDS = plan()
NB = len(ROUNDS)


def gene_at(y, z, offset):
    return ((y + offset[0]) % 4) * 4 + (z + offset[1]) % 4


def kernel(counts, out, *scratch):
    (vt, colbuf, rowbuf, totbuf, own, got, final), rest = scratch[:7], scratch[7:]
    prods, rest = rest[:NB], rest[NB:]
    halves, rest = rest[:NB], rest[NB:]
    early, rest = rest[:NB], rest[NB:]
    late, rest = rest[:NB], rest[NB:]
    pieces, rest = rest[:NB], rest[NB:]
    (stat_send, stat_recv, in_send, in_recv, rs_send, rs_recv, fin_send, fin_own, fin_recv) = rest
    genes, cells = own.shape[0] * own.shape[1], own.shape[2]
    S = genes // R
    nj = cells // 128
    c, g = lax.axis_index("cell"), lax.axis_index("gene")
    zl, x, core = c // 8, (c // 2) % 4, c % 2
    y, z = g // 4, g % 4
    pos = 8 * core + 2 * x + zl

    def cell_of(zl_, x_, core_):
        return {"cell": zl_ * 8 + x_ * 2 + core_}

    xp, xm = (x + 1) % 4, (x + 3) % 4
    to_xp, to_xm = cell_of(zl, xp, core), cell_of(zl, xm, core)
    to_core, to_zl = cell_of(zl, x, 1 - core), cell_of(1 - zl, x, core)
    to_yp, to_ym = {"gene": gene_at(y, z, (1, 0))}, {"gene": gene_at(y, z, (3, 0))}
    to_y2 = {"gene": gene_at(y, z, (2, 0))}
    to_zp, to_zm = {"gene": gene_at(y, z, (0, 1))}, {"gene": gene_at(y, z, (0, 3))}

    def remote(src, dst, ssem, rsem, device):
        return pltpu.make_async_remote_copy(
            src_ref=src, dst_ref=dst, send_sem=ssem, recv_sem=rsem, device_id=device, device_id_type=MESH
        )

    barrier = pltpu.get_barrier_semaphore()
    for k in range(1, NC):
        pl.semaphore_signal(barrier, inc=1, device_id={"cell": (c + k) % NC}, device_id_type=MESH)
        pl.semaphore_signal(barrier, inc=1, device_id={"gene": (g + k) % NC}, device_id_type=MESH)

    def local(j, acc):
        v = counts[pl.ds(j * 128, 128), :].astype(jnp.float32)
        t = v.T
        vt[j] = t
        rowbuf[g, pl.ds(j, 1), :] = jnp.sum(t, axis=0, keepdims=True)
        return acc + jnp.sum(v, axis=0, keepdims=True)

    nq = genes // 128
    colsum = lax.fori_loop(0, nj, local, jnp.zeros((1, genes), jnp.float32))
    colbuf[c] = jnp.zeros((8, 128), jnp.float32)
    for q in range(nq):
        colbuf[c, q : q + 1, :] = colsum[:, q * 128 : (q + 1) * 128]
    pl.semaphore_wait(barrier, 2 * (NC - 1))

    def spread(buf, axis, me, k):
        for d in range(1, NC):
            remote(buf.at[me], buf.at[me], stat_send.at[k], stat_recv.at[k], {axis: (me + d) % NC}).start()

    def others(buf, sem):
        return pltpu.make_async_copy(buf.at[0 : NC - 1], buf.at[0 : NC - 1], sem)

    spread(colbuf, "cell", c, 0)
    spread(rowbuf, "gene", g, 1)
    others(colbuf, stat_recv.at[0]).wait()
    totals = jnp.sum(colbuf[...], axis=0)
    totbuf[g] = jnp.broadcast_to(jnp.sum(totals, axis=0, keepdims=True), (8, 128))
    spread(totbuf, "gene", g, 2)
    gcol = [jnp.broadcast_to(totals[q : q + 1, :], (128, 128)).T for q in range(nq)]
    others(rowbuf, stat_recv.at[1]).wait()
    depths = jnp.sum(rowbuf[...], axis=0)
    others(totbuf, stat_recv.at[2]).wait()
    grand = jnp.sum(jnp.sum(totbuf[...], axis=0)[0:1, :])
    share = depths / grand
    ceiling = float(NC * cells) ** 0.5
    for q in range(nq):
        r, o = (q * 128) // S, (q * 128) % S
        for j in range(nj):
            v = vt[j, q * 128 : (q + 1) * 128, :]
            e = gcol[q] * share[j : j + 1, :]
            s = (v - e) * lax.rsqrt(e + e * e / 100.0)
            own[r, o : o + 128, j * 128 : (j + 1) * 128] = jnp.clip(s, -ceiling, ceiling).astype(jnp.bfloat16)

    def chunk(src, r, b, device):
        return remote(src, got.at[r, b], in_send.at[b, r], in_recv.at[b, r], device)

    def own_to(b, r, device):
        return chunk(own.at[r], r, b, device)

    def relay(a, b, r, device):
        return chunk(got.at[r, a], r, b, device)

    for r in range(R):
        own_to(ZM, r, to_zp).start()
        own_to(ZP, r, to_zm).start()
        if r < 1:
            own_to(YP, r, to_ym).start()

    def arrived(b, r):
        own_to(b, r, to_zp).wait_recv()

    def nt(a, b):
        return lax.dot_general(a, b, (((1,), (1,)), ((), ())), preferred_element_type=jnp.float32)

    def put(r, t, tile):
        prods[r][t] = tile.reshape(8, S // 8, S)

    def compute(m):
        base = {}
        for pair, t0, n, i, j, along in ROUNDS[m][1]:
            base.setdefault((pair, along), t0)
        if m == 0:

            @pl.loop(0, R)
            def _(i):
                d = nt(own[i], own[...].reshape(genes, cells))
                for j in range(R):
                    put(m, i * R + j, d[:, j * S : (j + 1) * S])

            return
        e, l = m - 1, m - 2
        if e < R:

            @pl.loop(0, R)
            def _(i):
                d = nt(own[i], got[e, YP : ZP + 1].reshape(2 * S, cells))
                for k in range(2):
                    put(m, base[k + 1, "i"] + i, d[:, k * S : (k + 1) * S])

            @pl.loop(0, e + 1)
            def _(j):
                put(m, base[5, "j"] + j, nt(got[e, YP], got[j, ZP]))
                put(m, base[9, "j"] + j, nt(got[e, ZP], got[j, ZM]))

            if e:

                @pl.loop(0, e)
                def _(i):
                    put(m, base[5, "i"] + i, nt(got[i, YP], got[e, ZP]))
                    put(m, base[9, "i"] + i, nt(got[i, ZP], got[e, ZM]))

        if l >= 0:

            @pl.loop(0, R)
            def _(i):
                d = nt(own[i], got[l, T : Y2 + 1].reshape(2 * S, cells))
                for k in range(2):
                    put(m, base[k + 3, "i"] + i, d[:, k * S : (k + 1) * S])

            @pl.loop(0, l + 1)
            def _(j):
                d = nt(got[l, ZP], got[j, T : Y2 + 1].reshape(2 * S, cells))
                for k in range(2):
                    put(m, base[k + 7, "j"] + j, d[:, k * S : (k + 1) * S])
                put(m, base[6, "j"] + j, nt(got[l, ZM], got[j, Y2]))

            if l:

                @pl.loop(0, l)
                def _(i):
                    d = nt(got[i, ZP], got[l, T : Y2 + 1].reshape(2 * S, cells))
                    for k in range(2):
                        put(m, base[k + 7, "i"] + i, d[:, k * S : (k + 1) * S])
                    put(m, base[6, "i"] + i, nt(got[i, ZM], got[l, Y2]))

    def rs(r, k, src, dst, device):
        return remote(src, dst, rs_send.at[r, k], rs_recv.at[r, k], device)

    def core_copy(r):
        return rs(r, 0, prods[r].at[:, pl.ds(4 * (1 - core), 4)], halves[r], to_core)

    def x_copy(r, k):
        n = ROUNDS[r][0]
        a, b, p, h = slice(0, n // 2), slice(n // 2, n), prods[r], 4 * core
        if k == "ep":
            return rs(r, 1, p.at[a, h + (x + 2) % 4], early[r].at[a], to_xp)
        if k == "em":
            return rs(r, 2, p.at[b, h + (x + 2) % 4], early[r].at[b], to_xm)
        if k == "dp":
            return rs(r, 3, p.at[b, h + xp], late[r].at[0, b], to_xp)
        if k == "dm":
            return rs(r, 4, p.at[a, h + xm], late[r].at[1, a], to_xm)
        if k == "fp":
            return rs(r, 5, p.at[a, h + xp], late[r].at[0, a], to_xp)
        return rs(r, 6, p.at[b, h + xm], late[r].at[1, b], to_xm)

    def zl_copy(r):
        s = S // 16
        return rs(r, 7, prods[r].at[:, 4 * core + x, pl.ds((1 - zl) * s, s)], pieces[r], to_zl)

    def s0(r):
        core_copy(r).start()

    def s1(r):
        n = ROUNDS[r][0]
        core_copy(r).wait_recv()

        @pl.loop(0, n)
        def _(t):
            prods[r][t, pl.ds(4 * core, 4)] = prods[r][t, pl.ds(4 * core, 4)] + halves[r][t]

        for k in ("ep", "em", "dp", "dm"):
            x_copy(r, k).start()

    def s2(r):
        n = ROUNDS[r][0]
        a, b = slice(0, n // 2), slice(n // 2, n)
        x_copy(r, "ep").wait_recv()
        prods[r][a, 4 * core + xp] = prods[r][a, 4 * core + xp] + early[r][a]
        x_copy(r, "fp").start()
        x_copy(r, "em").wait_recv()
        prods[r][b, 4 * core + xm] = prods[r][b, 4 * core + xm] + early[r][b]
        x_copy(r, "fm").start()

    def s3(r):
        for k in ("dp", "dm", "fp", "fm"):
            x_copy(r, k).wait_recv()
        prods[r][:, 4 * core + x] = prods[r][:, 4 * core + x] + late[r][0] + late[r][1]
        zl_copy(r).start()

    def final_sends(r):
        for pair, t0, n, i, j, along in ROUNDS[r][1]:
            a, b, both = PAIRS[pair]
            ga, gb = gene_at(y, z, OFFSET[a]), gene_at(y, z, OFFSET[b])
            if along == "j":
                dst = final.at[i, j : j + n, pos]
            else:
                dst = final.at[i : i + n, j, pos]
            yield pieces[r].at[t0 : t0 + n], dst, ga, gb, a == OWN
            if both:
                yield pieces[r].at[t0 : t0 + n], dst, gb, ga, False

    def s4(r):
        s = S // 16
        zl_copy(r).wait_recv()
        pieces[r][...] = pieces[r][...] + prods[r][:, 4 * core + x, pl.ds(zl * s, s)]
        k = 0
        for src, dst, row, col, maybe in final_sends(r):
            if maybe:

                @pl.when(col == c)
                def _():
                    pltpu.make_async_copy(src, dst, fin_recv).start()

                @pl.when(col != c)
                def _():
                    remote(src, dst, fin_own.at[r, k], fin_recv, {"cell": col, "gene": row}).start()

                k += 1
            else:
                remote(src, dst, fin_send, fin_recv, {"cell": col, "gene": row}).start()

    compute(0)
    s0(0)
    s1(0)
    s2(0)
    for k in range(R + 1):
        m = k + 1
        if k < R:
            arrived(ZM, k)
            relay(ZM, T, k, to_yp).start()
            relay(ZM, Y2, k, to_y2).start()
            if k + 1 < R:
                own_to(YP, k + 1, to_ym).start()
        if k:
            arrived(T, k - 1)
            arrived(Y2, k - 1)
        if k < R:
            arrived(ZP, k)
            arrived(YP, k)
        compute(m)
        s0(m)
        s1(m)
        s3(m - 1)
        s2(m)
    for m in range(NB - 2):
        s4(m)
    s3(NB - 1)
    s4(NB - 2)
    s4(NB - 1)

    pltpu.make_async_copy(final, final, fin_recv).wait()
    dy, dz = (c // 4 - y + 4) % 4, (c % 4 - z + 4) % 4
    flip = functools.reduce(jnp.logical_or, [(dy == a) & (dz == b) for a, b in MIRRORED])
    scale = 1.0 / float(NC * cells)

    def tile(i, j):
        return final[i, j].reshape(S, S) * scale

    @pl.when(flip)
    def _():
        for i in range(R):
            for j in range(R):
                out[j * S : (j + 1) * S, i * S : (i + 1) * S] = tile(i, j).T

    @pl.when(jnp.logical_not(flip))
    def _():
        for i in range(R):
            for j in range(R):
                out[i * S : (i + 1) * S, j * S : (j + 1) * S] = tile(i, j)

    for k, buf in ((0, colbuf), (1, rowbuf), (2, totbuf)):
        others(buf, stat_send.at[k]).wait()
    sent = 0
    for r in range(R):
        for b in range(5):
            own_to(b, r, to_zp).wait_send()
    for r in range(NB):
        core_copy(r).wait_send()
        for k in ("ep", "em", "dp", "dm", "fp", "fm"):
            x_copy(r, k).wait_send()
        zl_copy(r).wait_send()
        k = 0
        for src, dst, row, col, maybe in final_sends(r):
            if maybe:

                @pl.when(col != c)
                def _():
                    remote(src, dst, fin_own.at[r, k], fin_recv, {"cell": col, "gene": row}).wait_send()

                k += 1
            else:
                sent += src.shape[0]
    assert sent % 16 == 0
    pltpu.make_async_copy(prods[0].at[0 : sent // 16], prods[0].at[0 : sent // 16], fin_send).wait()


def body(counts):
    cells, genes = counts.shape
    S = genes // R
    ns = [n for n, _ in ROUNDS]
    f32 = jnp.float32
    dma = pltpu.SemaphoreType.DMA
    own_groups = max(sum(PAIRS[gr[0]][0] == OWN for gr in groups) for _, groups in ROUNDS)
    scratch = [
        pltpu.VMEM((cells // 128, genes, 128), f32),
        pltpu.VMEM((NC, 8, 128), f32),
        pltpu.VMEM((NC, 8, 128), f32),
        pltpu.VMEM((NC, 8, 128), f32),
        pltpu.VMEM((R, S, cells), jnp.bfloat16),
        pltpu.VMEM((R, 5, S, cells), jnp.bfloat16),
        pltpu.VMEM((R, R, 16, S // 16, S), f32),
        *[pltpu.VMEM((n, 8, S // 8, S), f32) for n in ns],
        *[pltpu.VMEM((n, 4, S // 8, S), f32) for n in ns],
        *[pltpu.VMEM((n, S // 8, S), f32) for n in ns],
        *[pltpu.VMEM((2, n, S // 8, S), f32) for n in ns],
        *[pltpu.VMEM((n, S // 16, S), f32) for n in ns],
        dma((3,)),
        dma((3,)),
        dma((5, R)),
        dma((5, R)),
        dma((NB, 8)),
        dma((NB, 8)),
        dma(()),
        dma((NB, own_groups)),
        dma(()),
    ]
    return pl.pallas_call(
        kernel,
        out_shape=jax.ShapeDtypeStruct((genes, genes), f32),
        in_specs=[pl.BlockSpec(memory_space=pltpu.VMEM)],
        out_specs=pl.BlockSpec(memory_space=pltpu.VMEM),
        scratch_shapes=scratch,
        compiler_params=pltpu.CompilerParams(
            collective_id=0, has_side_effects=True, vmem_limit_bytes=60 * 1024 * 1024
        ),
    )(counts)


def solution(mesh):
    return jax.shard_map(
        body,
        mesh=mesh,
        in_specs=(P("cell", "gene"),),
        out_specs=P("gene", "cell"),
        check_vma=False,
    )
```

```python
import functools

import jax
import jax.numpy as jnp
from jax import lax
from jax.experimental import pallas as pl
from jax.experimental.pallas import tpu as pltpu
from jax.sharding import PartitionSpec as P

MESH = pl.DeviceIdType.MESH
R = 4
H = 2
NC = 16
YP, ZP, T, Y2, ZM = range(5)
OWN = -1
OFFSET = {OWN: (0, 0), YP: (1, 0), ZP: (0, 1), T: (3, 3), Y2: (2, 3), ZM: (0, 3)}
PAIRS = (
    (OWN, OWN, False),
    (OWN, YP, True),
    (OWN, ZP, True),
    (OWN, T, True),
    (OWN, Y2, True),
    (YP, ZP, True),
    (ZM, Y2, False),
    (ZP, T, True),
    (ZP, Y2, False),
    (ZP, ZM, False),
)
MIRRORED = ((3, 0), (0, 3), (1, 1), (2, 1), (1, 3), (1, 2))


EARLY_OWN, EARLY_BOTH = (1, 2), (5, 9)
LATE_OWN, LATE_BOTH = (3, 4), (6, 7, 8)


def plan():
    batches = []
    for step in range(-1, R + 1):
        groups, n = [], 0

        def add(pair, count, i, j, along):
            nonlocal n
            groups.append((pair, n, count, i, j, along))
            n += count

        if step < 0:
            for i in range(R):
                add(0, R, i, 0, "j")
        for r, alone, both in ((step, EARLY_OWN, EARLY_BOTH), (step - 1, LATE_OWN, LATE_BOTH)):
            if 0 <= r < R:
                for pair in alone:
                    add(pair, R, 0, r, "i")
                for pair in both:
                    add(pair, r + 1, r, 0, "j")
                    if r:
                        add(pair, r, 0, r, "i")
        batches.append((n, groups))
    return batches


ROUNDS = plan()
NB = len(ROUNDS)


def gene_at(y, z, offset):
    return ((y + offset[0]) % 4) * 4 + (z + offset[1]) % 4


def kernel(counts, out, *scratch):
    (vt, colbuf, rowbuf, totbuf, own, got, final), rest = scratch[:7], scratch[7:]
    prods, rest = rest[:NB], rest[NB:]
    halves, rest = rest[:NB], rest[NB:]
    early, rest = rest[:NB], rest[NB:]
    late, rest = rest[:NB], rest[NB:]
    pieces, rest = rest[:NB], rest[NB:]
    (stat_send, stat_recv, in_send, in_recv, rs_send, rs_recv, fin_send, fin_own, fin_recv) = rest
    genes, cells = own.shape[0] * own.shape[1], own.shape[2]
    S = genes // R
    nj = cells // 128
    c, g = lax.axis_index("cell"), lax.axis_index("gene")
    zl, x, core = c // 8, (c // 2) % 4, c % 2
    y, z = g // 4, g % 4
    pos = 8 * core + 2 * x + zl

    def cell_of(zl_, x_, core_):
        return {"cell": zl_ * 8 + x_ * 2 + core_}

    xp, xm = (x + 1) % 4, (x + 3) % 4
    to_xp, to_xm = cell_of(zl, xp, core), cell_of(zl, xm, core)
    to_core, to_zl = cell_of(zl, x, 1 - core), cell_of(1 - zl, x, core)
    to_yp, to_ym = {"gene": gene_at(y, z, (1, 0))}, {"gene": gene_at(y, z, (3, 0))}
    to_y2 = {"gene": gene_at(y, z, (2, 0))}
    to_zp, to_zm = {"gene": gene_at(y, z, (0, 1))}, {"gene": gene_at(y, z, (0, 3))}

    def remote(src, dst, ssem, rsem, device):
        return pltpu.make_async_remote_copy(
            src_ref=src, dst_ref=dst, send_sem=ssem, recv_sem=rsem, device_id=device, device_id_type=MESH
        )

    barrier = pltpu.get_barrier_semaphore()
    for k in range(1, NC):
        pl.semaphore_signal(barrier, inc=1, device_id={"cell": (c + k) % NC}, device_id_type=MESH)
        pl.semaphore_signal(barrier, inc=1, device_id={"gene": (g + k) % NC}, device_id_type=MESH)

    def local(j, acc):
        v = counts[pl.ds(j * 128, 128), :].astype(jnp.float32)
        t = v.T
        vt[j] = t
        rowbuf[g, pl.ds(j, 1), :] = jnp.sum(t, axis=0, keepdims=True)
        return acc + jnp.sum(v, axis=0, keepdims=True)

    nq = genes // 128
    colsum = lax.fori_loop(0, nj, local, jnp.zeros((1, genes), jnp.float32))
    colbuf[c] = jnp.zeros((8, 128), jnp.float32)
    for q in range(nq):
        colbuf[c, q : q + 1, :] = colsum[:, q * 128 : (q + 1) * 128]
    pl.semaphore_wait(barrier, 2 * (NC - 1))

    def spread(buf, axis, me, k):
        for d in range(1, NC):
            remote(buf.at[me], buf.at[me], stat_send.at[k], stat_recv.at[k], {axis: (me + d) % NC}).start()

    def others(buf, sem):
        return pltpu.make_async_copy(buf.at[0 : NC - 1], buf.at[0 : NC - 1], sem)

    spread(colbuf, "cell", c, 0)
    spread(rowbuf, "gene", g, 1)
    others(colbuf, stat_recv.at[0]).wait()
    totals = jnp.sum(colbuf[...], axis=0)
    totbuf[g] = jnp.broadcast_to(jnp.sum(totals, axis=0, keepdims=True), (8, 128))
    spread(totbuf, "gene", g, 2)
    gcol = [jnp.broadcast_to(totals[q : q + 1, :], (128, 128)).T for q in range(nq)]
    others(rowbuf, stat_recv.at[1]).wait()
    depths = jnp.sum(rowbuf[...], axis=0)
    others(totbuf, stat_recv.at[2]).wait()
    grand = jnp.sum(jnp.sum(totbuf[...], axis=0)[0:1, :])
    share = depths / grand
    ceiling = float(NC * cells) ** 0.5
    for q in range(nq):
        r, o = (q * 128) // S, (q * 128) % S
        for j in range(nj):
            v = vt[j, q * 128 : (q + 1) * 128, :]
            e = gcol[q] * share[j : j + 1, :]
            s = (v - e) * lax.rsqrt(e + e * e / 100.0)
            own[r, o : o + 128, j * 128 : (j + 1) * 128] = jnp.clip(s, -ceiling, ceiling).astype(jnp.bfloat16)

    def part(h):
        return slice(h * (S // H), (h + 1) * (S // H))

    def own_to(b, r, h, device):
        return remote(own.at[r, part(h)], got.at[r, b, part(h)], in_send.at[b, r, h], in_recv.at[b, r, h], device)

    def arrived(b, r, h):
        own_to(b, r, h, to_zp).wait_recv()

    def pass_on(k, h):
        arrived(ZM, k, h)
        src = got.at[k, ZM, part(h)]
        for b, device in ((T, to_yp), (Y2, to_y2)):
            remote(src, got.at[k, b, part(h)], in_send.at[b, k, h], in_recv.at[b, k, h], device).start()

    def have(b, r):
        for h in range(H):
            arrived(b, r, h)

    for r in range(R):
        for h in range(H):
            own_to(ZM, r, h, to_zp).start()
            own_to(ZP, r, h, to_zm).start()
        if r < 1:
            for h in range(H):
                own_to(YP, r, h, to_ym).start()

    def nt(a, b):
        return lax.dot_general(a, b, (((1,), (1,)), ((), ())), preferred_element_type=jnp.float32)

    def put(r, t, tile):
        prods[r][t] = tile.reshape(8, S // 8, S)

    def compute(m):
        base = {}
        for pair, t0, n, i, j, along in ROUNDS[m][1]:
            base.setdefault((pair, along), t0)
        if m == 0:

            @pl.loop(0, R)
            def _(i):
                d = nt(own[i], own[...].reshape(genes, cells))
                for j in range(R):
                    put(m, i * R + j, d[:, j * S : (j + 1) * S])

            return
        e, l = m - 1, m - 2
        if e < R:

            @pl.loop(0, R)
            def _(i):
                d = nt(own[i], got[e, YP : ZP + 1].reshape(2 * S, cells))
                for k in range(2):
                    put(m, base[k + 1, "i"] + i, d[:, k * S : (k + 1) * S])

            @pl.loop(0, e + 1)
            def _(j):
                put(m, base[5, "j"] + j, nt(got[e, YP], got[j, ZP]))
                put(m, base[9, "j"] + j, nt(got[e, ZP], got[j, ZM]))

            if e:

                @pl.loop(0, e)
                def _(i):
                    put(m, base[5, "i"] + i, nt(got[i, YP], got[e, ZP]))
                    put(m, base[9, "i"] + i, nt(got[i, ZP], got[e, ZM]))

        if l >= 0:

            @pl.loop(0, R)
            def _(i):
                d = nt(own[i], got[l, T : Y2 + 1].reshape(2 * S, cells))
                for k in range(2):
                    put(m, base[k + 3, "i"] + i, d[:, k * S : (k + 1) * S])

            @pl.loop(0, l + 1)
            def _(j):
                d = nt(got[l, ZP], got[j, T : Y2 + 1].reshape(2 * S, cells))
                for k in range(2):
                    put(m, base[k + 7, "j"] + j, d[:, k * S : (k + 1) * S])
                put(m, base[6, "j"] + j, nt(got[l, ZM], got[j, Y2]))

            if l:

                @pl.loop(0, l)
                def _(i):
                    d = nt(got[i, ZP], got[l, T : Y2 + 1].reshape(2 * S, cells))
                    for k in range(2):
                        put(m, base[k + 7, "i"] + i, d[:, k * S : (k + 1) * S])
                    put(m, base[6, "i"] + i, nt(got[i, ZM], got[l, Y2]))

    def rs(r, k, src, dst, device):
        return remote(src, dst, rs_send.at[r, k], rs_recv.at[r, k], device)

    def core_copy(r):
        return rs(r, 0, prods[r].at[:, pl.ds(4 * (1 - core), 4)], halves[r], to_core)

    def x_copy(r, k):
        n = ROUNDS[r][0]
        a, b, p, h = slice(0, n // 2), slice(n // 2, n), prods[r], 4 * core
        if k == "ep":
            return rs(r, 1, p.at[a, h + (x + 2) % 4], early[r].at[a], to_xp)
        if k == "em":
            return rs(r, 2, p.at[b, h + (x + 2) % 4], early[r].at[b], to_xm)
        if k == "dp":
            return rs(r, 3, p.at[b, h + xp], late[r].at[0, b], to_xp)
        if k == "dm":
            return rs(r, 4, p.at[a, h + xm], late[r].at[1, a], to_xm)
        if k == "fp":
            return rs(r, 5, p.at[a, h + xp], late[r].at[0, a], to_xp)
        return rs(r, 6, p.at[b, h + xm], late[r].at[1, b], to_xm)

    def zl_copy(r):
        s = S // 16
        return rs(r, 7, prods[r].at[:, 4 * core + x, pl.ds((1 - zl) * s, s)], pieces[r], to_zl)

    def s0(r):
        core_copy(r).start()

    def s1(r):
        n = ROUNDS[r][0]
        core_copy(r).wait_recv()

        @pl.loop(0, n)
        def _(t):
            prods[r][t, pl.ds(4 * core, 4)] = prods[r][t, pl.ds(4 * core, 4)] + halves[r][t]

        for k in ("ep", "em", "dp", "dm"):
            x_copy(r, k).start()

    def s2(r):
        n = ROUNDS[r][0]
        a, b = slice(0, n // 2), slice(n // 2, n)
        x_copy(r, "ep").wait_recv()
        prods[r][a, 4 * core + xp] = prods[r][a, 4 * core + xp] + early[r][a]
        x_copy(r, "fp").start()
        x_copy(r, "em").wait_recv()
        prods[r][b, 4 * core + xm] = prods[r][b, 4 * core + xm] + early[r][b]
        x_copy(r, "fm").start()

    def s3(r):
        for k in ("dp", "dm", "fp", "fm"):
            x_copy(r, k).wait_recv()
        prods[r][:, 4 * core + x] = prods[r][:, 4 * core + x] + late[r][0] + late[r][1]
        zl_copy(r).start()

    def final_sends(r):
        for pair, t0, n, i, j, along in ROUNDS[r][1]:
            a, b, both = PAIRS[pair]
            ga, gb = gene_at(y, z, OFFSET[a]), gene_at(y, z, OFFSET[b])
            if along == "j":
                dst = final.at[i, j : j + n, pos]
            else:
                dst = final.at[i : i + n, j, pos]
            yield pieces[r].at[t0 : t0 + n], dst, ga, gb, a == OWN
            if both:
                yield pieces[r].at[t0 : t0 + n], dst, gb, ga, False

    def s4(r):
        s = S // 16
        zl_copy(r).wait_recv()
        pieces[r][...] = pieces[r][...] + prods[r][:, 4 * core + x, pl.ds(zl * s, s)]
        k = 0
        for src, dst, row, col, maybe in final_sends(r):
            if maybe:

                @pl.when(col == c)
                def _():
                    pltpu.make_async_copy(src, dst, fin_recv).start()

                @pl.when(col != c)
                def _():
                    remote(src, dst, fin_own.at[r, k], fin_recv, {"cell": col, "gene": row}).start()

                k += 1
            else:
                remote(src, dst, fin_send, fin_recv, {"cell": col, "gene": row}).start()

    compute(0)
    s0(0)
    s1(0)
    s2(0)
    pass_on(0, 0)
    for k in range(R + 1):
        m = k + 1
        if k < R:
            for h in range(1, H):
                pass_on(k, h)
            if k + 1 < R:
                for h in range(H):
                    own_to(YP, k + 1, h, to_ym).start()
        if k:
            have(T, k - 1)
            have(Y2, k - 1)
        if k < R:
            have(ZP, k)
            have(YP, k)
        compute(m)
        s0(m)
        s1(m)
        if k + 1 < R:
            pass_on(k + 1, 0)
        s3(m - 1)
        s2(m)
        if k == R - 1:
            for early_m in range(m - 1):
                s4(early_m)
    s4(NB - 3)
    s4(NB - 2)
    s3(NB - 1)
    s4(NB - 1)

    pltpu.make_async_copy(final, final, fin_recv).wait()
    dy, dz = (c // 4 - y + 4) % 4, (c % 4 - z + 4) % 4
    flip = functools.reduce(jnp.logical_or, [(dy == a) & (dz == b) for a, b in MIRRORED])
    scale = 1.0 / float(NC * cells)

    def tile(i, j):
        return final[i, j].reshape(S, S) * scale

    @pl.when(flip)
    def _():
        for i in range(R):
            for j in range(R):
                out[j * S : (j + 1) * S, i * S : (i + 1) * S] = tile(i, j).T

    @pl.when(jnp.logical_not(flip))
    def _():
        for i in range(R):
            for j in range(R):
                out[i * S : (i + 1) * S, j * S : (j + 1) * S] = tile(i, j)

    for k, buf in ((0, colbuf), (1, rowbuf), (2, totbuf)):
        others(buf, stat_send.at[k]).wait()
    sent = 0
    for r in range(R):
        for b in range(5):
            for h in range(H):
                own_to(b, r, h, to_zp).wait_send()
    for r in range(NB):
        core_copy(r).wait_send()
        for k in ("ep", "em", "dp", "dm", "fp", "fm"):
            x_copy(r, k).wait_send()
        zl_copy(r).wait_send()
        k = 0
        for src, dst, row, col, maybe in final_sends(r):
            if maybe:

                @pl.when(col != c)
                def _():
                    remote(src, dst, fin_own.at[r, k], fin_recv, {"cell": col, "gene": row}).wait_send()

                k += 1
            else:
                sent += src.shape[0]
    assert sent % 16 == 0
    pltpu.make_async_copy(prods[0].at[0 : sent // 16], prods[0].at[0 : sent // 16], fin_send).wait()


def body(counts):
    cells, genes = counts.shape
    S = genes // R
    ns = [n for n, _ in ROUNDS]
    f32 = jnp.float32
    dma = pltpu.SemaphoreType.DMA
    own_groups = max(sum(PAIRS[gr[0]][0] == OWN for gr in groups) for _, groups in ROUNDS)
    scratch = [
        pltpu.VMEM((cells // 128, genes, 128), f32),
        pltpu.VMEM((NC, 8, 128), f32),
        pltpu.VMEM((NC, 8, 128), f32),
        pltpu.VMEM((NC, 8, 128), f32),
        pltpu.VMEM((R, S, cells), jnp.bfloat16),
        pltpu.VMEM((R, 5, S, cells), jnp.bfloat16),
        pltpu.VMEM((R, R, 16, S // 16, S), f32),
        *[pltpu.VMEM((n, 8, S // 8, S), f32) for n in ns],
        *[pltpu.VMEM((n, 4, S // 8, S), f32) for n in ns],
        *[pltpu.VMEM((n, S // 8, S), f32) for n in ns],
        *[pltpu.VMEM((2, n, S // 8, S), f32) for n in ns],
        *[pltpu.VMEM((n, S // 16, S), f32) for n in ns],
        dma((3,)),
        dma((3,)),
        dma((5, R, H)),
        dma((5, R, H)),
        dma((NB, 8)),
        dma((NB, 8)),
        dma(()),
        dma((NB, own_groups)),
        dma(()),
    ]
    return pl.pallas_call(
        kernel,
        out_shape=jax.ShapeDtypeStruct((genes, genes), f32),
        in_specs=[pl.BlockSpec(memory_space=pltpu.VMEM)],
        out_specs=pl.BlockSpec(memory_space=pltpu.VMEM),
        scratch_shapes=scratch,
        compiler_params=pltpu.CompilerParams(
            collective_id=0, has_side_effects=True, vmem_limit_bytes=60 * 1024 * 1024
        ),
    )(counts)


def solution(mesh):
    return jax.shard_map(
        body,
        mesh=mesh,
        in_specs=(P("cell", "gene"),),
        out_specs=P("gene", "cell"),
        check_vma=False,
    )
```

```python
import functools

import jax
import jax.numpy as jnp
from jax import lax
from jax.experimental import pallas as pl
from jax.experimental.pallas import tpu as pltpu
from jax.sharding import PartitionSpec as P

MESH = pl.DeviceIdType.MESH
R = 4
H = 2
NC = 16
YP, ZP, T, Y2, ZM = range(5)
OWN = -1
OFFSET = {OWN: (0, 0), YP: (1, 0), ZP: (0, 1), T: (3, 3), Y2: (2, 3), ZM: (0, 3)}
PAIRS = (
    (OWN, OWN, None),
    (OWN, YP, "all"),
    (OWN, ZP, "all"),
    (OWN, T, "all"),
    (OWN, Y2, "all"),
    (YP, ZP, "all"),
    (ZM, Y2, "below"),
    (ZP, T, "all"),
    (ZP, Y2, "below"),
    (ZP, ZM, "below"),
)
HALVED = ((2, 0), (0, 2), (2, 2))
MIRRORED = ((3, 0), (0, 3), (1, 1), (2, 1), (1, 3), (1, 2))


EARLY_OWN, EARLY_BOTH = (1, 2), (5, 9)
LATE_OWN, LATE_BOTH = (3, 4), (6, 7, 8)


def plan():
    batches = []
    for step in range(-1, R + 1):
        groups, n = [], 0

        def add(pair, count, i, j, along):
            nonlocal n
            groups.append((pair, n, count, i, j, along))
            n += count

        if step < 0:
            for i in range(R):
                add(0, i + 1, i, 0, "j")
        for r, alone, both in ((step, EARLY_OWN, EARLY_BOTH), (step - 1, LATE_OWN, LATE_BOTH)):
            if 0 <= r < R:
                for pair in alone:
                    add(pair, R, 0, r, "i")
                for pair in both:
                    add(pair, r + 1, r, 0, "j")
                    if r and PAIRS[pair][2] == "all":
                        add(pair, r, 0, r, "i")
        batches.append((n, groups))
    return batches


ROUNDS = plan()
NB = len(ROUNDS)


def gene_at(y, z, offset):
    return ((y + offset[0]) % 4) * 4 + (z + offset[1]) % 4


def kernel(counts, out, *scratch):
    (vt, colbuf, rowbuf, totbuf, own, got, final), rest = scratch[:7], scratch[7:]
    prods, rest = rest[:NB], rest[NB:]
    halves, rest = rest[:NB], rest[NB:]
    early, rest = rest[:NB], rest[NB:]
    late, rest = rest[:NB], rest[NB:]
    pieces, rest = rest[:NB], rest[NB:]
    (stat_send, stat_recv, in_send, in_recv, rs_send, rs_recv, fin_send, fin_own, fin_recv) = rest
    genes, cells = own.shape[0] * own.shape[1], own.shape[2]
    S = genes // R
    nj = cells // 128
    c, g = lax.axis_index("cell"), lax.axis_index("gene")
    zl, x, core = c // 8, (c // 2) % 4, c % 2
    y, z = g // 4, g % 4
    pos = 8 * core + 2 * x + zl

    def cell_of(zl_, x_, core_):
        return {"cell": zl_ * 8 + x_ * 2 + core_}

    xp, xm = (x + 1) % 4, (x + 3) % 4
    to_xp, to_xm = cell_of(zl, xp, core), cell_of(zl, xm, core)
    to_core, to_zl = cell_of(zl, x, 1 - core), cell_of(1 - zl, x, core)
    to_yp, to_ym = {"gene": gene_at(y, z, (1, 0))}, {"gene": gene_at(y, z, (3, 0))}
    to_y2 = {"gene": gene_at(y, z, (2, 0))}
    to_zp, to_zm = {"gene": gene_at(y, z, (0, 1))}, {"gene": gene_at(y, z, (0, 3))}

    def remote(src, dst, ssem, rsem, device):
        return pltpu.make_async_remote_copy(
            src_ref=src, dst_ref=dst, send_sem=ssem, recv_sem=rsem, device_id=device, device_id_type=MESH
        )

    barrier = pltpu.get_barrier_semaphore()
    for k in range(1, NC):
        pl.semaphore_signal(barrier, inc=1, device_id={"cell": (c + k) % NC}, device_id_type=MESH)
        pl.semaphore_signal(barrier, inc=1, device_id={"gene": (g + k) % NC}, device_id_type=MESH)

    def local(j, acc):
        v = counts[pl.ds(j * 128, 128), :].astype(jnp.float32)
        t = v.T
        vt[j] = t
        rowbuf[g, pl.ds(j, 1), :] = jnp.sum(t, axis=0, keepdims=True)
        return acc + jnp.sum(v, axis=0, keepdims=True)

    nq = genes // 128
    colsum = lax.fori_loop(0, nj, local, jnp.zeros((1, genes), jnp.float32))
    colbuf[c] = jnp.zeros((8, 128), jnp.float32)
    for q in range(nq):
        colbuf[c, q : q + 1, :] = colsum[:, q * 128 : (q + 1) * 128]
    pl.semaphore_wait(barrier, 2 * (NC - 1))

    def spread(buf, axis, me, k):
        for d in range(1, NC):
            remote(buf.at[me], buf.at[me], stat_send.at[k], stat_recv.at[k], {axis: (me + d) % NC}).start()

    def others(buf, sem):
        return pltpu.make_async_copy(buf.at[0 : NC - 1], buf.at[0 : NC - 1], sem)

    spread(colbuf, "cell", c, 0)
    spread(rowbuf, "gene", g, 1)
    others(colbuf, stat_recv.at[0]).wait()
    totals = jnp.sum(colbuf[...], axis=0)
    totbuf[g] = jnp.broadcast_to(jnp.sum(totals, axis=0, keepdims=True), (8, 128))
    spread(totbuf, "gene", g, 2)
    gcol = [jnp.broadcast_to(totals[q : q + 1, :], (128, 128)).T for q in range(nq)]
    others(rowbuf, stat_recv.at[1]).wait()
    depths = jnp.sum(rowbuf[...], axis=0)
    others(totbuf, stat_recv.at[2]).wait()
    grand = jnp.sum(jnp.sum(totbuf[...], axis=0)[0:1, :])
    share = depths / grand
    ceiling = float(NC * cells) ** 0.5
    for q in range(nq):
        r, o = (q * 128) // S, (q * 128) % S
        for j in range(nj):
            v = vt[j, q * 128 : (q + 1) * 128, :]
            e = gcol[q] * share[j : j + 1, :]
            s = (v - e) * lax.rsqrt(e + e * e / 100.0)
            own[r, o : o + 128, j * 128 : (j + 1) * 128] = jnp.clip(s, -ceiling, ceiling).astype(jnp.bfloat16)

    def part(h):
        return slice(h * (S // H), (h + 1) * (S // H))

    def own_to(b, r, h, device):
        return remote(own.at[r, part(h)], got.at[r, b, part(h)], in_send.at[b, r, h], in_recv.at[b, r, h], device)

    def arrived(b, r, h):
        own_to(b, r, h, to_zp).wait_recv()

    def pass_on(k, h):
        arrived(ZM, k, h)
        src = got.at[k, ZM, part(h)]
        for b, device in ((T, to_yp), (Y2, to_y2)):
            remote(src, got.at[k, b, part(h)], in_send.at[b, k, h], in_recv.at[b, k, h], device).start()

    def have(b, r):
        for h in range(H):
            arrived(b, r, h)

    for r in range(R):
        for h in range(H):
            own_to(ZM, r, h, to_zp).start()
            own_to(ZP, r, h, to_zm).start()
        if r < 1:
            for h in range(H):
                own_to(YP, r, h, to_ym).start()

    def nt(a, b):
        return lax.dot_general(a, b, (((1,), (1,)), ((), ())), preferred_element_type=jnp.float32)

    def put(r, t, tile):
        prods[r][t] = tile.reshape(8, S // 8, S)

    def base_of(m):
        base = {}
        for pair, t0, n, i, j, along in ROUNDS[m][1]:
            base.setdefault((pair, along), t0)
        return base

    def compute_diagonal():
        for i in range(R):
            d = nt(own[i], own[0 : i + 1].reshape((i + 1) * S, cells))
            for j in range(i + 1):
                put(0, i * (i + 1) // 2 + j, d[:, j * S : (j + 1) * S])

    def compute_early(m):
        base, e = base_of(m), m - 1

        @pl.loop(0, R)
        def _(i):
            d = nt(own[i], got[e, YP : ZP + 1].reshape(2 * S, cells))
            for k in range(2):
                put(m, base[k + 1, "i"] + i, d[:, k * S : (k + 1) * S])

        @pl.loop(0, e + 1)
        def _(j):
            put(m, base[5, "j"] + j, nt(got[e, YP], got[j, ZP]))
            put(m, base[9, "j"] + j, nt(got[e, ZP], got[j, ZM]))

        if e:

            @pl.loop(0, e)
            def _(i):
                put(m, base[5, "i"] + i, nt(got[i, YP], got[e, ZP]))

    def compute_late(m):
        base, l = base_of(m), m - 2

        @pl.loop(0, R)
        def _(i):
            d = nt(own[i], got[l, T : Y2 + 1].reshape(2 * S, cells))
            for k in range(2):
                put(m, base[k + 3, "i"] + i, d[:, k * S : (k + 1) * S])

        @pl.loop(0, l + 1)
        def _(j):
            d = nt(got[l, ZP], got[j, T : Y2 + 1].reshape(2 * S, cells))
            for k in range(2):
                put(m, base[k + 7, "j"] + j, d[:, k * S : (k + 1) * S])
            put(m, base[6, "j"] + j, nt(got[l, ZM], got[j, Y2]))

        if l:

            @pl.loop(0, l)
            def _(i):
                put(m, base[7, "i"] + i, nt(got[i, ZP], got[l, T]))

    def rs(r, k, src, dst, device):
        return remote(src, dst, rs_send.at[r, k], rs_recv.at[r, k], device)

    def core_copy(r):
        return rs(r, 0, prods[r].at[:, pl.ds(4 * (1 - core), 4)], halves[r], to_core)

    def x_copy(r, k):
        n = ROUNDS[r][0]
        a, b, p, h = slice(0, n // 2), slice(n // 2, n), prods[r], 4 * core
        if k == "ep":
            return rs(r, 1, p.at[a, h + (x + 2) % 4], early[r].at[a], to_xp)
        if k == "em":
            return rs(r, 2, p.at[b, h + (x + 2) % 4], early[r].at[b], to_xm)
        if k == "dp":
            return rs(r, 3, p.at[b, h + xp], late[r].at[0, b], to_xp)
        if k == "dm":
            return rs(r, 4, p.at[a, h + xm], late[r].at[1, a], to_xm)
        if k == "fp":
            return rs(r, 5, p.at[a, h + xp], late[r].at[0, a], to_xp)
        return rs(r, 6, p.at[b, h + xm], late[r].at[1, b], to_xm)

    def zl_copy(r):
        s = S // 16
        return rs(r, 7, prods[r].at[:, 4 * core + x, pl.ds((1 - zl) * s, s)], pieces[r], to_zl)

    def s0(r):
        core_copy(r).start()

    def s1(r):
        n = ROUNDS[r][0]
        core_copy(r).wait_recv()

        @pl.loop(0, n)
        def _(t):
            prods[r][t, pl.ds(4 * core, 4)] = prods[r][t, pl.ds(4 * core, 4)] + halves[r][t]

        for k in ("ep", "em", "dp", "dm"):
            x_copy(r, k).start()

    def s2(r):
        n = ROUNDS[r][0]
        a, b = slice(0, n // 2), slice(n // 2, n)
        x_copy(r, "ep").wait_recv()
        prods[r][a, 4 * core + xp] = prods[r][a, 4 * core + xp] + early[r][a]
        x_copy(r, "fp").start()
        x_copy(r, "em").wait_recv()
        prods[r][b, 4 * core + xm] = prods[r][b, 4 * core + xm] + early[r][b]
        x_copy(r, "fm").start()

    def s3(r):
        for k in ("dp", "dm", "fp", "fm"):
            x_copy(r, k).wait_recv()
        prods[r][:, 4 * core + x] = prods[r][:, 4 * core + x] + late[r][0] + late[r][1]
        zl_copy(r).start()

    def final_sends(r):
        for pair, t0, n, i, j, along in ROUNDS[r][1]:
            a, b, both = PAIRS[pair]
            ga, gb = gene_at(y, z, OFFSET[a]), gene_at(y, z, OFFSET[b])
            if along == "j":
                dst = final.at[i, j : j + n, pos]
            else:
                dst = final.at[i : i + n, j, pos]
            yield pieces[r].at[t0 : t0 + n], dst, ga, gb, a == OWN
            if both == "all":
                yield pieces[r].at[t0 : t0 + n], dst, gb, ga, False
            if both == "below" and i:
                yield pieces[r].at[t0 : t0 + i], final.at[0:i, i, pos], gb, ga, False

    def s4(r):
        s = S // 16
        zl_copy(r).wait_recv()
        pieces[r][...] = pieces[r][...] + prods[r][:, 4 * core + x, pl.ds(zl * s, s)]
        k = 0
        for src, dst, row, col, maybe in final_sends(r):
            if maybe:

                @pl.when(col == c)
                def _():
                    pltpu.make_async_copy(src, dst, fin_recv).start()

                @pl.when(col != c)
                def _():
                    remote(src, dst, fin_own.at[r, k], fin_recv, {"cell": col, "gene": row}).start()

                k += 1
            else:
                remote(src, dst, fin_send, fin_recv, {"cell": col, "gene": row}).start()

    compute_diagonal()
    s0(0)
    s1(0)
    s2(0)
    pass_on(0, 0)
    for k in range(R + 1):
        m = k + 1
        if k < R:
            for h in range(1, H):
                pass_on(k, h)
            if k + 1 < R:
                for h in range(H):
                    own_to(YP, k + 1, h, to_ym).start()
        if k < R:
            have(ZP, k)
            have(YP, k)
            compute_early(m)
        if k:
            have(T, k - 1)
            have(Y2, k - 1)
            compute_late(m)
        s0(m)
        s1(m)
        if k + 1 < R:
            pass_on(k + 1, 0)
        s3(m - 1)
        s2(m)
        if k == R - 1:
            for done in range(m):
                s4(done)
    s4(NB - 2)
    s3(NB - 1)
    s4(NB - 1)

    dy, dz = (c // 4 - y + 4) % 4, (c % 4 - z + 4) % 4

    def among(offsets):
        return functools.reduce(jnp.logical_or, [(dy == a) & (dz == b) for a, b in offsets])

    diagonal, halved, flip = among(((0, 0),)), among(HALVED), among(MIRRORED)
    scale = 1.0 / float(NC * cells)

    def write(i, j, tile):
        out[i * S : (i + 1) * S, j * S : (j + 1) * S] = tile

    def tile(i, j):
        return final[i, j].reshape(S, S) * scale

    below = [(i, j) for i in range(R) for j in range(i)]
    above = [(i, j) for j, i in below]
    even = [(i, i) for i in range(R)]

    @pl.when(diagonal)
    def _():
        lower = prods[0].at[0 : len(below + even)]
        pltpu.make_async_copy(lower, lower, fin_recv).wait()
        for i, j in below:
            write(i, j, tile(i, j))
            write(j, i, tile(i, j).T)
        for i, j in even:
            write(i, j, tile(i, j))

    @pl.when(jnp.logical_not(diagonal))
    def _():
        pltpu.make_async_copy(final, final, fin_recv).wait()

        @pl.when(flip)
        def _():
            for i, j in below + even + above:
                write(j, i, tile(i, j).T)

        @pl.when(jnp.logical_not(flip))
        def _():
            for i, j in below + even:
                write(i, j, tile(i, j))

            @pl.when(halved)
            def _():
                for i, j in above:
                    write(i, j, tile(i, j).T)

            @pl.when(jnp.logical_not(halved))
            def _():
                for i, j in above:
                    write(i, j, tile(i, j))

    for k, buf in ((0, colbuf), (1, rowbuf), (2, totbuf)):
        others(buf, stat_send.at[k]).wait()
    sent = 0
    for r in range(R):
        for b in range(5):
            for h in range(H):
                own_to(b, r, h, to_zp).wait_send()
    for r in range(NB):
        core_copy(r).wait_send()
        for k in ("ep", "em", "dp", "dm", "fp", "fm"):
            x_copy(r, k).wait_send()
        zl_copy(r).wait_send()
        k = 0
        for src, dst, row, col, maybe in final_sends(r):
            if maybe:

                @pl.when(col != c)
                def _():
                    remote(src, dst, fin_own.at[r, k], fin_recv, {"cell": col, "gene": row}).wait_send()

                k += 1
            else:
                sent += src.shape[0]
    assert sent % 16 == 0
    pltpu.make_async_copy(prods[2].at[0 : sent // 16], prods[2].at[0 : sent // 16], fin_send).wait()


def body(counts):
    cells, genes = counts.shape
    S = genes // R
    ns = [n for n, _ in ROUNDS]
    f32 = jnp.float32
    dma = pltpu.SemaphoreType.DMA
    own_groups = max(sum(PAIRS[gr[0]][0] == OWN for gr in groups) for _, groups in ROUNDS)
    scratch = [
        pltpu.VMEM((cells // 128, genes, 128), f32),
        pltpu.VMEM((NC, 8, 128), f32),
        pltpu.VMEM((NC, 8, 128), f32),
        pltpu.VMEM((NC, 8, 128), f32),
        pltpu.VMEM((R, S, cells), jnp.bfloat16),
        pltpu.VMEM((R, 5, S, cells), jnp.bfloat16),
        pltpu.VMEM((R, R, 16, S // 16, S), f32),
        *[pltpu.VMEM((n, 8, S // 8, S), f32) for n in ns],
        *[pltpu.VMEM((n, 4, S // 8, S), f32) for n in ns],
        *[pltpu.VMEM((n, S // 8, S), f32) for n in ns],
        *[pltpu.VMEM((2, n, S // 8, S), f32) for n in ns],
        *[pltpu.VMEM((n, S // 16, S), f32) for n in ns],
        dma((3,)),
        dma((3,)),
        dma((5, R, H)),
        dma((5, R, H)),
        dma((NB, 8)),
        dma((NB, 8)),
        dma(()),
        dma((NB, own_groups)),
        dma(()),
    ]
    return pl.pallas_call(
        kernel,
        out_shape=jax.ShapeDtypeStruct((genes, genes), f32),
        in_specs=[pl.BlockSpec(memory_space=pltpu.VMEM)],
        out_specs=pl.BlockSpec(memory_space=pltpu.VMEM),
        scratch_shapes=scratch,
        compiler_params=pltpu.CompilerParams(
            collective_id=0, has_side_effects=True, vmem_limit_bytes=60 * 1024 * 1024
        ),
    )(counts)


def solution(mesh):
    return jax.shard_map(
        body,
        mesh=mesh,
        in_specs=(P("cell", "gene"),),
        out_specs=P("gene", "cell"),
        check_vma=False,
    )
```

```python
import functools

import jax
import jax.numpy as jnp
from jax import lax
from jax.experimental import pallas as pl
from jax.experimental.pallas import tpu as pltpu
from jax.sharding import PartitionSpec as P

MESH = pl.DeviceIdType.MESH
R = 4
H = 2
NC = 16
YP, ZP, T, Y2, ZM = range(5)
OWN = -1
OFFSET = {OWN: (0, 0), YP: (1, 0), ZP: (0, 1), T: (3, 3), Y2: (2, 3), ZM: (0, 3)}
PAIRS = (
    (OWN, OWN, None),
    (OWN, YP, "all"),
    (OWN, ZP, "all"),
    (OWN, T, "all"),
    (OWN, Y2, "all"),
    (YP, ZP, "all"),
    (ZM, Y2, "below"),
    (ZP, T, "all"),
    (ZP, Y2, "below"),
    (ZP, ZM, "below"),
)
HALVED = ((2, 0), (0, 2), (2, 2))
MIRRORED = ((3, 0), (0, 3), (1, 1), (2, 1), (1, 3), (1, 2))


EARLY_OWN, EARLY_BOTH = (1, 2), (5, 9)
LATE_OWN, LATE_BOTH = (3, 4), (6, 7, 8)


def plan():
    batches = []
    for step in range(-1, R + 1):
        groups, n = [], 0

        def add(pair, count, i, j, along):
            nonlocal n
            groups.append((pair, n, count, i, j, along))
            n += count

        if step < 0:
            for i in range(R):
                add(0, i + 1, i, 0, "j")
        for r, alone, both in ((step, EARLY_OWN, EARLY_BOTH), (step - 1, LATE_OWN, LATE_BOTH)):
            if 0 <= r < R:
                for pair in alone:
                    add(pair, R, 0, r, "i")
                for pair in both:
                    add(pair, r + 1, r, 0, "j")
                    if r and PAIRS[pair][2] == "all":
                        add(pair, r, 0, r, "i")
        batches.append((n, groups))
    return batches


ROUNDS = plan()
NB = len(ROUNDS)


def gene_at(y, z, offset):
    return ((y + offset[0]) % 4) * 4 + (z + offset[1]) % 4


def kernel(counts, out, *scratch):
    (vt, colbuf, rowbuf, totbuf, own, got, mid, final), rest = scratch[:8], scratch[8:]
    prods, rest = rest[:NB], rest[NB:]
    halves, rest = rest[:NB], rest[NB:]
    early, rest = rest[:NB], rest[NB:]
    late, rest = rest[:NB], rest[NB:]
    pieces, rest = rest[:NB], rest[NB:]
    (stat_send, stat_recv, in_send, in_recv, rs_send, rs_recv, fin_send, fin_own, mid_recv, mid_send, fin_recv) = rest
    genes, cells = own.shape[0] * own.shape[1], own.shape[2]
    S = genes // R
    nj = cells // 128
    c, g = lax.axis_index("cell"), lax.axis_index("gene")
    zl, x, core = c // 8, (c // 2) % 4, c % 2
    y, z = g // 4, g % 4
    pos = 8 * core + 2 * x + zl

    def cell_of(zl_, x_, core_):
        return {"cell": zl_ * 8 + x_ * 2 + core_}

    xp, xm = (x + 1) % 4, (x + 3) % 4
    to_xp, to_xm = cell_of(zl, xp, core), cell_of(zl, xm, core)
    to_core, to_zl = cell_of(zl, x, 1 - core), cell_of(1 - zl, x, core)
    to_yp, to_ym = {"gene": gene_at(y, z, (1, 0))}, {"gene": gene_at(y, z, (3, 0))}
    to_y2 = {"gene": gene_at(y, z, (2, 0))}
    to_zp, to_zm = {"gene": gene_at(y, z, (0, 1))}, {"gene": gene_at(y, z, (0, 3))}

    def remote(src, dst, ssem, rsem, device):
        return pltpu.make_async_remote_copy(
            src_ref=src, dst_ref=dst, send_sem=ssem, recv_sem=rsem, device_id=device, device_id_type=MESH
        )

    barrier = pltpu.get_barrier_semaphore()
    for k in range(1, NC):
        pl.semaphore_signal(barrier, inc=1, device_id={"cell": (c + k) % NC}, device_id_type=MESH)
        pl.semaphore_signal(barrier, inc=1, device_id={"gene": (g + k) % NC}, device_id_type=MESH)

    def local(j, acc):
        v = counts[pl.ds(j * 128, 128), :].astype(jnp.float32)
        t = v.T
        vt[j] = t
        rowbuf[g, pl.ds(j, 1), :] = jnp.sum(t, axis=0, keepdims=True)
        return acc + jnp.sum(v, axis=0, keepdims=True)

    nq = genes // 128
    colsum = lax.fori_loop(0, nj, local, jnp.zeros((1, genes), jnp.float32))
    colbuf[c] = jnp.zeros((8, 128), jnp.float32)
    for q in range(nq):
        colbuf[c, q : q + 1, :] = colsum[:, q * 128 : (q + 1) * 128]
    pl.semaphore_wait(barrier, 2 * (NC - 1))

    def spread(buf, axis, me, k):
        for d in range(1, NC):
            remote(buf.at[me], buf.at[me], stat_send.at[k], stat_recv.at[k], {axis: (me + d) % NC}).start()

    def others(buf, sem):
        return pltpu.make_async_copy(buf.at[0 : NC - 1], buf.at[0 : NC - 1], sem)

    spread(colbuf, "cell", c, 0)
    spread(rowbuf, "gene", g, 1)
    others(colbuf, stat_recv.at[0]).wait()
    totals = jnp.sum(colbuf[...], axis=0)
    totbuf[g] = jnp.broadcast_to(jnp.sum(totals, axis=0, keepdims=True), (8, 128))
    spread(totbuf, "gene", g, 2)
    gcol = [jnp.broadcast_to(totals[q : q + 1, :], (128, 128)).T for q in range(nq)]
    others(rowbuf, stat_recv.at[1]).wait()
    depths = jnp.sum(rowbuf[...], axis=0)
    others(totbuf, stat_recv.at[2]).wait()
    grand = jnp.sum(jnp.sum(totbuf[...], axis=0)[0:1, :])
    share = depths / grand
    ceiling = float(NC * cells) ** 0.5
    for q in range(nq):
        r, o = (q * 128) // S, (q * 128) % S
        for j in range(nj):
            v = vt[j, q * 128 : (q + 1) * 128, :]
            e = gcol[q] * share[j : j + 1, :]
            s = (v - e) * lax.rsqrt(e + e * e / 100.0)
            own[r, o : o + 128, j * 128 : (j + 1) * 128] = jnp.clip(s, -ceiling, ceiling).astype(jnp.bfloat16)

    def part(h):
        return slice(h * (S // H), (h + 1) * (S // H))

    def own_to(b, r, h, device):
        return remote(own.at[r, part(h)], got.at[r, b, part(h)], in_send.at[b, r, h], in_recv.at[b, r, h], device)

    def arrived(b, r, h):
        own_to(b, r, h, to_zp).wait_recv()

    def pass_on(k, h):
        arrived(ZM, k, h)
        src = got.at[k, ZM, part(h)]
        for b, device in ((T, to_yp), (Y2, to_y2)):
            remote(src, got.at[k, b, part(h)], in_send.at[b, k, h], in_recv.at[b, k, h], device).start()

    def have(b, r):
        for h in range(H):
            arrived(b, r, h)

    for r in range(R):
        for h in range(H):
            own_to(ZM, r, h, to_zp).start()
            own_to(ZP, r, h, to_zm).start()
        if r < 1:
            for h in range(H):
                own_to(YP, r, h, to_ym).start()

    def nt(a, b):
        return lax.dot_general(a, b, (((1,), (1,)), ((), ())), preferred_element_type=jnp.float32)

    def put(r, t, tile):
        prods[r][t] = tile.reshape(8, S // 8, S)

    def base_of(m):
        base = {}
        for pair, t0, n, i, j, along in ROUNDS[m][1]:
            base.setdefault((pair, along), t0)
        return base

    def compute_diagonal():
        for i in range(R):
            d = nt(own[i], own[0 : i + 1].reshape((i + 1) * S, cells))
            for j in range(i + 1):
                put(0, i * (i + 1) // 2 + j, d[:, j * S : (j + 1) * S])

    def compute_early(m):
        base, e = base_of(m), m - 1

        @pl.loop(0, R)
        def _(i):
            d = nt(own[i], got[e, YP : ZP + 1].reshape(2 * S, cells))
            for k in range(2):
                put(m, base[k + 1, "i"] + i, d[:, k * S : (k + 1) * S])

        @pl.loop(0, e + 1)
        def _(j):
            put(m, base[5, "j"] + j, nt(got[e, YP], got[j, ZP]))
            put(m, base[9, "j"] + j, nt(got[e, ZP], got[j, ZM]))

        if e:

            @pl.loop(0, e)
            def _(i):
                put(m, base[5, "i"] + i, nt(got[i, YP], got[e, ZP]))

    def compute_late(m):
        base, l = base_of(m), m - 2

        @pl.loop(0, R)
        def _(i):
            d = nt(own[i], got[l, T : Y2 + 1].reshape(2 * S, cells))
            for k in range(2):
                put(m, base[k + 3, "i"] + i, d[:, k * S : (k + 1) * S])

        @pl.loop(0, l + 1)
        def _(j):
            d = nt(got[l, ZP], got[j, T : Y2 + 1].reshape(2 * S, cells))
            for k in range(2):
                put(m, base[k + 7, "j"] + j, d[:, k * S : (k + 1) * S])
            put(m, base[6, "j"] + j, nt(got[l, ZM], got[j, Y2]))

        if l:

            @pl.loop(0, l)
            def _(i):
                put(m, base[7, "i"] + i, nt(got[i, ZP], got[l, T]))

    def rs(r, k, src, dst, device):
        return remote(src, dst, rs_send.at[r, k], rs_recv.at[r, k], device)

    def core_copy(r):
        return rs(r, 0, prods[r].at[:, pl.ds(4 * (1 - core), 4)], halves[r], to_core)

    def x_copy(r, k):
        n = ROUNDS[r][0]
        a, b, p, h = slice(0, n // 2), slice(n // 2, n), prods[r], 4 * core
        if k == "ep":
            return rs(r, 1, p.at[a, h + (x + 2) % 4], early[r].at[a], to_xp)
        if k == "em":
            return rs(r, 2, p.at[b, h + (x + 2) % 4], early[r].at[b], to_xm)
        if k == "dp":
            return rs(r, 3, p.at[b, h + xp], late[r].at[0, b], to_xp)
        if k == "dm":
            return rs(r, 4, p.at[a, h + xm], late[r].at[1, a], to_xm)
        if k == "fp":
            return rs(r, 5, p.at[a, h + xp], late[r].at[0, a], to_xp)
        return rs(r, 6, p.at[b, h + xm], late[r].at[1, b], to_xm)

    def zl_copy(r):
        s = S // 16
        return rs(r, 7, prods[r].at[:, 4 * core + x, pl.ds((1 - zl) * s, s)], pieces[r], to_zl)

    def s0(r):
        core_copy(r).start()

    def s1(r):
        n = ROUNDS[r][0]
        core_copy(r).wait_recv()

        @pl.loop(0, n)
        def _(t):
            prods[r][t, pl.ds(4 * core, 4)] = prods[r][t, pl.ds(4 * core, 4)] + halves[r][t]

        for k in ("ep", "em", "dp", "dm"):
            x_copy(r, k).start()

    def s2(r):
        n = ROUNDS[r][0]
        a, b = slice(0, n // 2), slice(n // 2, n)
        x_copy(r, "ep").wait_recv()
        prods[r][a, 4 * core + xp] = prods[r][a, 4 * core + xp] + early[r][a]
        x_copy(r, "fp").start()
        x_copy(r, "em").wait_recv()
        prods[r][b, 4 * core + xm] = prods[r][b, 4 * core + xm] + early[r][b]
        x_copy(r, "fm").start()

    def s3(r):
        for k in ("dp", "dm", "fp", "fm"):
            x_copy(r, k).wait_recv()
        prods[r][:, 4 * core + x] = prods[r][:, 4 * core + x] + late[r][0] + late[r][1]
        zl_copy(r).start()

    def final_sends(r):
        for pair, t0, n, i, j, along in ROUNDS[r][1]:
            a, b, both = PAIRS[pair]
            ga, gb = gene_at(y, z, OFFSET[a]), gene_at(y, z, OFFSET[b])
            ti, tj = (i, slice(j, j + n)) if along == "j" else (slice(i, i + n), j)
            yield pieces[r].at[t0 : t0 + n], ti, tj, ga, gb, a == OWN
            if both == "all":
                yield pieces[r].at[t0 : t0 + n], ti, tj, gb, ga, False
            if both == "below" and i:
                yield pieces[r].at[t0 : t0 + i], slice(0, i), i, gb, ga, False

    def first_leg(r, src, ti, tj, row, col, sem):
        to = {"cell": (col // 8) * 8 + c % 8, "gene": row}
        return remote(src, mid.at[col % 8, ti, tj, zl], sem, mid_recv.at[col % 8], to)

    def s4(r):
        s = S // 16
        zl_copy(r).wait_recv()
        pieces[r][...] = pieces[r][...] + prods[r][:, 4 * core + x, pl.ds(zl * s, s)]
        k = 0
        for src, ti, tj, row, col, maybe in final_sends(r):
            if maybe:

                @pl.when(col // 8 == zl)
                def _():
                    pltpu.make_async_copy(src, mid.at[col % 8, ti, tj, zl], mid_recv.at[col % 8]).start()

                @pl.when(col // 8 != zl)
                def _():
                    first_leg(r, src, ti, tj, row, col, fin_own.at[r, k]).start()

                k += 1
            else:
                first_leg(r, src, ti, tj, row, col, fin_send).start()

    def second_leg(s):
        dst = final.at[:, :, pl.ds(pos - zl, 2)]
        return remote(mid.at[s], dst, mid_send.at[s], fin_recv, {"cell": zl * 8 + s})

    def pass_final():
        for d in range(8):
            s = (c % 8 + d) % 8

            @pl.when(zl * 8 + s == g)
            def _():
                lower = halves[0].at[:, 0:1]
                pltpu.make_async_copy(lower, lower, mid_recv.at[s]).wait()

            @pl.when(zl * 8 + s != g)
            def _():
                pltpu.make_async_copy(mid.at[s], mid.at[s], mid_recv.at[s]).wait()

            if d:
                second_leg(s).start()
            else:
                pltpu.make_async_copy(mid.at[s], final.at[:, :, pl.ds(pos - zl, 2)], fin_recv).start()

    compute_diagonal()
    s0(0)
    s1(0)
    s2(0)
    pass_on(0, 0)
    for k in range(R + 1):
        m = k + 1
        if k < R:
            for h in range(1, H):
                pass_on(k, h)
            if k + 1 < R:
                for h in range(H):
                    own_to(YP, k + 1, h, to_ym).start()
        if k < R:
            have(ZP, k)
            have(YP, k)
            compute_early(m)
        if k:
            have(T, k - 1)
            have(Y2, k - 1)
            compute_late(m)
        s0(m)
        s1(m)
        if k + 1 < R:
            pass_on(k + 1, 0)
        s3(m - 1)
        s2(m)
        if k == R - 1:
            for done in range(m):
                s4(done)
    s4(NB - 2)
    s3(NB - 1)
    s4(NB - 1)
    pass_final()

    pltpu.make_async_copy(final, final, fin_recv).wait()
    dy, dz = (c // 4 - y + 4) % 4, (c % 4 - z + 4) % 4

    def among(offsets):
        return functools.reduce(jnp.logical_or, [(dy == a) & (dz == b) for a, b in offsets])

    diagonal, halved, flip = among(((0, 0),)), among(HALVED), among(MIRRORED)
    scale = 1.0 / float(NC * cells)

    def write(i, j, tile):
        out[i * S : (i + 1) * S, j * S : (j + 1) * S] = tile

    def tile(i, j):
        return final[i, j].reshape(S, S) * scale

    below = [(i, j) for i in range(R) for j in range(i)]
    above = [(i, j) for j, i in below]
    even = [(i, i) for i in range(R)]

    @pl.when(diagonal)
    def _():
        for i, j in below:
            write(i, j, tile(i, j))
            write(j, i, tile(i, j).T)
        for i, j in even:
            write(i, j, tile(i, j))

    @pl.when(jnp.logical_not(diagonal))
    def _():

        @pl.when(flip)
        def _():
            for i, j in below + even + above:
                write(j, i, tile(i, j).T)

        @pl.when(jnp.logical_not(flip))
        def _():
            for i, j in below + even:
                write(i, j, tile(i, j))

            @pl.when(halved)
            def _():
                for i, j in above:
                    write(i, j, tile(i, j).T)

            @pl.when(jnp.logical_not(halved))
            def _():
                for i, j in above:
                    write(i, j, tile(i, j))

    for k, buf in ((0, colbuf), (1, rowbuf), (2, totbuf)):
        others(buf, stat_send.at[k]).wait()
    sent = 0
    for r in range(R):
        for b in range(5):
            for h in range(H):
                own_to(b, r, h, to_zp).wait_send()
    for r in range(NB):
        core_copy(r).wait_send()
        for k in ("ep", "em", "dp", "dm", "fp", "fm"):
            x_copy(r, k).wait_send()
        zl_copy(r).wait_send()
        k = 0
        for src, ti, tj, row, col, maybe in final_sends(r):
            if maybe:

                @pl.when(col // 8 != zl)
                def _():
                    first_leg(r, src, ti, tj, row, col, fin_own.at[r, k]).wait_send()

                k += 1
            else:
                sent += src.shape[0]
    for d in range(1, 8):
        second_leg((c % 8 + d) % 8).wait_send()
    assert sent % 16 == 0
    pltpu.make_async_copy(prods[2].at[0 : sent // 16], prods[2].at[0 : sent // 16], fin_send).wait()


def body(counts):
    cells, genes = counts.shape
    S = genes // R
    ns = [n for n, _ in ROUNDS]
    f32 = jnp.float32
    dma = pltpu.SemaphoreType.DMA
    own_groups = max(sum(PAIRS[gr[0]][0] == OWN for gr in groups) for _, groups in ROUNDS)
    scratch = [
        pltpu.VMEM((cells // 128, genes, 128), f32),
        pltpu.VMEM((NC, 8, 128), f32),
        pltpu.VMEM((NC, 8, 128), f32),
        pltpu.VMEM((NC, 8, 128), f32),
        pltpu.VMEM((R, S, cells), jnp.bfloat16),
        pltpu.VMEM((R, 5, S, cells), jnp.bfloat16),
        pltpu.VMEM((8, R, R, 2, S // 16, S), f32),
        pltpu.VMEM((R, R, 16, S // 16, S), f32),
        *[pltpu.VMEM((n, 8, S // 8, S), f32) for n in ns],
        *[pltpu.VMEM((n, 4, S // 8, S), f32) for n in ns],
        *[pltpu.VMEM((n, S // 8, S), f32) for n in ns],
        *[pltpu.VMEM((2, n, S // 8, S), f32) for n in ns],
        *[pltpu.VMEM((n, S // 16, S), f32) for n in ns],
        dma((3,)),
        dma((3,)),
        dma((5, R, H)),
        dma((5, R, H)),
        dma((NB, 8)),
        dma((NB, 8)),
        dma(()),
        dma((NB, own_groups)),
        dma((8,)),
        dma((8,)),
        dma(()),
    ]
    return pl.pallas_call(
        kernel,
        out_shape=jax.ShapeDtypeStruct((genes, genes), f32),
        in_specs=[pl.BlockSpec(memory_space=pltpu.VMEM)],
        out_specs=pl.BlockSpec(memory_space=pltpu.VMEM),
        scratch_shapes=scratch,
        compiler_params=pltpu.CompilerParams(
            collective_id=0, has_side_effects=True, vmem_limit_bytes=60 * 1024 * 1024
        ),
    )(counts)


def solution(mesh):
    return jax.shard_map(
        body,
        mesh=mesh,
        in_specs=(P("cell", "gene"),),
        out_specs=P("gene", "cell"),
        check_vma=False,
    )
```

```python
import functools

import jax
import jax.numpy as jnp
from jax import lax
from jax.experimental import pallas as pl
from jax.experimental.pallas import tpu as pltpu
from jax.sharding import PartitionSpec as P

MESH = pl.DeviceIdType.MESH
R = 4
H = 2
NC = 16
YP, ZP, T, Y2, ZM = range(5)
OWN = -1
OFFSET = {OWN: (0, 0), YP: (1, 0), ZP: (0, 1), T: (3, 3), Y2: (2, 3), ZM: (0, 3)}
PAIRS = (
    (OWN, OWN, None),
    (OWN, YP, "all"),
    (OWN, ZP, "all"),
    (YP, ZM, "all"),
    (OWN, Y2, "all"),
    (YP, ZP, "all"),
    (ZM, Y2, "below"),
    (ZP, T, "all"),
    (ZP, Y2, "below"),
    (ZP, ZM, "below"),
)
HALVED = ((2, 0), (0, 2), (2, 2))
MIRRORED = ((3, 0), (0, 3), (1, 1), (2, 1), (1, 3), (1, 2))


def whole_at(step):
    found = []
    if step < 2:
        found += [(1, r) for r in range(2 * step, 2 * step + 2)]
    if step < R:
        found += [(2, step)]
    if 0 < step < R:
        found += [(pair, r) for r in range(0 if step == 1 else step, step + 1) for pair in (3, 5)]
    if step:
        found += [(4, step - 1)]
    return found


def plan():
    batches = []
    for step in range(-1, R + 1):
        groups, n = [], 0

        def add(pair, count, i, j, along):
            nonlocal n
            groups.append((pair, n, count, i, j, along))
            n += count

        if step < 0:
            for i in range(R):
                add(0, i + 1, i, 0, "j")
        if step >= 0:
            for pair, r in whole_at(step):
                add(pair, R, 0, r, "i")
            if step < R:
                add(9, step + 1, step, 0, "j")
            if step:
                for pair in (6, 7, 8):
                    add(pair, step, step - 1, 0, "j")
                if step > 1:
                    add(7, step - 1, 0, step - 1, "i")
        batches.append((n, groups))
    return batches


ROUNDS = plan()
NB = len(ROUNDS)


def gene_at(y, z, offset):
    return ((y + offset[0]) % 4) * 4 + (z + offset[1]) % 4


def kernel(counts, out, *scratch):
    (vt, colbuf, rowbuf, totbuf, own, got, mid, final), rest = scratch[:8], scratch[8:]
    prods, rest = rest[:NB], rest[NB:]
    halves, rest = rest[:NB], rest[NB:]
    early, rest = rest[:NB], rest[NB:]
    late, rest = rest[:NB], rest[NB:]
    pieces, rest = rest[:NB], rest[NB:]
    (stat_send, stat_recv, in_send, in_recv, rs_send, rs_recv, fin_send, fin_own, mid_recv, mid_send, fin_recv) = rest
    genes, cells = own.shape[0] * own.shape[1], own.shape[2]
    S = genes // R
    nj = cells // 128
    c, g = lax.axis_index("cell"), lax.axis_index("gene")
    zl, x, core = c // 8, (c // 2) % 4, c % 2
    y, z = g // 4, g % 4
    pos = 8 * core + 2 * x + zl

    def cell_of(zl_, x_, core_):
        return {"cell": zl_ * 8 + x_ * 2 + core_}

    xp, xm = (x + 1) % 4, (x + 3) % 4
    to_xp, to_xm = cell_of(zl, xp, core), cell_of(zl, xm, core)
    to_core, to_zl = cell_of(zl, x, 1 - core), cell_of(1 - zl, x, core)
    to_yp, to_ym = {"gene": gene_at(y, z, (1, 0))}, {"gene": gene_at(y, z, (3, 0))}
    to_y2 = {"gene": gene_at(y, z, (2, 0))}
    to_zp, to_zm = {"gene": gene_at(y, z, (0, 1))}, {"gene": gene_at(y, z, (0, 3))}

    def remote(src, dst, ssem, rsem, device):
        return pltpu.make_async_remote_copy(
            src_ref=src, dst_ref=dst, send_sem=ssem, recv_sem=rsem, device_id=device, device_id_type=MESH
        )

    barrier = pltpu.get_barrier_semaphore()
    for k in range(1, NC):
        pl.semaphore_signal(barrier, inc=1, device_id={"cell": (c + k) % NC}, device_id_type=MESH)
        pl.semaphore_signal(barrier, inc=1, device_id={"gene": (g + k) % NC}, device_id_type=MESH)

    def local(j, acc):
        v = counts[pl.ds(j * 128, 128), :].astype(jnp.float32)
        t = v.T
        vt[j] = t
        rowbuf[g, pl.ds(j, 1), :] = jnp.sum(t, axis=0, keepdims=True)
        return acc + jnp.sum(v, axis=0, keepdims=True)

    nq = genes // 128
    colsum = lax.fori_loop(0, nj, local, jnp.zeros((1, genes), jnp.float32))
    colbuf[c] = jnp.zeros((8, 128), jnp.float32)
    for q in range(nq):
        colbuf[c, q : q + 1, :] = colsum[:, q * 128 : (q + 1) * 128]
    pl.semaphore_wait(barrier, 2 * (NC - 1))

    def spread(buf, axis, me, k):
        for d in range(1, NC):
            remote(buf.at[me], buf.at[me], stat_send.at[k], stat_recv.at[k], {axis: (me + d) % NC}).start()

    def others(buf, sem):
        return pltpu.make_async_copy(buf.at[0 : NC - 1], buf.at[0 : NC - 1], sem)

    spread(colbuf, "cell", c, 0)
    spread(rowbuf, "gene", g, 1)
    others(colbuf, stat_recv.at[0]).wait()
    totals = jnp.sum(colbuf[...], axis=0)
    totbuf[g] = jnp.broadcast_to(jnp.sum(totals, axis=0, keepdims=True), (8, 128))
    spread(totbuf, "gene", g, 2)
    gcol = [jnp.broadcast_to(totals[q : q + 1, :], (128, 128)).T for q in range(nq)]
    others(rowbuf, stat_recv.at[1]).wait()
    depths = jnp.sum(rowbuf[...], axis=0)
    others(totbuf, stat_recv.at[2]).wait()
    grand = jnp.sum(jnp.sum(totbuf[...], axis=0)[0:1, :])
    share = depths / grand
    ceiling = float(NC * cells) ** 0.5
    def part(h):
        return slice(h * (S // H), (h + 1) * (S // H))

    def own_to(b, r, h, device):
        return remote(own.at[r, part(h)], got.at[r, b, part(h)], in_send.at[b, r, h], in_recv.at[b, r, h], device)

    def arrived(b, r, h):
        own_to(b, r, h, to_zp).wait_recv()

    def pass_on(k, h):
        arrived(ZM, k, h)
        src = got.at[k, ZM, part(h)]
        for b, device in ((T, to_yp), (Y2, to_y2)):
            remote(src, got.at[k, b, part(h)], in_send.at[b, k, h], in_recv.at[b, k, h], device).start()

    def have(b, r):
        for h in range(H):
            arrived(b, r, h)

    assert S == 128
    for r in range(R):
        for j in range(nj):
            v = vt[j, r * S : (r + 1) * S, :]
            e = gcol[r] * share[j : j + 1, :]
            t = (v - e) * lax.rsqrt(e + e * e / 100.0)
            own[r, :, j * 128 : (j + 1) * 128] = jnp.clip(t, -ceiling, ceiling).astype(jnp.bfloat16)
        for h in range(H):
            own_to(ZM, r, h, to_zp).start()
            own_to(ZP, r, h, to_zm).start()
        if r < 2:
            for h in range(H):
                own_to(YP, r, h, to_ym).start()

    def nt(a, b):
        return lax.dot_general(a, b, (((1,), (1,)), ((), ())), preferred_element_type=jnp.float32)

    def put(r, t, tile):
        prods[r][t] = tile.reshape(8, S // 8, S)

    def base_of(m):
        base = {}
        for pair, t0, n, i, j, along in ROUNDS[m][1]:
            base.setdefault((pair, along), t0)
        return base

    def compute_diagonal():
        for i in range(R):
            d = nt(own[i], own[0 : i + 1].reshape((i + 1) * S, cells))
            for j in range(i + 1):
                put(0, i * (i + 1) // 2 + j, d[:, j * S : (j + 1) * S])

    def whole(m, pairs):
        for pair, t0, n, _, j, along in ROUNDS[m][1]:
            if pair in pairs:
                a, b, _ = PAIRS[pair]

                @pl.loop(0, R)
                def _(i):
                    left = own[i] if a == OWN else got[i, a]
                    put(m, t0 + i, nt(left, got[j, b]))

    def compute_early(m):
        base, e = base_of(m), m - 1
        whole(m, (1, 2, 3, 5))

        @pl.loop(0, e + 1)
        def _(j):
            put(m, base[9, "j"] + j, nt(got[e, ZP], got[j, ZM]))

    def compute_late(m):
        base, l = base_of(m), m - 2
        whole(m, (4,))

        @pl.loop(0, l + 1)
        def _(j):
            d = nt(got[l, ZP], got[j, T : Y2 + 1].reshape(2 * S, cells))
            for k in range(2):
                put(m, base[k + 7, "j"] + j, d[:, k * S : (k + 1) * S])
            put(m, base[6, "j"] + j, nt(got[l, ZM], got[j, Y2]))

        if l:

            @pl.loop(0, l)
            def _(i):
                put(m, base[7, "i"] + i, nt(got[i, ZP], got[l, T]))

    def rs(r, k, src, dst, device):
        return remote(src, dst, rs_send.at[r, k], rs_recv.at[r, k], device)

    def core_copy(r):
        return rs(r, 0, prods[r].at[:, pl.ds(4 * (1 - core), 4)], halves[r], to_core)

    def x_copy(r, k):
        n = ROUNDS[r][0]
        a, b, p, h = slice(0, n // 2), slice(n // 2, n), prods[r], 4 * core
        if k == "ep":
            return rs(r, 1, p.at[a, h + (x + 2) % 4], early[r].at[a], to_xp)
        if k == "em":
            return rs(r, 2, p.at[b, h + (x + 2) % 4], early[r].at[b], to_xm)
        if k == "dp":
            return rs(r, 3, p.at[b, h + xp], late[r].at[0, b], to_xp)
        if k == "dm":
            return rs(r, 4, p.at[a, h + xm], late[r].at[1, a], to_xm)
        if k == "fp":
            return rs(r, 5, p.at[a, h + xp], late[r].at[0, a], to_xp)
        return rs(r, 6, p.at[b, h + xm], late[r].at[1, b], to_xm)

    def zl_copy(r):
        s = S // 16
        return rs(r, 7, prods[r].at[:, 4 * core + x, pl.ds((1 - zl) * s, s)], pieces[r], to_zl)

    def s0(r):
        core_copy(r).start()

    def s1(r):
        n = ROUNDS[r][0]
        core_copy(r).wait_recv()

        @pl.loop(0, n)
        def _(t):
            prods[r][t, pl.ds(4 * core, 4)] = prods[r][t, pl.ds(4 * core, 4)] + halves[r][t]

        for k in ("ep", "em", "dp", "dm"):
            x_copy(r, k).start()

    def s2(r):
        n = ROUNDS[r][0]
        a, b = slice(0, n // 2), slice(n // 2, n)
        x_copy(r, "ep").wait_recv()
        prods[r][a, 4 * core + xp] = prods[r][a, 4 * core + xp] + early[r][a]
        x_copy(r, "fp").start()
        x_copy(r, "em").wait_recv()
        prods[r][b, 4 * core + xm] = prods[r][b, 4 * core + xm] + early[r][b]
        x_copy(r, "fm").start()

    def s3(r):
        for k in ("dp", "dm", "fp", "fm"):
            x_copy(r, k).wait_recv()
        prods[r][:, 4 * core + x] = prods[r][:, 4 * core + x] + late[r][0] + late[r][1]
        zl_copy(r).start()

    def final_sends(r):
        for pair, t0, n, i, j, along in ROUNDS[r][1]:
            a, b, both = PAIRS[pair]
            ga, gb = gene_at(y, z, OFFSET[a]), gene_at(y, z, OFFSET[b])
            ti, tj = (i, slice(j, j + n)) if along == "j" else (slice(i, i + n), j)
            yield pieces[r].at[t0 : t0 + n], ti, tj, ga, gb, a == OWN
            if both == "all":
                yield pieces[r].at[t0 : t0 + n], ti, tj, gb, ga, False
            if both == "below" and i:
                yield pieces[r].at[t0 : t0 + i], slice(0, i), i, gb, ga, False

    def first_leg(r, src, ti, tj, row, col, sem):
        to = {"cell": (col // 8) * 8 + c % 8, "gene": row}
        return remote(src, mid.at[col % 8, ti, tj, zl], sem, mid_recv.at[r // (NB - 1), col % 8], to)

    def s4(r):
        s = S // 16
        zl_copy(r).wait_recv()
        pieces[r][...] = pieces[r][...] + prods[r][:, 4 * core + x, pl.ds(zl * s, s)]
        k = 0
        for src, ti, tj, row, col, maybe in final_sends(r):
            if maybe:

                @pl.when(col // 8 == zl)
                def _():
                    pltpu.make_async_copy(src, mid.at[col % 8, ti, tj, zl], mid_recv.at[r // (NB - 1), col % 8]).start()

                @pl.when(col // 8 != zl)
                def _():
                    first_leg(r, src, ti, tj, row, col, fin_own.at[r, k]).start()

                k += 1
            else:
                first_leg(r, src, ti, tj, row, col, fin_send).start()

    regions = ((slice(0, R - 1), slice(0, R - 1)), (R - 1, slice(0, R)), (slice(0, R - 1), R - 1))

    def second_leg(s, k):
        ti, tj = regions[k]
        dst = final.at[ti, tj, pl.ds(pos - zl, 2)]
        return remote(mid.at[s, ti, tj], dst, mid_send.at[k, s], fin_recv, {"cell": zl * 8 + s})

    def pass_final(phase):
        inner, rows = (R - 1) * (R - 1), R * (R - 1)
        for d in range(8):
            s = (c % 8 + d) % 8
            col = zl * 8 + s
            dy, dz = (col // 4 - y + 4) % 4, (col % 4 - z + 4) % 4
            diagonal = col == g
            lagging = (dy == 2) & ((dz == 1) | (dz == 3))
            inward = ((dz == 2) & (dy != 0)) | ((dz == 0) & (dy == 2))

            def await_tiles(n):
                like = late[2].at[0, 0:n]
                pltpu.make_async_copy(like, like, mid_recv.at[phase, s]).wait()

            @pl.when(lagging)
            def _():
                await_tiles(R if phase else rows)

            @pl.when(inward)
            def _():
                await_tiles(R * R - inner if phase else inner)

            if phase == 0:

                @pl.when(diagonal)
                def _():
                    await_tiles(R * (R + 1) // 2)

                @pl.when(jnp.logical_not(diagonal | lagging | inward))
                def _():
                    await_tiles(R * R)

            for k in (1, 2) if phase else (0,):
                if d:
                    second_leg(s, k).start()
                else:
                    ti, tj = regions[k]
                    pltpu.make_async_copy(mid.at[s, ti, tj], final.at[ti, tj, pl.ds(pos - zl, 2)], fin_recv).start()

    compute_diagonal()
    s0(0)
    s1(0)
    s2(0)
    pass_on(0, 0)
    for k in range(R + 1):
        m = k + 1
        if k < R:
            for h in range(1, H):
                pass_on(k, h)
            if k == 0:
                for r in range(2, R):
                    for h in range(H):
                        own_to(YP, r, h, to_ym).start()
        if k < R:
            have(ZP, k)
            for r in range(2 * k, 2 * k + 2 if k < 2 else 0):
                have(YP, r)
            compute_early(m)
        if k:
            have(T, k - 1)
            have(Y2, k - 1)
            compute_late(m)
        s0(m)
        s1(m)
        if k + 1 < R:
            pass_on(k + 1, 0)
        s3(m - 1)
        s2(m)
        if k == R - 1:
            for done in range(m):
                s4(done)
    s4(NB - 2)
    s3(NB - 1)
    s4(NB - 1)
    pass_final(0)
    pass_final(1)

    pltpu.make_async_copy(final, final, fin_recv).wait()
    dy, dz = (c // 4 - y + 4) % 4, (c % 4 - z + 4) % 4

    def among(offsets):
        return functools.reduce(jnp.logical_or, [(dy == a) & (dz == b) for a, b in offsets])

    diagonal, halved, flip = among(((0, 0),)), among(HALVED), among(MIRRORED)
    scale = 1.0 / float(NC * cells)

    def write(i, j, tile):
        out[i * S : (i + 1) * S, j * S : (j + 1) * S] = tile

    def tile(i, j):
        return final[i, j].reshape(S, S) * scale

    below = [(i, j) for i in range(R) for j in range(i)]
    above = [(i, j) for j, i in below]
    even = [(i, i) for i in range(R)]

    @pl.when(diagonal)
    def _():
        for i, j in below:
            write(i, j, tile(i, j))
            write(j, i, tile(i, j).T)
        for i, j in even:
            write(i, j, tile(i, j))

    @pl.when(jnp.logical_not(diagonal))
    def _():

        @pl.when(flip)
        def _():
            for i, j in below + even + above:
                write(j, i, tile(i, j).T)

        @pl.when(jnp.logical_not(flip))
        def _():
            for i, j in below + even:
                write(i, j, tile(i, j))

            @pl.when(halved)
            def _():
                for i, j in above:
                    write(i, j, tile(i, j).T)

            @pl.when(jnp.logical_not(halved))
            def _():
                for i, j in above:
                    write(i, j, tile(i, j))

    for k, buf in ((0, colbuf), (1, rowbuf), (2, totbuf)):
        others(buf, stat_send.at[k]).wait()
    sent = 0
    for r in range(R):
        for b in range(5):
            for h in range(H):
                own_to(b, r, h, to_zp).wait_send()
    for r in range(NB):
        core_copy(r).wait_send()
        for k in ("ep", "em", "dp", "dm", "fp", "fm"):
            x_copy(r, k).wait_send()
        zl_copy(r).wait_send()
        k = 0
        for src, ti, tj, row, col, maybe in final_sends(r):
            if maybe:

                @pl.when(col // 8 != zl)
                def _():
                    first_leg(r, src, ti, tj, row, col, fin_own.at[r, k]).wait_send()

                k += 1
            else:
                sent += src.shape[0]
    for d in range(1, 8):
        for k in range(3):
            second_leg((c % 8 + d) % 8, k).wait_send()
    assert sent % 16 == 0
    pltpu.make_async_copy(prods[2].at[0 : sent // 16], prods[2].at[0 : sent // 16], fin_send).wait()


def body(counts):
    cells, genes = counts.shape
    S = genes // R
    ns = [n for n, _ in ROUNDS]
    f32 = jnp.float32
    dma = pltpu.SemaphoreType.DMA
    own_groups = max(sum(PAIRS[gr[0]][0] == OWN for gr in groups) for _, groups in ROUNDS)
    scratch = [
        pltpu.VMEM((cells // 128, genes, 128), f32),
        pltpu.VMEM((NC, 8, 128), f32),
        pltpu.VMEM((NC, 8, 128), f32),
        pltpu.VMEM((NC, 8, 128), f32),
        pltpu.VMEM((R, S, cells), jnp.bfloat16),
        pltpu.VMEM((R, 5, S, cells), jnp.bfloat16),
        pltpu.VMEM((8, R, R, 2, S // 16, S), f32),
        pltpu.VMEM((R, R, 16, S // 16, S), f32),
        *[pltpu.VMEM((n, 8, S // 8, S), f32) for n in ns],
        *[pltpu.VMEM((n, 4, S // 8, S), f32) for n in ns],
        *[pltpu.VMEM((n, S // 8, S), f32) for n in ns],
        *[pltpu.VMEM((2, n, S // 8, S), f32) for n in ns],
        *[pltpu.VMEM((n, S // 16, S), f32) for n in ns],
        dma((3,)),
        dma((3,)),
        dma((5, R, H)),
        dma((5, R, H)),
        dma((NB, 8)),
        dma((NB, 8)),
        dma(()),
        dma((NB, own_groups)),
        dma((2, 8)),
        dma((3, 8)),
        dma(()),
    ]
    return pl.pallas_call(
        kernel,
        out_shape=jax.ShapeDtypeStruct((genes, genes), f32),
        in_specs=[pl.BlockSpec(memory_space=pltpu.VMEM)],
        out_specs=pl.BlockSpec(memory_space=pltpu.VMEM),
        scratch_shapes=scratch,
        compiler_params=pltpu.CompilerParams(
            collective_id=0, has_side_effects=True, vmem_limit_bytes=60 * 1024 * 1024
        ),
    )(counts)


def solution(mesh):
    return jax.shard_map(
        body,
        mesh=mesh,
        in_specs=(P("cell", "gene"),),
        out_specs=P("gene", "cell"),
        check_vma=False,
    )
```

```python
import functools

import jax
import jax.numpy as jnp
from jax import lax
from jax.experimental import pallas as pl
from jax.experimental.pallas import tpu as pltpu
from jax.sharding import PartitionSpec as P

MESH = pl.DeviceIdType.MESH
R = 4
H = 2
NC = 16
YP, ZP, T, Y2, ZM = range(5)
OWN = -1
OFFSET = {OWN: (0, 0), YP: (1, 0), ZP: (0, 1), T: (3, 3), Y2: (2, 3), ZM: (0, 3)}
PAIRS = (
    (OWN, OWN, None),
    (OWN, YP, "all"),
    (OWN, ZP, "all"),
    (YP, ZM, "all"),
    (OWN, Y2, "all"),
    (YP, ZP, "all"),
    (ZM, Y2, "below"),
    (ZP, T, "all"),
    (ZP, Y2, "below"),
    (ZP, ZM, "below"),
)
HALVED = ((2, 0), (0, 2), (2, 2))
MIRRORED = ((3, 0), (0, 3), (1, 1), (2, 1), (1, 3), (1, 2))


def whole_at(step):
    found = []
    if step < 2:
        found += [(1, r) for r in range(2 * step, 2 * step + 2)]
    if step < R:
        found += [(2, step)]
    if 0 < step < R:
        found += [(pair, r) for r in range(0 if step == 1 else step, step + 1) for pair in (3, 5)]
    if step:
        found += [(4, step - 1)]
    return found


def plan():
    batches = []
    for step in range(-1, R + 1):
        groups, n = [], 0

        def add(pair, count, i, j, along):
            nonlocal n
            groups.append((pair, n, count, i, j, along))
            n += count

        if step < 0:
            for i in range(R):
                add(0, i + 1, i, 0, "j")
        if step >= 0:
            for pair, r in whole_at(step):
                add(pair, R, 0, r, "i")
            if step < R:
                add(9, step + 1, step, 0, "j")
            if step:
                for pair in (6, 7, 8):
                    add(pair, step, step - 1, 0, "j")
                if step > 1:
                    add(7, step - 1, 0, step - 1, "i")
        batches.append((n, groups))
    return batches


ROUNDS = plan()
NB = len(ROUNDS)


def gene_at(y, z, offset):
    return ((y + offset[0]) % 4) * 4 + (z + offset[1]) % 4


def kernel(counts, out, *scratch):
    (vt, colbuf, rowbuf, totbuf, own, got, mid, final), rest = scratch[:8], scratch[8:]
    prods, rest = rest[:NB], rest[NB:]
    halves, rest = rest[:NB], rest[NB:]
    early, rest = rest[:NB], rest[NB:]
    late, rest = rest[:NB], rest[NB:]
    pieces, rest = rest[:NB], rest[NB:]
    (stat_send, stat_recv, in_send, in_recv, rs_send, rs_recv, fin_send, fin_own, mid_recv, mid_send, fin_recv) = rest
    genes, cells = own.shape[0] * own.shape[1], own.shape[2]
    S = genes // R
    nj = cells // 128
    c, g = lax.axis_index("cell"), lax.axis_index("gene")
    zl, x, core = c // 8, (c // 2) % 4, c % 2
    y, z = g // 4, g % 4
    pos = 8 * core + 2 * x + zl

    def cell_of(zl_, x_, core_):
        return {"cell": zl_ * 8 + x_ * 2 + core_}

    xp, xm = (x + 1) % 4, (x + 3) % 4
    to_xp, to_xm = cell_of(zl, xp, core), cell_of(zl, xm, core)
    to_core, to_zl = cell_of(zl, x, 1 - core), cell_of(1 - zl, x, core)
    to_yp, to_ym = {"gene": gene_at(y, z, (1, 0))}, {"gene": gene_at(y, z, (3, 0))}
    to_y2 = {"gene": gene_at(y, z, (2, 0))}
    to_zp, to_zm = {"gene": gene_at(y, z, (0, 1))}, {"gene": gene_at(y, z, (0, 3))}

    def remote(src, dst, ssem, rsem, device):
        return pltpu.make_async_remote_copy(
            src_ref=src, dst_ref=dst, send_sem=ssem, recv_sem=rsem, device_id=device, device_id_type=MESH
        )

    barrier = pltpu.get_barrier_semaphore()
    for k in range(1, NC):
        pl.semaphore_signal(barrier, inc=1, device_id={"cell": (c + k) % NC}, device_id_type=MESH)
        pl.semaphore_signal(barrier, inc=1, device_id={"gene": (g + k) % NC}, device_id_type=MESH)

    def local(j, acc):
        v = counts[pl.ds(j * 128, 128), :].astype(jnp.float32)
        t = v.T
        vt[j] = t
        rowbuf[g, pl.ds(j, 1), :] = jnp.sum(t, axis=0, keepdims=True)
        return acc + jnp.sum(v, axis=0, keepdims=True)

    nq = genes // 128
    colsum = lax.fori_loop(0, nj, local, jnp.zeros((1, genes), jnp.float32))
    colbuf[c] = jnp.zeros((8, 128), jnp.float32)
    for q in range(nq):
        colbuf[c, q : q + 1, :] = colsum[:, q * 128 : (q + 1) * 128]
    pl.semaphore_wait(barrier, 2 * (NC - 1))

    def spread(buf, axis, me, k):
        for d in range(1, NC):
            remote(buf.at[me], buf.at[me], stat_send.at[k], stat_recv.at[k], {axis: (me + d) % NC}).start()

    def others(buf, sem):
        return pltpu.make_async_copy(buf.at[0 : NC - 1], buf.at[0 : NC - 1], sem)

    spread(colbuf, "cell", c, 0)
    spread(rowbuf, "gene", g, 1)
    others(colbuf, stat_recv.at[0]).wait()
    totals = jnp.sum(colbuf[...], axis=0)
    totbuf[g] = jnp.broadcast_to(jnp.sum(totals, axis=0, keepdims=True), (8, 128))
    spread(totbuf, "gene", g, 2)
    gcol = [jnp.broadcast_to(totals[q : q + 1, :], (128, 128)).T for q in range(nq)]
    others(rowbuf, stat_recv.at[1]).wait()
    depths = jnp.sum(rowbuf[...], axis=0)
    others(totbuf, stat_recv.at[2]).wait()
    grand = jnp.sum(jnp.sum(totbuf[...], axis=0)[0:1, :])
    share = depths / grand
    ceiling = float(NC * cells) ** 0.5
    def part(h):
        return slice(h * (S // H), (h + 1) * (S // H))

    def own_to(b, r, h, device):
        return remote(own.at[r, part(h)], got.at[r, b, part(h)], in_send.at[b, r, h], in_recv.at[b, r, h], device)

    def arrived(b, r, h):
        own_to(b, r, h, to_zp).wait_recv()

    def pass_on(k, h):
        arrived(ZM, k, h)
        src = got.at[k, ZM, part(h)]
        for b, device in ((T, to_yp), (Y2, to_y2)):
            remote(src, got.at[k, b, part(h)], in_send.at[b, k, h], in_recv.at[b, k, h], device).start()

    def have(b, r):
        for h in range(H):
            arrived(b, r, h)

    assert S == 128
    for r in range(R):
        for j in range(nj):
            v = vt[j, r * S : (r + 1) * S, :]
            e = gcol[r] * share[j : j + 1, :]
            t = (v - e) * lax.rsqrt(e + e * e / 100.0)
            own[r, :, j * 128 : (j + 1) * 128] = jnp.clip(t, -ceiling, ceiling).astype(jnp.bfloat16)
        for h in range(H):
            own_to(ZM, r, h, to_zp).start()
            own_to(ZP, r, h, to_zm).start()
        if r < 2:
            for h in range(H):
                own_to(YP, r, h, to_ym).start()

    def nt(a, b):
        return lax.dot_general(a, b, (((1,), (1,)), ((), ())), preferred_element_type=jnp.float32)

    def put(r, t, tile):
        prods[r][t] = tile.reshape(8, S // 8, S)

    def base_of(m):
        base = {}
        for pair, t0, n, i, j, along in ROUNDS[m][1]:
            base.setdefault((pair, along), t0)
        return base

    def compute_diagonal():
        for i in range(R):
            d = nt(own[i], own[0 : i + 1].reshape((i + 1) * S, cells))
            for j in range(i + 1):
                put(0, i * (i + 1) // 2 + j, d[:, j * S : (j + 1) * S])

    def whole(m, pairs):
        for a in (OWN, YP):
            cols = [(gr[1], gr[4], PAIRS[gr[0]][1]) for gr in ROUNDS[m][1] if gr[0] in pairs and PAIRS[gr[0]][0] == a]
            for two in (cols[k : k + 2] for k in range(0, len(cols), 2)):

                @pl.loop(0, R // 2)
                def _(i):
                    rows = pl.ds(2 * i, 2)
                    left = (own[rows] if a == OWN else got[rows, a]).reshape(2 * S, cells)
                    right = [got[j, b] for _, j, b in two]
                    d = nt(left, jnp.concatenate(right, axis=0) if len(two) > 1 else right[0])
                    for u in range(2):
                        for k, (t0, _, _) in enumerate(two):
                            put(m, t0 + 2 * i + u, d[u * S : (u + 1) * S, k * S : (k + 1) * S])

    def corner(m, pair, r):
        (a, b, _), t0 = PAIRS[pair], base_of(m)[pair, "j"]
        d = nt(got[r, a], got[0 : r + 1, b].reshape((r + 1) * S, cells))
        for j in range(r + 1):
            put(m, t0 + j, d[:, j * S : (j + 1) * S])

    def compute_early(m):
        whole(m, (1, 2, 3, 5))
        corner(m, 9, m - 1)

    def compute_late(m):
        base, l = base_of(m), m - 2
        whole(m, (4,))
        for pair in (6, 7, 8):
            corner(m, pair, l)
        if l:
            d = nt(got[0:l, ZP].reshape(l * S, cells), got[l, T])
            for i in range(l):
                put(m, base[7, "i"] + i, d[i * S : (i + 1) * S])

    def rs(r, k, src, dst, device):
        return remote(src, dst, rs_send.at[r, k], rs_recv.at[r, k], device)

    def core_copy(r):
        return rs(r, 0, prods[r].at[:, pl.ds(4 * (1 - core), 4)], halves[r], to_core)

    def x_copy(r, k):
        n = ROUNDS[r][0]
        a, b, p, h = slice(0, n // 2), slice(n // 2, n), prods[r], 4 * core
        if k == "ep":
            return rs(r, 1, p.at[a, h + (x + 2) % 4], early[r].at[a], to_xp)
        if k == "em":
            return rs(r, 2, p.at[b, h + (x + 2) % 4], early[r].at[b], to_xm)
        if k == "dp":
            return rs(r, 3, p.at[b, h + xp], late[r].at[0, b], to_xp)
        if k == "dm":
            return rs(r, 4, p.at[a, h + xm], late[r].at[1, a], to_xm)
        if k == "fp":
            return rs(r, 5, p.at[a, h + xp], late[r].at[0, a], to_xp)
        return rs(r, 6, p.at[b, h + xm], late[r].at[1, b], to_xm)

    def zl_copy(r):
        s = S // 16
        return rs(r, 7, prods[r].at[:, 4 * core + x, pl.ds((1 - zl) * s, s)], pieces[r], to_zl)

    def s0(r):
        core_copy(r).start()

    def s1(r):
        n = ROUNDS[r][0]
        core_copy(r).wait_recv()

        @pl.loop(0, n)
        def _(t):
            prods[r][t, pl.ds(4 * core, 4)] = prods[r][t, pl.ds(4 * core, 4)] + halves[r][t]

        for k in ("ep", "em", "dp", "dm"):
            x_copy(r, k).start()

    def s2(r):
        n = ROUNDS[r][0]
        a, b = slice(0, n // 2), slice(n // 2, n)
        x_copy(r, "ep").wait_recv()
        prods[r][a, 4 * core + xp] = prods[r][a, 4 * core + xp] + early[r][a]
        x_copy(r, "fp").start()
        x_copy(r, "em").wait_recv()
        prods[r][b, 4 * core + xm] = prods[r][b, 4 * core + xm] + early[r][b]
        x_copy(r, "fm").start()

    def s3(r):
        for k in ("dp", "dm", "fp", "fm"):
            x_copy(r, k).wait_recv()
        prods[r][:, 4 * core + x] = prods[r][:, 4 * core + x] + late[r][0] + late[r][1]
        zl_copy(r).start()

    def final_sends(r):
        for pair, t0, n, i, j, along in ROUNDS[r][1]:
            a, b, both = PAIRS[pair]
            ga, gb = gene_at(y, z, OFFSET[a]), gene_at(y, z, OFFSET[b])
            ti, tj = (i, slice(j, j + n)) if along == "j" else (slice(i, i + n), j)
            yield pieces[r].at[t0 : t0 + n], ti, tj, ga, gb, a == OWN
            if both == "all":
                yield pieces[r].at[t0 : t0 + n], ti, tj, gb, ga, False
            if both == "below" and i:
                yield pieces[r].at[t0 : t0 + i], slice(0, i), i, gb, ga, False

    def first_leg(r, src, ti, tj, row, col, sem):
        to = {"cell": (col // 8) * 8 + c % 8, "gene": row}
        return remote(src, mid.at[col % 8, ti, tj, zl], sem, mid_recv.at[r // (NB - 1), col % 8], to)

    def s4(r):
        s = S // 16
        zl_copy(r).wait_recv()
        pieces[r][...] = pieces[r][...] + prods[r][:, 4 * core + x, pl.ds(zl * s, s)]
        k = 0
        for src, ti, tj, row, col, maybe in final_sends(r):
            if maybe:

                @pl.when(col // 8 == zl)
                def _():
                    pltpu.make_async_copy(src, mid.at[col % 8, ti, tj, zl], mid_recv.at[r // (NB - 1), col % 8]).start()

                @pl.when(col // 8 != zl)
                def _():
                    first_leg(r, src, ti, tj, row, col, fin_own.at[r, k]).start()

                k += 1
            else:
                first_leg(r, src, ti, tj, row, col, fin_send).start()

    regions = ((slice(0, R - 1), slice(0, R - 1)), (R - 1, slice(0, R)), (slice(0, R - 1), R - 1))

    def second_leg(s, k):
        ti, tj = regions[k]
        dst = final.at[ti, tj, pl.ds(pos - zl, 2)]
        return remote(mid.at[s, ti, tj], dst, mid_send.at[k, s], fin_recv, {"cell": zl * 8 + s})

    def pass_final(phase):
        inner, rows = (R - 1) * (R - 1), R * (R - 1)
        for d in range(8):
            s = (c % 8 + d) % 8
            col = zl * 8 + s
            dy, dz = (col // 4 - y + 4) % 4, (col % 4 - z + 4) % 4
            diagonal = col == g
            lagging = (dy == 2) & ((dz == 1) | (dz == 3))
            inward = ((dz == 2) & (dy != 0)) | ((dz == 0) & (dy == 2))

            def await_tiles(n):
                like = late[2].at[0, 0:n]
                pltpu.make_async_copy(like, like, mid_recv.at[phase, s]).wait()

            @pl.when(lagging)
            def _():
                await_tiles(R if phase else rows)

            @pl.when(inward)
            def _():
                await_tiles(R * R - inner if phase else inner)

            if phase == 0:

                @pl.when(diagonal)
                def _():
                    await_tiles(R * (R + 1) // 2)

                @pl.when(jnp.logical_not(diagonal | lagging | inward))
                def _():
                    await_tiles(R * R)

            for k in (1, 2) if phase else (0,):
                if d:
                    second_leg(s, k).start()
                else:
                    ti, tj = regions[k]
                    pltpu.make_async_copy(mid.at[s, ti, tj], final.at[ti, tj, pl.ds(pos - zl, 2)], fin_recv).start()

    compute_diagonal()
    s0(0)
    s1(0)
    pass_on(0, 0)
    for k in range(R + 1):
        m = k + 1
        if k < R:
            for h in range(1, H):
                pass_on(k, h)
            if k == 0:
                for r in range(2, R):
                    for h in range(H):
                        own_to(YP, r, h, to_ym).start()
        if k < R:
            have(ZP, k)
            for r in range(2 * k, 2 * k + 2 if k < 2 else 0):
                have(YP, r)
            compute_early(m)
        if k:
            have(T, k - 1)
            have(Y2, k - 1)
            compute_late(m)
        s0(m)
        if k == R:
            s1(m)
            s3(m - 1)
            s2(m)
            continue
        s2(m - 1)
        if k:
            s3(m - 2)
        s1(m)
        if k + 1 < R:
            pass_on(k + 1, 0)
            continue
        for done in range(m - 1):
            s4(done)
        s2(m)
        s3(m - 1)
        s4(m - 1)
    s4(NB - 2)
    s3(NB - 1)
    s4(NB - 1)
    pass_final(0)
    pass_final(1)

    pltpu.make_async_copy(final, final, fin_recv).wait()
    dy, dz = (c // 4 - y + 4) % 4, (c % 4 - z + 4) % 4

    def among(offsets):
        return functools.reduce(jnp.logical_or, [(dy == a) & (dz == b) for a, b in offsets])

    diagonal, halved, flip = among(((0, 0),)), among(HALVED), among(MIRRORED)
    scale = 1.0 / float(NC * cells)

    def write(i, j, tile):
        out[i * S : (i + 1) * S, j * S : (j + 1) * S] = tile

    def tile(i, j):
        return final[i, j].reshape(S, S) * scale

    below = [(i, j) for i in range(R) for j in range(i)]
    above = [(i, j) for j, i in below]
    even = [(i, i) for i in range(R)]

    @pl.when(diagonal)
    def _():
        for i, j in below:
            write(i, j, tile(i, j))
            write(j, i, tile(i, j).T)
        for i, j in even:
            write(i, j, tile(i, j))

    @pl.when(jnp.logical_not(diagonal))
    def _():

        @pl.when(flip)
        def _():
            for i, j in below + even + above:
                write(j, i, tile(i, j).T)

        @pl.when(jnp.logical_not(flip))
        def _():
            for i, j in below + even:
                write(i, j, tile(i, j))

            @pl.when(halved)
            def _():
                for i, j in above:
                    write(i, j, tile(i, j).T)

            @pl.when(jnp.logical_not(halved))
            def _():
                for i, j in above:
                    write(i, j, tile(i, j))

    for k, buf in ((0, colbuf), (1, rowbuf), (2, totbuf)):
        others(buf, stat_send.at[k]).wait()
    sent = 0
    for r in range(R):
        for b in range(5):
            for h in range(H):
                own_to(b, r, h, to_zp).wait_send()
    for r in range(NB):
        core_copy(r).wait_send()
        for k in ("ep", "em", "dp", "dm", "fp", "fm"):
            x_copy(r, k).wait_send()
        zl_copy(r).wait_send()
        k = 0
        for src, ti, tj, row, col, maybe in final_sends(r):
            if maybe:

                @pl.when(col // 8 != zl)
                def _():
                    first_leg(r, src, ti, tj, row, col, fin_own.at[r, k]).wait_send()

                k += 1
            else:
                sent += src.shape[0]
    for d in range(1, 8):
        for k in range(3):
            second_leg((c % 8 + d) % 8, k).wait_send()
    assert sent % 16 == 0
    pltpu.make_async_copy(prods[2].at[0 : sent // 16], prods[2].at[0 : sent // 16], fin_send).wait()


def body(counts):
    cells, genes = counts.shape
    S = genes // R
    ns = [n for n, _ in ROUNDS]
    f32 = jnp.float32
    dma = pltpu.SemaphoreType.DMA
    own_groups = max(sum(PAIRS[gr[0]][0] == OWN for gr in groups) for _, groups in ROUNDS)
    scratch = [
        pltpu.VMEM((cells // 128, genes, 128), f32),
        pltpu.VMEM((NC, 8, 128), f32),
        pltpu.VMEM((NC, 8, 128), f32),
        pltpu.VMEM((NC, 8, 128), f32),
        pltpu.VMEM((R, S, cells), jnp.bfloat16),
        pltpu.VMEM((R, 5, S, cells), jnp.bfloat16),
        pltpu.VMEM((8, R, R, 2, S // 16, S), f32),
        pltpu.VMEM((R, R, 16, S // 16, S), f32),
        *[pltpu.VMEM((n, 8, S // 8, S), f32) for n in ns],
        *[pltpu.VMEM((n, 4, S // 8, S), f32) for n in ns],
        *[pltpu.VMEM((n, S // 8, S), f32) for n in ns],
        *[pltpu.VMEM((2, n, S // 8, S), f32) for n in ns],
        *[pltpu.VMEM((n, S // 16, S), f32) for n in ns],
        dma((3,)),
        dma((3,)),
        dma((5, R, H)),
        dma((5, R, H)),
        dma((NB, 8)),
        dma((NB, 8)),
        dma(()),
        dma((NB, own_groups)),
        dma((2, 8)),
        dma((3, 8)),
        dma(()),
    ]
    return pl.pallas_call(
        kernel,
        out_shape=jax.ShapeDtypeStruct((genes, genes), f32),
        in_specs=[pl.BlockSpec(memory_space=pltpu.VMEM)],
        out_specs=pl.BlockSpec(memory_space=pltpu.VMEM),
        scratch_shapes=scratch,
        compiler_params=pltpu.CompilerParams(
            collective_id=0, has_side_effects=True, vmem_limit_bytes=60 * 1024 * 1024
        ),
    )(counts)


def solution(mesh):
    return jax.shard_map(
        body,
        mesh=mesh,
        in_specs=(P("cell", "gene"),),
        out_specs=P("gene", "cell"),
        check_vma=False,
    )
```

```python
import functools

import jax
import jax.numpy as jnp
from jax import lax
from jax.experimental import pallas as pl
from jax.experimental.pallas import tpu as pltpu
from jax.sharding import PartitionSpec as P

MESH = pl.DeviceIdType.MESH
R = 4
H = 4
NC = 16
YP, ZP, T, Y2, ZM = range(5)
OWN = -1
OFFSET = {OWN: (0, 0), YP: (1, 0), ZP: (0, 1), T: (3, 3), Y2: (2, 3), ZM: (0, 3)}
PAIRS = (
    (OWN, OWN, None),
    (OWN, YP, "all"),
    (OWN, ZP, "all"),
    (YP, ZM, "all"),
    (OWN, Y2, "all"),
    (YP, ZP, "all"),
    (ZM, Y2, "below"),
    (ZP, T, "all"),
    (ZP, Y2, "below"),
    (ZP, ZM, "below"),
)
HALVED = ((2, 0), (0, 2), (2, 2))
MIRRORED = ((3, 0), (0, 3), (1, 1), (2, 1), (1, 3), (1, 2))


def whole_at(step):
    found = []
    if step < 2:
        found += [(1, r) for r in range(2 * step, 2 * step + 2)]
    if step < R:
        found += [(2, step)]
    if 0 < step < R:
        found += [(pair, r) for r in range(0 if step == 1 else step, step + 1) for pair in (3, 5)]
    if step:
        found += [(4, step - 1)]
    return found


def plan():
    batches = []
    for step in range(-1, R + 1):
        groups, n = [], 0

        def add(pair, count, i, j, along):
            nonlocal n
            groups.append((pair, n, count, i, j, along))
            n += count

        if step < 0:
            for i in range(R):
                add(0, i + 1, i, 0, "j")
        if step >= 0:
            for pair, r in whole_at(step):
                add(pair, R, 0, r, "i")
            if step < R:
                add(9, step + 1, step, 0, "j")
            if step:
                for pair in (6, 7, 8):
                    add(pair, step, step - 1, 0, "j")
                if step > 1:
                    add(7, step - 1, 0, step - 1, "i")
        batches.append((n, groups))
    return batches


ROUNDS = plan()
NB = len(ROUNDS)


def gene_at(y, z, offset):
    return ((y + offset[0]) % 4) * 4 + (z + offset[1]) % 4


def kernel(counts, out, *scratch):
    (vt, colbuf, rowbuf, totbuf, own, got, mid, final), rest = scratch[:8], scratch[8:]
    prods, rest = rest[:NB], rest[NB:]
    halves, rest = rest[:NB], rest[NB:]
    early, rest = rest[:NB], rest[NB:]
    late, rest = rest[:NB], rest[NB:]
    pieces, rest = rest[:NB], rest[NB:]
    (stat_send, stat_recv, in_send, in_recv, rs_send, rs_recv, fin_send, fin_own, mid_recv, mid_send, fin_recv) = rest
    genes, cells = own.shape[0] * own.shape[1], own.shape[2]
    S = genes // R
    nj = cells // 128
    c, g = lax.axis_index("cell"), lax.axis_index("gene")
    zl, x, core = c // 8, (c // 2) % 4, c % 2
    y, z = g // 4, g % 4
    pos = 8 * core + 2 * x + zl

    def cell_of(zl_, x_, core_):
        return {"cell": zl_ * 8 + x_ * 2 + core_}

    xp, xm = (x + 1) % 4, (x + 3) % 4
    to_xp, to_xm = cell_of(zl, xp, core), cell_of(zl, xm, core)
    to_core, to_zl = cell_of(zl, x, 1 - core), cell_of(1 - zl, x, core)
    to_yp, to_ym = {"gene": gene_at(y, z, (1, 0))}, {"gene": gene_at(y, z, (3, 0))}
    to_y2 = {"gene": gene_at(y, z, (2, 0))}
    to_zp, to_zm = {"gene": gene_at(y, z, (0, 1))}, {"gene": gene_at(y, z, (0, 3))}

    def remote(src, dst, ssem, rsem, device):
        return pltpu.make_async_remote_copy(
            src_ref=src, dst_ref=dst, send_sem=ssem, recv_sem=rsem, device_id=device, device_id_type=MESH
        )

    barrier = pltpu.get_barrier_semaphore()
    for k in range(1, NC):
        pl.semaphore_signal(barrier, inc=1, device_id={"cell": (c + k) % NC}, device_id_type=MESH)
        pl.semaphore_signal(barrier, inc=1, device_id={"gene": (g + k) % NC}, device_id_type=MESH)

    def local(j, acc):
        v = counts[pl.ds(j * 128, 128), :].astype(jnp.float32)
        t = v.T
        vt[j] = t
        rowbuf[g, pl.ds(j, 1), :] = jnp.sum(t, axis=0, keepdims=True)
        return acc + jnp.sum(v, axis=0, keepdims=True)

    nq = genes // 128
    colsum = lax.fori_loop(0, nj, local, jnp.zeros((1, genes), jnp.float32))
    colbuf[c] = jnp.zeros((8, 128), jnp.float32)
    for q in range(nq):
        colbuf[c, q : q + 1, :] = colsum[:, q * 128 : (q + 1) * 128]
    pl.semaphore_wait(barrier, 2 * (NC - 1))

    def spread(buf, axis, me, k):
        for d in range(1, NC):
            remote(buf.at[me], buf.at[me], stat_send.at[k], stat_recv.at[k], {axis: (me + d) % NC}).start()

    def others(buf, sem):
        return pltpu.make_async_copy(buf.at[0 : NC - 1], buf.at[0 : NC - 1], sem)

    spread(colbuf, "cell", c, 0)
    spread(rowbuf, "gene", g, 1)
    others(colbuf, stat_recv.at[0]).wait()
    totals = jnp.sum(colbuf[...], axis=0)
    totbuf[g] = jnp.broadcast_to(jnp.sum(totals, axis=0, keepdims=True), (8, 128))
    spread(totbuf, "gene", g, 2)
    gcol = [jnp.broadcast_to(totals[q : q + 1, :], (128, 128)).T for q in range(nq)]
    others(rowbuf, stat_recv.at[1]).wait()
    depths = jnp.sum(rowbuf[...], axis=0)
    others(totbuf, stat_recv.at[2]).wait()
    grand = jnp.sum(jnp.sum(totbuf[...], axis=0)[0:1, :])
    share = depths / grand
    ceiling = float(NC * cells) ** 0.5
    def part(h):
        return slice(h * (S // H), (h + 1) * (S // H))

    def own_to(b, r, h, device):
        return remote(own.at[r, part(h)], got.at[r, b, part(h)], in_send.at[b, r, h], in_recv.at[b, r, h], device)

    def arrived(b, r, h):
        own_to(b, r, h, to_zp).wait_recv()

    def pass_on(k, h):
        arrived(ZM, k, h)
        src = got.at[k, ZM, part(h)]
        for b, device in ((T, to_yp), (Y2, to_y2)):
            remote(src, got.at[k, b, part(h)], in_send.at[b, k, h], in_recv.at[b, k, h], device).start()

    def have(b, r):
        for h in range(H):
            arrived(b, r, h)

    assert S == 128
    for r in range(R):
        for j in range(nj):
            v = vt[j, r * S : (r + 1) * S, :]
            e = gcol[r] * share[j : j + 1, :]
            t = (v - e) * lax.rsqrt(e + e * e / 100.0)
            own[r, :, j * 128 : (j + 1) * 128] = jnp.clip(t, -ceiling, ceiling).astype(jnp.bfloat16)
        for h in range(H):
            own_to(ZM, r, h, to_zp).start()
            own_to(ZP, r, h, to_zm).start()
        if r < 2:
            for h in range(H):
                own_to(YP, r, h, to_ym).start()

    def nt(a, b):
        return lax.dot_general(a, b, (((1,), (1,)), ((), ())), preferred_element_type=jnp.float32)

    def put(r, t, tile):
        prods[r][t] = tile.reshape(8, S // 8, S)

    def base_of(m):
        base = {}
        for pair, t0, n, i, j, along in ROUNDS[m][1]:
            base.setdefault((pair, along), t0)
        return base

    def compute_diagonal():
        for i in range(R):
            d = nt(own[i], own[0 : i + 1].reshape((i + 1) * S, cells))
            for j in range(i + 1):
                put(0, i * (i + 1) // 2 + j, d[:, j * S : (j + 1) * S])

    def whole(m, pairs):
        for a in (OWN, YP):
            cols = [(gr[1], gr[4], PAIRS[gr[0]][1]) for gr in ROUNDS[m][1] if gr[0] in pairs and PAIRS[gr[0]][0] == a]
            for two in (cols[k : k + 2] for k in range(0, len(cols), 2)):

                @pl.loop(0, R // 2)
                def _(i):
                    rows = pl.ds(2 * i, 2)
                    left = (own[rows] if a == OWN else got[rows, a]).reshape(2 * S, cells)
                    right = [got[j, b] for _, j, b in two]
                    d = nt(left, jnp.concatenate(right, axis=0) if len(two) > 1 else right[0])
                    for u in range(2):
                        for k, (t0, _, _) in enumerate(two):
                            put(m, t0 + 2 * i + u, d[u * S : (u + 1) * S, k * S : (k + 1) * S])

    def corner(m, pair, r):
        (a, b, _), t0 = PAIRS[pair], base_of(m)[pair, "j"]
        d = nt(got[r, a], got[0 : r + 1, b].reshape((r + 1) * S, cells))
        for j in range(r + 1):
            put(m, t0 + j, d[:, j * S : (j + 1) * S])

    def compute_early(m):
        whole(m, (1, 2, 3, 5))
        corner(m, 9, m - 1)

    def compute_late(m):
        base, l = base_of(m), m - 2
        whole(m, (4,))
        for pair in (6, 7, 8):
            corner(m, pair, l)
        if l:
            d = nt(got[0:l, ZP].reshape(l * S, cells), got[l, T])
            for i in range(l):
                put(m, base[7, "i"] + i, d[i * S : (i + 1) * S])

    def rs(r, k, src, dst, device):
        return remote(src, dst, rs_send.at[r, k], rs_recv.at[r, k], device)

    def core_copy(r):
        return rs(r, 0, prods[r].at[:, pl.ds(4 * (1 - core), 4)], halves[r], to_core)

    def x_copy(r, k):
        n = ROUNDS[r][0]
        a, b, p, h = slice(0, n // 2), slice(n // 2, n), prods[r], 4 * core
        if k == "ep":
            return rs(r, 1, p.at[a, h + (x + 2) % 4], early[r].at[a], to_xp)
        if k == "em":
            return rs(r, 2, p.at[b, h + (x + 2) % 4], early[r].at[b], to_xm)
        if k == "dp":
            return rs(r, 3, p.at[b, h + xp], late[r].at[0, b], to_xp)
        if k == "dm":
            return rs(r, 4, p.at[a, h + xm], late[r].at[1, a], to_xm)
        if k == "fp":
            return rs(r, 5, p.at[a, h + xp], late[r].at[0, a], to_xp)
        return rs(r, 6, p.at[b, h + xm], late[r].at[1, b], to_xm)

    def zl_copy(r):
        s = S // 16
        return rs(r, 7, prods[r].at[:, 4 * core + x, pl.ds((1 - zl) * s, s)], pieces[r], to_zl)

    def s0(r):
        core_copy(r).start()

    def s1(r):
        n = ROUNDS[r][0]
        core_copy(r).wait_recv()

        @pl.loop(0, n)
        def _(t):
            prods[r][t, pl.ds(4 * core, 4)] = prods[r][t, pl.ds(4 * core, 4)] + halves[r][t]

        for k in ("ep", "em", "dp", "dm"):
            x_copy(r, k).start()

    def s2(r):
        n = ROUNDS[r][0]
        a, b = slice(0, n // 2), slice(n // 2, n)
        x_copy(r, "ep").wait_recv()
        prods[r][a, 4 * core + xp] = prods[r][a, 4 * core + xp] + early[r][a]
        x_copy(r, "fp").start()
        x_copy(r, "em").wait_recv()
        prods[r][b, 4 * core + xm] = prods[r][b, 4 * core + xm] + early[r][b]
        x_copy(r, "fm").start()

    def s3(r):
        for k in ("dp", "dm", "fp", "fm"):
            x_copy(r, k).wait_recv()
        prods[r][:, 4 * core + x] = prods[r][:, 4 * core + x] + late[r][0] + late[r][1]
        zl_copy(r).start()

    def final_sends(r):
        for pair, t0, n, i, j, along in ROUNDS[r][1]:
            a, b, both = PAIRS[pair]
            ga, gb = gene_at(y, z, OFFSET[a]), gene_at(y, z, OFFSET[b])
            ti, tj = (i, slice(j, j + n)) if along == "j" else (slice(i, i + n), j)
            yield pieces[r].at[t0 : t0 + n], ti, tj, ga, gb, a == OWN
            if both == "all":
                yield pieces[r].at[t0 : t0 + n], ti, tj, gb, ga, False
            if both == "below" and i:
                yield pieces[r].at[t0 : t0 + i], slice(0, i), i, gb, ga, False

    def first_leg(r, src, ti, tj, row, col, sem):
        to = {"cell": (col // 8) * 8 + c % 8, "gene": row}
        return remote(src, mid.at[col % 8, ti, tj, zl], sem, mid_recv.at[r // (NB - 1), col % 8], to)

    def s4(r):
        s = S // 16
        zl_copy(r).wait_recv()
        pieces[r][...] = pieces[r][...] + prods[r][:, 4 * core + x, pl.ds(zl * s, s)]
        k = 0
        for src, ti, tj, row, col, maybe in final_sends(r):
            if maybe:

                @pl.when(col // 8 == zl)
                def _():
                    pltpu.make_async_copy(src, mid.at[col % 8, ti, tj, zl], mid_recv.at[r // (NB - 1), col % 8]).start()

                @pl.when(col // 8 != zl)
                def _():
                    first_leg(r, src, ti, tj, row, col, fin_own.at[r, k]).start()

                k += 1
            else:
                first_leg(r, src, ti, tj, row, col, fin_send).start()

    regions = ((slice(0, R - 1), slice(0, R - 1)), (R - 1, slice(0, R)), (slice(0, R - 1), R - 1))

    def second_leg(s, k):
        ti, tj = regions[k]
        dst = final.at[ti, tj, pl.ds(pos - zl, 2)]
        return remote(mid.at[s, ti, tj], dst, mid_send.at[k, s], fin_recv.at[min(k, 1)], {"cell": zl * 8 + s})

    def pass_final(phase):
        inner, rows = (R - 1) * (R - 1), R * (R - 1)
        for d in range(8):
            s = (c % 8 + d) % 8
            col = zl * 8 + s
            dy, dz = (col // 4 - y + 4) % 4, (col % 4 - z + 4) % 4
            diagonal = col == g
            lagging = (dy == 2) & ((dz == 1) | (dz == 3))
            inward = ((dz == 2) & (dy != 0)) | ((dz == 0) & (dy == 2))

            def await_tiles(n):
                like = late[2].at[0, 0:n]
                pltpu.make_async_copy(like, like, mid_recv.at[phase, s]).wait()

            @pl.when(lagging)
            def _():
                await_tiles(R if phase else rows)

            @pl.when(inward)
            def _():
                await_tiles(R * R - inner if phase else inner)

            if phase == 0:

                @pl.when(diagonal)
                def _():
                    await_tiles(R * (R + 1) // 2)

                @pl.when(jnp.logical_not(diagonal | lagging | inward))
                def _():
                    await_tiles(R * R)

            for k in (1, 2) if phase else (0,):
                if d:
                    second_leg(s, k).start()
                else:
                    ti, tj = regions[k]
                    pltpu.make_async_copy(mid.at[s, ti, tj], final.at[ti, tj, pl.ds(pos - zl, 2)], fin_recv.at[min(k, 1)]).start()

    compute_diagonal()
    s0(0)
    s1(0)
    for h in range(H // 2):
        pass_on(0, h)
    for k in range(R + 1):
        m = k + 1
        if k < R:
            for h in range(H // 2, H):
                pass_on(k, h)
            if k == 0:
                for r in range(2, R):
                    for h in range(H):
                        own_to(YP, r, h, to_ym).start()
        if k < R:
            have(ZP, k)
            for r in range(2 * k, 2 * k + 2 if k < 2 else 0):
                have(YP, r)
            compute_early(m)
        if k:
            have(T, k - 1)
            have(Y2, k - 1)
            compute_late(m)
        s0(m)
        if k == R:
            s1(m)
            s3(m - 1)
            s2(m)
            continue
        s2(m - 1)
        if k:
            s3(m - 2)
        s1(m)
        if k + 1 < R:
            for h in range(H // 2):
                pass_on(k + 1, h)
            continue
        for done in range(m - 1):
            s4(done)
        s2(m)
        s3(m - 1)
        s4(m - 1)
    s4(NB - 2)
    s3(NB - 1)
    s4(NB - 1)
    pass_final(0)
    pass_final(1)

    dy, dz = (c // 4 - y + 4) % 4, (c % 4 - z + 4) % 4

    def among(offsets):
        return functools.reduce(jnp.logical_or, [(dy == a) & (dz == b) for a, b in offsets])

    diagonal, halved, flip = among(((0, 0),)), among(HALVED), among(MIRRORED)
    scale = 1.0 / float(NC * cells)

    def write(i, j, tile):
        out[i * S : (i + 1) * S, j * S : (j + 1) * S] = tile

    def tile(i, j):
        return final[i, j].reshape(S, S) * scale

    first = R - 1
    for tiles in ([(i, j) for i in range(first) for j in range(first)], [(i, j) for i in range(R) for j in range(R) if first in (i, j)]):
        phase = int(len(tiles) < first * first)
        like = prods[2].at[0 : len(tiles)]
        pltpu.make_async_copy(like, like, fin_recv.at[phase]).wait()
        lower = [t for t in tiles if t[0] >= t[1]]
        above = [t for t in tiles if t[0] < t[1]]

        @pl.when(flip)
        def _():
            for i, j in tiles:
                write(j, i, tile(i, j).T)

        @pl.when(jnp.logical_not(flip))
        def _():
            for i, j in lower:
                write(i, j, tile(i, j))

        @pl.when(diagonal)
        def _():
            for i, j in lower:
                if i > j:
                    write(j, i, tile(i, j).T)

        @pl.when(halved)
        def _():
            for i, j in above:
                write(i, j, tile(i, j).T)

        @pl.when(jnp.logical_not(flip | diagonal | halved))
        def _():
            for i, j in above:
                write(i, j, tile(i, j))

    for k, buf in ((0, colbuf), (1, rowbuf), (2, totbuf)):
        others(buf, stat_send.at[k]).wait()
    sent = 0
    for r in range(R):
        for b in range(5):
            for h in range(H):
                own_to(b, r, h, to_zp).wait_send()
    for r in range(NB):
        core_copy(r).wait_send()
        for k in ("ep", "em", "dp", "dm", "fp", "fm"):
            x_copy(r, k).wait_send()
        zl_copy(r).wait_send()
        k = 0
        for src, ti, tj, row, col, maybe in final_sends(r):
            if maybe:

                @pl.when(col // 8 != zl)
                def _():
                    first_leg(r, src, ti, tj, row, col, fin_own.at[r, k]).wait_send()

                k += 1
            else:
                sent += src.shape[0]
    for d in range(1, 8):
        for k in range(3):
            second_leg((c % 8 + d) % 8, k).wait_send()
    assert sent % 16 == 0
    pltpu.make_async_copy(prods[2].at[0 : sent // 16], prods[2].at[0 : sent // 16], fin_send).wait()


def body(counts):
    cells, genes = counts.shape
    S = genes // R
    ns = [n for n, _ in ROUNDS]
    f32 = jnp.float32
    dma = pltpu.SemaphoreType.DMA
    own_groups = max(sum(PAIRS[gr[0]][0] == OWN for gr in groups) for _, groups in ROUNDS)
    scratch = [
        pltpu.VMEM((cells // 128, genes, 128), f32),
        pltpu.VMEM((NC, 8, 128), f32),
        pltpu.VMEM((NC, 8, 128), f32),
        pltpu.VMEM((NC, 8, 128), f32),
        pltpu.VMEM((R, S, cells), jnp.bfloat16),
        pltpu.VMEM((R, 5, S, cells), jnp.bfloat16),
        pltpu.VMEM((8, R, R, 2, S // 16, S), f32),
        pltpu.VMEM((R, R, 16, S // 16, S), f32),
        *[pltpu.VMEM((n, 8, S // 8, S), f32) for n in ns],
        *[pltpu.VMEM((n, 4, S // 8, S), f32) for n in ns],
        *[pltpu.VMEM((n, S // 8, S), f32) for n in ns],
        *[pltpu.VMEM((2, n, S // 8, S), f32) for n in ns],
        *[pltpu.VMEM((n, S // 16, S), f32) for n in ns],
        dma((3,)),
        dma((3,)),
        dma((5, R, H)),
        dma((5, R, H)),
        dma((NB, 8)),
        dma((NB, 8)),
        dma(()),
        dma((NB, own_groups)),
        dma((2, 8)),
        dma((3, 8)),
        dma((2,)),
    ]
    return pl.pallas_call(
        kernel,
        out_shape=jax.ShapeDtypeStruct((genes, genes), f32),
        in_specs=[pl.BlockSpec(memory_space=pltpu.VMEM)],
        out_specs=pl.BlockSpec(memory_space=pltpu.VMEM),
        scratch_shapes=scratch,
        compiler_params=pltpu.CompilerParams(
            collective_id=0, has_side_effects=True, vmem_limit_bytes=60 * 1024 * 1024
        ),
    )(counts)


def solution(mesh):
    return jax.shard_map(
        body,
        mesh=mesh,
        in_specs=(P("cell", "gene"),),
        out_specs=P("gene", "cell"),
        check_vma=False,
    )
```

```python
import functools

import jax
import jax.numpy as jnp
from jax import lax
from jax.experimental import pallas as pl
from jax.experimental.pallas import tpu as pltpu
from jax.sharding import PartitionSpec as P

MESH = pl.DeviceIdType.MESH
R = 4
H = 2
NC = 16
YP, ZP, T, Y2, ZM = range(5)
OWN = -1
OFFSET = {OWN: (0, 0), YP: (1, 0), ZP: (0, 1), T: (3, 3), Y2: (2, 3), ZM: (0, 3)}
PAIRS = (
    (OWN, OWN, None),
    (OWN, YP, "all"),
    (OWN, ZP, "all"),
    (YP, ZM, "all"),
    (OWN, Y2, "all"),
    (YP, ZP, "all"),
    (ZM, Y2, "below"),
    (ZP, T, "all"),
    (ZP, Y2, "below"),
    (ZP, ZM, "below"),
)
HALVED = ((2, 0), (0, 2), (2, 2))
MIRRORED = ((3, 0), (0, 3), (1, 1), (2, 1), (1, 3), (1, 2))


def whole_at(step):
    found = []
    if step < 2:
        found += [(1, r) for r in range(2 * step, 2 * step + 2)]
    if step < R:
        found += [(2, step)]
    if 0 < step < R:
        found += [(pair, r) for r in range(0 if step == 1 else step, step + 1) for pair in (3, 5)]
    if step:
        found += [(4, step - 1)]
    return found


def plan():
    batches = []
    for step in range(-1, R + 1):
        groups, n = [], 0

        def add(pair, count, i, j, along):
            nonlocal n
            groups.append((pair, n, count, i, j, along))
            n += count

        if step < 0:
            for i in range(R):
                add(0, i + 1, i, 0, "j")
        if step >= 0:
            for pair, r in whole_at(step):
                add(pair, R, 0, r, "i")
            if step < R:
                add(9, step + 1, step, 0, "j")
            if step:
                for pair in (6, 7, 8):
                    add(pair, step, step - 1, 0, "j")
                if step > 1:
                    add(7, step - 1, 0, step - 1, "i")
        batches.append((n, groups))
    return batches


ROUNDS = plan()
NB = len(ROUNDS)


def gene_at(y, z, offset):
    return ((y + offset[0]) % 4) * 4 + (z + offset[1]) % 4


def kernel(counts, out, *scratch):
    (vt, colbuf, rowbuf, totbuf, own, got, mid, final), rest = scratch[:8], scratch[8:]
    prods, rest = rest[:NB], rest[NB:]
    halves, rest = rest[:NB], rest[NB:]
    early, rest = rest[:NB], rest[NB:]
    late, rest = rest[:NB], rest[NB:]
    pieces, rest = rest[:NB], rest[NB:]
    (stat_send, stat_recv, in_send, in_recv, rs_send, rs_recv, fin_send, fin_own, mid_recv, mid_send, fin_recv) = rest
    genes, cells = own.shape[0] * own.shape[1], own.shape[2]
    S = genes // R
    nj = cells // 128
    c, g = lax.axis_index("cell"), lax.axis_index("gene")
    zl, x, core = c // 8, (c // 2) % 4, c % 2
    y, z = g // 4, g % 4
    pos = 8 * core + 2 * x + zl

    def cell_of(zl_, x_, core_):
        return {"cell": zl_ * 8 + x_ * 2 + core_}

    xp, xm = (x + 1) % 4, (x + 3) % 4
    to_xp, to_xm = cell_of(zl, xp, core), cell_of(zl, xm, core)
    to_core, to_zl = cell_of(zl, x, 1 - core), cell_of(1 - zl, x, core)
    to_yp, to_ym = {"gene": gene_at(y, z, (1, 0))}, {"gene": gene_at(y, z, (3, 0))}
    to_y2 = {"gene": gene_at(y, z, (2, 0))}
    to_zp, to_zm = {"gene": gene_at(y, z, (0, 1))}, {"gene": gene_at(y, z, (0, 3))}

    def remote(src, dst, ssem, rsem, device):
        return pltpu.make_async_remote_copy(
            src_ref=src, dst_ref=dst, send_sem=ssem, recv_sem=rsem, device_id=device, device_id_type=MESH
        )

    barrier = pltpu.get_barrier_semaphore()
    for k in range(1, NC):
        pl.semaphore_signal(barrier, inc=1, device_id={"cell": (c + k) % NC}, device_id_type=MESH)
        pl.semaphore_signal(barrier, inc=1, device_id={"gene": (g + k) % NC}, device_id_type=MESH)

    def local(j, acc):
        v = counts[pl.ds(j * 128, 128), :].astype(jnp.float32)
        t = v.T
        vt[j] = t
        rowbuf[g, pl.ds(j, 1), :] = jnp.sum(t, axis=0, keepdims=True)
        return acc + jnp.sum(v, axis=0, keepdims=True)

    nq = genes // 128
    colsum = lax.fori_loop(0, nj, local, jnp.zeros((1, genes), jnp.float32))
    colbuf[c] = jnp.zeros((8, 128), jnp.float32)
    for q in range(nq):
        colbuf[c, q : q + 1, :] = colsum[:, q * 128 : (q + 1) * 128]
    pl.semaphore_wait(barrier, 2 * (NC - 1))

    def spread(buf, axis, me, k):
        for d in range(1, NC):
            remote(buf.at[me], buf.at[me], stat_send.at[k], stat_recv.at[k], {axis: (me + d) % NC}).start()

    def others(buf, sem):
        return pltpu.make_async_copy(buf.at[0 : NC - 1], buf.at[0 : NC - 1], sem)

    spread(colbuf, "cell", c, 0)
    spread(rowbuf, "gene", g, 1)
    others(colbuf, stat_recv.at[0]).wait()
    totals = jnp.sum(colbuf[...], axis=0)
    totbuf[g] = jnp.broadcast_to(jnp.sum(totals, axis=0, keepdims=True), (8, 128))
    spread(totbuf, "gene", g, 2)
    gcol = [jnp.broadcast_to(totals[q : q + 1, :], (128, 128)).T for q in range(nq)]
    others(rowbuf, stat_recv.at[1]).wait()
    depths = jnp.sum(rowbuf[...], axis=0)
    others(totbuf, stat_recv.at[2]).wait()
    grand = jnp.sum(jnp.sum(totbuf[...], axis=0)[0:1, :])
    share = depths / grand
    ceiling = float(NC * cells) ** 0.5
    def part(h):
        return slice(h * (S // H), (h + 1) * (S // H))

    def own_to(b, r, h, device):
        return remote(own.at[r, part(h)], got.at[r, b, part(h)], in_send.at[b, r, h], in_recv.at[b, r, h], device)

    def arrived(b, r, h):
        own_to(b, r, h, to_zp).wait_recv()

    def pass_on(k, h):
        arrived(ZM, k, h)
        src = got.at[k, ZM, part(h)]
        for b, device in ((T, to_yp), (Y2, to_y2)):
            remote(src, got.at[k, b, part(h)], in_send.at[b, k, h], in_recv.at[b, k, h], device).start()

    def have(b, r):
        for h in range(H):
            arrived(b, r, h)

    assert S == 128
    for r in range(R):
        for j in range(nj):
            v = vt[j, r * S : (r + 1) * S, :]
            e = gcol[r] * share[j : j + 1, :]
            t = (v - e) * lax.rsqrt(e + e * e / 100.0)
            own[r, :, j * 128 : (j + 1) * 128] = jnp.clip(t, -ceiling, ceiling).astype(jnp.bfloat16)
        for h in range(H):
            own_to(ZM, r, h, to_zp).start()
            own_to(ZP, r, h, to_zm).start()
        if r < 2:
            for h in range(H):
                own_to(YP, r, h, to_ym).start()

    def nt(a, b):
        return lax.dot_general(a, b, (((1,), (1,)), ((), ())), preferred_element_type=jnp.float32)

    def put(r, t, tile):
        prods[r][t] = tile.reshape(8, S // 8, S)

    def base_of(m):
        base = {}
        for pair, t0, n, i, j, along in ROUNDS[m][1]:
            base.setdefault((pair, along), t0)
        return base

    def compute_diagonal():
        for i in range(R):
            d = nt(own[i], own[0 : i + 1].reshape((i + 1) * S, cells))
            for j in range(i + 1):
                put(0, i * (i + 1) // 2 + j, d[:, j * S : (j + 1) * S])

    def whole(m, pairs):
        for a in (OWN, YP):
            cols = [(gr[1], gr[4], PAIRS[gr[0]][1]) for gr in ROUNDS[m][1] if gr[0] in pairs and PAIRS[gr[0]][0] == a]
            for two in (cols[k : k + 2] for k in range(0, len(cols), 2)):

                @pl.loop(0, R // 2)
                def _(i):
                    rows = pl.ds(2 * i, 2)
                    left = (own[rows] if a == OWN else got[rows, a]).reshape(2 * S, cells)
                    right = [got[j, b] for _, j, b in two]
                    d = nt(left, jnp.concatenate(right, axis=0) if len(two) > 1 else right[0])
                    for u in range(2):
                        for k, (t0, _, _) in enumerate(two):
                            put(m, t0 + 2 * i + u, d[u * S : (u + 1) * S, k * S : (k + 1) * S])

    def corner(m, pair, r):
        (a, b, _), t0 = PAIRS[pair], base_of(m)[pair, "j"]
        d = nt(got[r, a], got[0 : r + 1, b].reshape((r + 1) * S, cells))
        for j in range(r + 1):
            put(m, t0 + j, d[:, j * S : (j + 1) * S])

    def compute_early(m):
        whole(m, (1, 2, 3, 5))
        corner(m, 9, m - 1)

    def compute_late(m):
        base, l = base_of(m), m - 2
        whole(m, (4,))
        for pair in (6, 7, 8):
            corner(m, pair, l)
        if l:
            d = nt(got[0:l, ZP].reshape(l * S, cells), got[l, T])
            for i in range(l):
                put(m, base[7, "i"] + i, d[i * S : (i + 1) * S])

    def rs(r, k, src, dst, device):
        return remote(src, dst, rs_send.at[r, k], rs_recv.at[r, k], device)

    def core_copy(r):
        return rs(r, 0, prods[r].at[:, pl.ds(4 * (1 - core), 4)], halves[r], to_core)

    def x_copy(r, k):
        n = ROUNDS[r][0]
        a, b, p, h = slice(0, n // 2), slice(n // 2, n), prods[r], 4 * core
        if k == "ep":
            return rs(r, 1, p.at[a, h + (x + 2) % 4], early[r].at[a], to_xp)
        if k == "em":
            return rs(r, 2, p.at[b, h + (x + 2) % 4], early[r].at[b], to_xm)
        if k == "dp":
            return rs(r, 3, p.at[b, h + xp], late[r].at[0, b], to_xp)
        if k == "dm":
            return rs(r, 4, p.at[a, h + xm], late[r].at[1, a], to_xm)
        if k == "fp":
            return rs(r, 5, p.at[a, h + xp], late[r].at[0, a], to_xp)
        return rs(r, 6, p.at[b, h + xm], late[r].at[1, b], to_xm)

    def zl_copy(r):
        s = S // 16
        return rs(r, 7, prods[r].at[:, 4 * core + x, pl.ds((1 - zl) * s, s)], pieces[r], to_zl)

    def s0(r):
        core_copy(r).start()

    def s1(r):
        n = ROUNDS[r][0]
        core_copy(r).wait_recv()

        @pl.loop(0, n)
        def _(t):
            prods[r][t, pl.ds(4 * core, 4)] = prods[r][t, pl.ds(4 * core, 4)] + halves[r][t]

        for k in ("ep", "em", "dp", "dm"):
            x_copy(r, k).start()

    def s2(r):
        n = ROUNDS[r][0]
        a, b = slice(0, n // 2), slice(n // 2, n)
        x_copy(r, "ep").wait_recv()
        prods[r][a, 4 * core + xp] = prods[r][a, 4 * core + xp] + early[r][a]
        x_copy(r, "fp").start()
        x_copy(r, "em").wait_recv()
        prods[r][b, 4 * core + xm] = prods[r][b, 4 * core + xm] + early[r][b]
        x_copy(r, "fm").start()

    def s3(r):
        for k in ("dp", "dm", "fp", "fm"):
            x_copy(r, k).wait_recv()
        prods[r][:, 4 * core + x] = prods[r][:, 4 * core + x] + late[r][0] + late[r][1]
        zl_copy(r).start()

    def final_sends(r):
        for pair, t0, n, i, j, along in ROUNDS[r][1]:
            a, b, both = PAIRS[pair]
            ga, gb = gene_at(y, z, OFFSET[a]), gene_at(y, z, OFFSET[b])
            ti, tj = (i, slice(j, j + n)) if along == "j" else (slice(i, i + n), j)
            yield pieces[r].at[t0 : t0 + n], ti, tj, ga, gb, a == OWN
            if both == "all":
                yield pieces[r].at[t0 : t0 + n], ti, tj, gb, ga, False
            if both == "below" and i:
                yield pieces[r].at[t0 : t0 + i], slice(0, i), i, gb, ga, False

    def first_leg(r, src, ti, tj, row, col, sem):
        to = {"cell": (col // 8) * 8 + c % 8, "gene": row}
        return remote(src, mid.at[col % 8, ti, tj, zl], sem, mid_recv.at[r // (NB - 1), col % 8], to)

    def s4(r):
        s = S // 16
        zl_copy(r).wait_recv()
        pieces[r][...] = pieces[r][...] + prods[r][:, 4 * core + x, pl.ds(zl * s, s)]
        k = 0
        for src, ti, tj, row, col, maybe in final_sends(r):
            if maybe:

                @pl.when(col // 8 == zl)
                def _():
                    pltpu.make_async_copy(src, mid.at[col % 8, ti, tj, zl], mid_recv.at[r // (NB - 1), col % 8]).start()

                @pl.when(col // 8 != zl)
                def _():
                    first_leg(r, src, ti, tj, row, col, fin_own.at[r, k]).start()

                k += 1
            else:
                first_leg(r, src, ti, tj, row, col, fin_send).start()

    regions = ((slice(0, R - 1), slice(0, R - 1)), (R - 1, slice(0, R)), (slice(0, R - 1), R - 1))

    def second_leg(s, k):
        ti, tj = regions[k]
        dst = final.at[ti, tj, pl.ds(pos - zl, 2)]
        return remote(mid.at[s, ti, tj], dst, mid_send.at[k, s], fin_recv.at[min(k, 1)], {"cell": zl * 8 + s})

    def pass_final(phase):
        inner, rows = (R - 1) * (R - 1), R * (R - 1)
        for d in range(8):
            s = (c % 8 + d) % 8
            col = zl * 8 + s
            dy, dz = (col // 4 - y + 4) % 4, (col % 4 - z + 4) % 4
            diagonal = col == g
            lagging = (dy == 2) & ((dz == 1) | (dz == 3))
            inward = ((dz == 2) & (dy != 0)) | ((dz == 0) & (dy == 2))

            def await_tiles(n):
                like = late[2].at[0, 0:n]
                pltpu.make_async_copy(like, like, mid_recv.at[phase, s]).wait()

            @pl.when(lagging)
            def _():
                await_tiles(R if phase else rows)

            @pl.when(inward)
            def _():
                await_tiles(R * R - inner if phase else inner)

            if phase == 0:

                @pl.when(diagonal)
                def _():
                    await_tiles(R * (R + 1) // 2)

                @pl.when(jnp.logical_not(diagonal | lagging | inward))
                def _():
                    await_tiles(R * R)

            for k in (1, 2) if phase else (0,):
                if d:
                    second_leg(s, k).start()
                else:
                    ti, tj = regions[k]
                    pltpu.make_async_copy(mid.at[s, ti, tj], final.at[ti, tj, pl.ds(pos - zl, 2)], fin_recv.at[min(k, 1)]).start()

    compute_diagonal()
    s0(0)
    s1(0)
    for h in range(H // 2):
        pass_on(0, h)
    for k in range(R + 1):
        m = k + 1
        if k < R:
            for h in range(H // 2, H):
                pass_on(k, h)
            if k == 0:
                for r in range(2, R):
                    for h in range(H):
                        own_to(YP, r, h, to_ym).start()
        if k < R:
            have(ZP, k)
            for r in range(2 * k, 2 * k + 2 if k < 2 else 0):
                have(YP, r)
            compute_early(m)
        if k:
            have(T, k - 1)
            have(Y2, k - 1)
            compute_late(m)
        s0(m)
        if k == R:
            s3(m - 1)
            s1(m)
            s4(m - 1)
            s2(m)
            continue
        s2(m - 1)
        if k:
            s3(m - 2)
        s1(m)
        if k + 1 < R:
            for h in range(H // 2):
                pass_on(k + 1, h)
            continue
        s4(0)
        s2(m)
        for done in range(1, m - 1):
            s4(done)
        s3(m - 1)
        s4(m - 1)
    s3(NB - 1)
    s4(NB - 1)
    pass_final(0)
    pass_final(1)

    dy, dz = (c // 4 - y + 4) % 4, (c % 4 - z + 4) % 4

    def among(offsets):
        return functools.reduce(jnp.logical_or, [(dy == a) & (dz == b) for a, b in offsets])

    diagonal, halved, flip = among(((0, 0),)), among(HALVED), among(MIRRORED)
    scale = 1.0 / float(NC * cells)

    def write(i, j, tile):
        out[i * S : (i + 1) * S, j * S : (j + 1) * S] = tile

    def tile(i, j):
        return final[i, j].reshape(S, S) * scale

    first = R - 1
    for tiles in ([(i, j) for i in range(first) for j in range(first)], [(i, j) for i in range(R) for j in range(R) if first in (i, j)]):
        phase = int(len(tiles) < first * first)
        like = prods[2].at[0 : len(tiles)]
        pltpu.make_async_copy(like, like, fin_recv.at[phase]).wait()
        lower = [t for t in tiles if t[0] >= t[1]]
        above = [t for t in tiles if t[0] < t[1]]

        @pl.when(flip)
        def _():
            for i, j in tiles:
                write(j, i, tile(i, j).T)

        @pl.when(jnp.logical_not(flip))
        def _():
            for i, j in lower:
                write(i, j, tile(i, j))

        @pl.when(diagonal)
        def _():
            for i, j in lower:
                if i > j:
                    write(j, i, tile(i, j).T)

        @pl.when(halved)
        def _():
            for i, j in above:
                write(i, j, tile(i, j).T)

        @pl.when(jnp.logical_not(flip | diagonal | halved))
        def _():
            for i, j in above:
                write(i, j, tile(i, j))

    for k, buf in ((0, colbuf), (1, rowbuf), (2, totbuf)):
        others(buf, stat_send.at[k]).wait()
    sent = 0
    for r in range(R):
        for b in range(5):
            for h in range(H):
                own_to(b, r, h, to_zp).wait_send()
    for r in range(NB):
        core_copy(r).wait_send()
        for k in ("ep", "em", "dp", "dm", "fp", "fm"):
            x_copy(r, k).wait_send()
        zl_copy(r).wait_send()
        k = 0
        for src, ti, tj, row, col, maybe in final_sends(r):
            if maybe:

                @pl.when(col // 8 != zl)
                def _():
                    first_leg(r, src, ti, tj, row, col, fin_own.at[r, k]).wait_send()

                k += 1
            else:
                sent += src.shape[0]
    for d in range(1, 8):
        for k in range(3):
            second_leg((c % 8 + d) % 8, k).wait_send()
    assert sent % 16 == 0
    pltpu.make_async_copy(prods[2].at[0 : sent // 16], prods[2].at[0 : sent // 16], fin_send).wait()


def body(counts):
    cells, genes = counts.shape
    S = genes // R
    ns = [n for n, _ in ROUNDS]
    f32 = jnp.float32
    dma = pltpu.SemaphoreType.DMA
    own_groups = max(sum(PAIRS[gr[0]][0] == OWN for gr in groups) for _, groups in ROUNDS)
    scratch = [
        pltpu.VMEM((cells // 128, genes, 128), f32),
        pltpu.VMEM((NC, 8, 128), f32),
        pltpu.VMEM((NC, 8, 128), f32),
        pltpu.VMEM((NC, 8, 128), f32),
        pltpu.VMEM((R, S, cells), jnp.bfloat16),
        pltpu.VMEM((R, 5, S, cells), jnp.bfloat16),
        pltpu.VMEM((8, R, R, 2, S // 16, S), f32),
        pltpu.VMEM((R, R, 16, S // 16, S), f32),
        *[pltpu.VMEM((n, 8, S // 8, S), f32) for n in ns],
        *[pltpu.VMEM((n, 4, S // 8, S), f32) for n in ns],
        *[pltpu.VMEM((n, S // 8, S), f32) for n in ns],
        *[pltpu.VMEM((2, n, S // 8, S), f32) for n in ns],
        *[pltpu.VMEM((n, S // 16, S), f32) for n in ns],
        dma((3,)),
        dma((3,)),
        dma((5, R, H)),
        dma((5, R, H)),
        dma((NB, 8)),
        dma((NB, 8)),
        dma(()),
        dma((NB, own_groups)),
        dma((2, 8)),
        dma((3, 8)),
        dma((2,)),
    ]
    return pl.pallas_call(
        kernel,
        out_shape=jax.ShapeDtypeStruct((genes, genes), f32),
        in_specs=[pl.BlockSpec(memory_space=pltpu.VMEM)],
        out_specs=pl.BlockSpec(memory_space=pltpu.VMEM),
        scratch_shapes=scratch,
        compiler_params=pltpu.CompilerParams(
            collective_id=0, has_side_effects=True, vmem_limit_bytes=60 * 1024 * 1024
        ),
    )(counts)


def solution(mesh):
    return jax.shard_map(
        body,
        mesh=mesh,
        in_specs=(P("cell", "gene"),),
        out_specs=P("gene", "cell"),
        check_vma=False,
    )
```

```python
import functools

import jax
import jax.numpy as jnp
from jax import lax
from jax.experimental import pallas as pl
from jax.experimental.pallas import tpu as pltpu
from jax.sharding import PartitionSpec as P

MESH = pl.DeviceIdType.MESH
R = 4
H = 2
NC = 16
YP, ZP, T, Y2, ZM = range(5)
OWN = -1
OFFSET = {OWN: (0, 0), YP: (1, 0), ZP: (0, 1), T: (3, 3), Y2: (2, 3), ZM: (0, 3)}
PAIRS = (
    (OWN, OWN, None),
    (OWN, YP, "all"),
    (OWN, ZP, "all"),
    (YP, ZM, "all"),
    (OWN, Y2, "all"),
    (YP, ZP, "all"),
    (ZM, Y2, "below"),
    (ZP, T, "all"),
    (ZP, Y2, "below"),
    (ZP, ZM, "below"),
)
HALVED = ((2, 0), (0, 2), (2, 2))
MIRRORED = ((3, 0), (0, 3), (1, 1), (2, 1), (1, 3), (1, 2))


def whole_at(step):
    found = []
    if step < 2:
        found += [(1, r) for r in range(2 * step, 2 * step + 2)]
    if step < R:
        found += [(2, step)]
    if 0 < step < R:
        found += [(pair, r) for r in range(0 if step == 1 else step, step + 1) for pair in (3, 5)]
    if step:
        found += [(4, step - 1)]
    return found


def plan():
    batches = []
    for step in range(-1, R + 1):
        groups, n = [], 0

        def add(pair, count, i, j, along):
            nonlocal n
            groups.append((pair, n, count, i, j, along))
            n += count

        if step < 0:
            for i in range(R):
                add(0, i + 1, i, 0, "j")
        if step >= 0:
            for pair, r in whole_at(step):
                add(pair, R, 0, r, "i")
            if step < R:
                add(9, step + 1, step, 0, "j")
            if step:
                for pair in (6, 7, 8):
                    add(pair, step, step - 1, 0, "j")
                if step > 1:
                    add(7, step - 1, 0, step - 1, "i")
        batches.append((n, groups))
    return batches


ROUNDS = plan()
NB = len(ROUNDS)


def gene_at(y, z, offset):
    return ((y + offset[0]) % 4) * 4 + (z + offset[1]) % 4


def kernel(counts, out, *scratch):
    (vt, colbuf, rowbuf, totbuf, own, got, mid, final), rest = scratch[:8], scratch[8:]
    prods, rest = rest[:NB], rest[NB:]
    halves, rest = rest[:NB], rest[NB:]
    early, rest = rest[:NB], rest[NB:]
    late, rest = rest[:NB], rest[NB:]
    pieces, rest = rest[:NB], rest[NB:]
    (stat_send, stat_recv, in_send, in_recv, rs_send, rs_recv, fin_send, fin_own, mid_recv, mid_send, fin_recv) = rest
    genes, cells = own.shape[0] * own.shape[1], own.shape[2]
    S = genes // R
    nj = cells // 128
    c, g = lax.axis_index("cell"), lax.axis_index("gene")
    zl, x, core = c // 8, (c // 2) % 4, c % 2
    y, z = g // 4, g % 4
    pos = 8 * core + 2 * x + zl

    def cell_of(zl_, x_, core_):
        return {"cell": zl_ * 8 + x_ * 2 + core_}

    xp, xm = (x + 1) % 4, (x + 3) % 4
    to_xp, to_xm = cell_of(zl, xp, core), cell_of(zl, xm, core)
    to_core, to_zl = cell_of(zl, x, 1 - core), cell_of(1 - zl, x, core)
    to_yp, to_ym = {"gene": gene_at(y, z, (1, 0))}, {"gene": gene_at(y, z, (3, 0))}
    to_y2 = {"gene": gene_at(y, z, (2, 0))}
    to_zp, to_zm = {"gene": gene_at(y, z, (0, 1))}, {"gene": gene_at(y, z, (0, 3))}

    def remote(src, dst, ssem, rsem, device):
        return pltpu.make_async_remote_copy(
            src_ref=src, dst_ref=dst, send_sem=ssem, recv_sem=rsem, device_id=device, device_id_type=MESH
        )

    barrier = pltpu.get_barrier_semaphore()
    for k in range(1, NC):
        pl.semaphore_signal(barrier, inc=1, device_id={"cell": (c + k) % NC}, device_id_type=MESH)
        pl.semaphore_signal(barrier, inc=1, device_id={"gene": (g + k) % NC}, device_id_type=MESH)

    def local(j, acc):
        v = counts[pl.ds(j * 128, 128), :].astype(jnp.float32)
        t = v.T
        vt[j] = t
        rowbuf[g, pl.ds(j, 1), :] = jnp.sum(t, axis=0, keepdims=True)
        return acc + jnp.sum(v, axis=0, keepdims=True)

    nq = genes // 128
    colsum = lax.fori_loop(0, nj, local, jnp.zeros((1, genes), jnp.float32))
    colbuf[c] = jnp.zeros((8, 128), jnp.float32)
    for q in range(nq):
        colbuf[c, q : q + 1, :] = colsum[:, q * 128 : (q + 1) * 128]
    pl.semaphore_wait(barrier, 2 * (NC - 1))

    def spread(buf, axis, me, k):
        for d in range(1, NC):
            remote(buf.at[me], buf.at[me], stat_send.at[k], stat_recv.at[k], {axis: (me + d) % NC}).start()

    def others(buf, sem):
        return pltpu.make_async_copy(buf.at[0 : NC - 1], buf.at[0 : NC - 1], sem)

    spread(colbuf, "cell", c, 0)
    spread(rowbuf, "gene", g, 1)
    others(colbuf, stat_recv.at[0]).wait()
    totals = jnp.sum(colbuf[...], axis=0)
    totbuf[g] = jnp.broadcast_to(jnp.sum(totals, axis=0, keepdims=True), (8, 128))
    spread(totbuf, "gene", g, 2)
    gcol = [jnp.broadcast_to(totals[q : q + 1, :], (128, 128)).T for q in range(nq)]
    others(rowbuf, stat_recv.at[1]).wait()
    depths = jnp.sum(rowbuf[...], axis=0)
    others(totbuf, stat_recv.at[2]).wait()
    grand = jnp.sum(jnp.sum(totbuf[...], axis=0)[0:1, :])
    share = depths / grand
    ceiling = float(NC * cells) ** 0.5
    def part(h):
        return slice(h * (S // H), (h + 1) * (S // H))

    def own_to(b, r, h, device):
        return remote(own.at[r, part(h)], got.at[r, b, part(h)], in_send.at[b, r, h], in_recv.at[b, r, h], device)

    def arrived(b, r, h):
        own_to(b, r, h, to_zp).wait_recv()

    def pass_on(k, h):
        arrived(ZM, k, h)
        src = got.at[k, ZM, part(h)]
        for b, device in ((T, to_yp), (Y2, to_y2)) if h else ((T, to_yp),):
            remote(src, got.at[k, b, part(h)], in_send.at[b, k, h], in_recv.at[b, k, h], device).start()
        if h == H - 1:
            arrived(T, k, 0)
            src = got.at[k, T, part(0)]
            remote(src, got.at[k, Y2, part(0)], in_send.at[Y2, k, 0], in_recv.at[Y2, k, 0], to_yp).start()

    def have(b, r):
        for h in range(H):
            arrived(b, r, h)

    assert S == 128
    for r in range(R):
        for j in range(nj):
            v = vt[j, r * S : (r + 1) * S, :]
            e = gcol[r] * share[j : j + 1, :]
            t = (v - e) * lax.rsqrt(e + e * e / 100.0)
            own[r, :, j * 128 : (j + 1) * 128] = jnp.clip(t, -ceiling, ceiling).astype(jnp.bfloat16)
        for h in range(H):
            own_to(ZM, r, h, to_zp).start()
            own_to(ZP, r, h, to_zm).start()
        if r < 2:
            for h in range(H):
                own_to(YP, r, h, to_ym).start()

    def nt(a, b):
        return lax.dot_general(a, b, (((1,), (1,)), ((), ())), preferred_element_type=jnp.float32)

    def put(r, t, tile):
        prods[r][t] = tile.reshape(8, S // 8, S)

    def base_of(m):
        base = {}
        for pair, t0, n, i, j, along in ROUNDS[m][1]:
            base.setdefault((pair, along), t0)
        return base

    def compute_diagonal():
        for i in range(R):
            d = nt(own[i], own[0 : i + 1].reshape((i + 1) * S, cells))
            for j in range(i + 1):
                put(0, i * (i + 1) // 2 + j, d[:, j * S : (j + 1) * S])

    def whole(m, pairs):
        for a in (OWN, YP):
            cols = [(gr[1], gr[4], PAIRS[gr[0]][1]) for gr in ROUNDS[m][1] if gr[0] in pairs and PAIRS[gr[0]][0] == a]
            for two in (cols[k : k + 2] for k in range(0, len(cols), 2)):

                @pl.loop(0, R // 2)
                def _(i):
                    rows = pl.ds(2 * i, 2)
                    left = (own[rows] if a == OWN else got[rows, a]).reshape(2 * S, cells)
                    right = [got[j, b] for _, j, b in two]
                    d = nt(left, jnp.concatenate(right, axis=0) if len(two) > 1 else right[0])
                    for u in range(2):
                        for k, (t0, _, _) in enumerate(two):
                            put(m, t0 + 2 * i + u, d[u * S : (u + 1) * S, k * S : (k + 1) * S])

    def corner(m, pair, r):
        (a, b, _), t0 = PAIRS[pair], base_of(m)[pair, "j"]
        d = nt(got[r, a], got[0 : r + 1, b].reshape((r + 1) * S, cells))
        for j in range(r + 1):
            put(m, t0 + j, d[:, j * S : (j + 1) * S])

    def compute_early(m):
        whole(m, (1, 2, 3, 5))
        corner(m, 9, m - 1)

    def compute_late(m):
        base, l = base_of(m), m - 2
        whole(m, (4,))
        for pair in (6, 7, 8):
            corner(m, pair, l)
        if l:
            d = nt(got[0:l, ZP].reshape(l * S, cells), got[l, T])
            for i in range(l):
                put(m, base[7, "i"] + i, d[i * S : (i + 1) * S])

    def rs(r, k, src, dst, device):
        return remote(src, dst, rs_send.at[r, k], rs_recv.at[r, k], device)

    def core_copy(r):
        return rs(r, 0, prods[r].at[:, pl.ds(4 * (1 - core), 4)], halves[r], to_core)

    def x_copy(r, k):
        n = ROUNDS[r][0]
        a, b, p, h = slice(0, n // 2), slice(n // 2, n), prods[r], 4 * core
        if k == "ep":
            return rs(r, 1, p.at[a, h + (x + 2) % 4], early[r].at[a], to_xp)
        if k == "em":
            return rs(r, 2, p.at[b, h + (x + 2) % 4], early[r].at[b], to_xm)
        if k == "dp":
            return rs(r, 3, p.at[b, h + xp], late[r].at[0, b], to_xp)
        if k == "dm":
            return rs(r, 4, p.at[a, h + xm], late[r].at[1, a], to_xm)
        if k == "fp":
            return rs(r, 5, p.at[a, h + xp], late[r].at[0, a], to_xp)
        return rs(r, 6, p.at[b, h + xm], late[r].at[1, b], to_xm)

    def zl_copy(r):
        s = S // 16
        return rs(r, 7, prods[r].at[:, 4 * core + x, pl.ds((1 - zl) * s, s)], pieces[r], to_zl)

    def s0(r):
        core_copy(r).start()

    def s1(r):
        n = ROUNDS[r][0]
        core_copy(r).wait_recv()

        @pl.loop(0, n)
        def _(t):
            prods[r][t, pl.ds(4 * core, 4)] = prods[r][t, pl.ds(4 * core, 4)] + halves[r][t]

        for k in ("ep", "em", "dp", "dm"):
            x_copy(r, k).start()

    def s2(r):
        n = ROUNDS[r][0]
        a, b = slice(0, n // 2), slice(n // 2, n)
        x_copy(r, "ep").wait_recv()
        prods[r][a, 4 * core + xp] = prods[r][a, 4 * core + xp] + early[r][a]
        x_copy(r, "fp").start()
        x_copy(r, "em").wait_recv()
        prods[r][b, 4 * core + xm] = prods[r][b, 4 * core + xm] + early[r][b]
        x_copy(r, "fm").start()

    def s3(r):
        for k in ("dp", "dm", "fp", "fm"):
            x_copy(r, k).wait_recv()
        prods[r][:, 4 * core + x] = prods[r][:, 4 * core + x] + late[r][0] + late[r][1]
        zl_copy(r).start()

    def final_sends(r):
        for pair, t0, n, i, j, along in ROUNDS[r][1]:
            a, b, both = PAIRS[pair]
            ga, gb = gene_at(y, z, OFFSET[a]), gene_at(y, z, OFFSET[b])
            ti, tj = (i, slice(j, j + n)) if along == "j" else (slice(i, i + n), j)
            yield pieces[r].at[t0 : t0 + n], ti, tj, ga, gb, a == OWN
            if both == "all":
                yield pieces[r].at[t0 : t0 + n], ti, tj, gb, ga, False
            if both == "below" and i:
                yield pieces[r].at[t0 : t0 + i], slice(0, i), i, gb, ga, False

    def first_leg(r, src, ti, tj, row, col, sem):
        to = {"cell": (col // 8) * 8 + c % 8, "gene": row}
        return remote(src, mid.at[col % 8, ti, tj, zl], sem, mid_recv.at[r // (NB - 1), col % 8], to)

    def s4(r):
        s = S // 16
        zl_copy(r).wait_recv()
        pieces[r][...] = pieces[r][...] + prods[r][:, 4 * core + x, pl.ds(zl * s, s)]
        k = 0
        for src, ti, tj, row, col, maybe in final_sends(r):
            if maybe:

                @pl.when(col // 8 == zl)
                def _():
                    pltpu.make_async_copy(src, mid.at[col % 8, ti, tj, zl], mid_recv.at[r // (NB - 1), col % 8]).start()

                @pl.when(col // 8 != zl)
                def _():
                    first_leg(r, src, ti, tj, row, col, fin_own.at[r, k]).start()

                k += 1
            else:
                first_leg(r, src, ti, tj, row, col, fin_send).start()

    regions = ((slice(0, R - 1), slice(0, R - 1)), (R - 1, slice(0, R)), (slice(0, R - 1), R - 1))

    def second_leg(s, k):
        ti, tj = regions[k]
        dst = final.at[ti, tj, pl.ds(pos - zl, 2)]
        return remote(mid.at[s, ti, tj], dst, mid_send.at[k, s], fin_recv, {"cell": zl * 8 + s})

    def pass_final(phase):
        inner, rows = (R - 1) * (R - 1), R * (R - 1)
        for d in range(8):
            s = (c % 8 + d) % 8
            col = zl * 8 + s
            dy, dz = (col // 4 - y + 4) % 4, (col % 4 - z + 4) % 4
            diagonal = col == g
            lagging = (dy == 2) & ((dz == 1) | (dz == 3))
            inward = ((dz == 2) & (dy != 0)) | ((dz == 0) & (dy == 2))

            def await_tiles(n):
                like = late[2].at[0, 0:n]
                pltpu.make_async_copy(like, like, mid_recv.at[phase, s]).wait()

            @pl.when(lagging)
            def _():
                await_tiles(R if phase else rows)

            @pl.when(inward)
            def _():
                await_tiles(R * R - inner if phase else inner)

            if phase == 0:

                @pl.when(diagonal)
                def _():
                    await_tiles(R * (R + 1) // 2)

                @pl.when(jnp.logical_not(diagonal | lagging | inward))
                def _():
                    await_tiles(R * R)

            for k in (1, 2) if phase else (0,):
                if d:
                    second_leg(s, k).start()
                else:
                    ti, tj = regions[k]
                    pltpu.make_async_copy(mid.at[s, ti, tj], final.at[ti, tj, pl.ds(pos - zl, 2)], fin_recv).start()

    compute_diagonal()
    s0(0)
    s1(0)
    pass_on(0, 0)
    for k in range(R + 1):
        m = k + 1
        if k < R:
            for h in range(1, H):
                pass_on(k, h)
            if k == 0:
                for r in range(2, R):
                    for h in range(H):
                        own_to(YP, r, h, to_ym).start()
        if k < R:
            have(ZP, k)
            for r in range(2 * k, 2 * k + 2 if k < 2 else 0):
                have(YP, r)
            compute_early(m)
        if k:
            for h in range(1, H):
                arrived(T, k - 1, h)
            have(Y2, k - 1)
            compute_late(m)
        s0(m)
        if k == R:
            s1(m)
            s3(m - 1)
            s2(m)
            continue
        s2(m - 1)
        if k:
            s3(m - 2)
        s1(m)
        if k + 1 < R:
            pass_on(k + 1, 0)
            continue
        for done in range(m - 1):
            s4(done)
        s2(m)
        s3(m - 1)
        s4(m - 1)
    s4(NB - 2)
    s3(NB - 1)
    s4(NB - 1)
    pass_final(0)
    pass_final(1)

    pltpu.make_async_copy(final, final, fin_recv).wait()
    dy, dz = (c // 4 - y + 4) % 4, (c % 4 - z + 4) % 4

    def among(offsets):
        return functools.reduce(jnp.logical_or, [(dy == a) & (dz == b) for a, b in offsets])

    diagonal, halved, flip = among(((0, 0),)), among(HALVED), among(MIRRORED)
    scale = 1.0 / float(NC * cells)

    def write(i, j, tile):
        out[i * S : (i + 1) * S, j * S : (j + 1) * S] = tile

    def tile(i, j):
        return final[i, j].reshape(S, S) * scale

    below = [(i, j) for i in range(R) for j in range(i)]
    above = [(i, j) for j, i in below]
    even = [(i, i) for i in range(R)]

    @pl.when(diagonal)
    def _():
        for i, j in below:
            write(i, j, tile(i, j))
            write(j, i, tile(i, j).T)
        for i, j in even:
            write(i, j, tile(i, j))

    @pl.when(jnp.logical_not(diagonal))
    def _():

        @pl.when(flip)
        def _():
            for i, j in below + even + above:
                write(j, i, tile(i, j).T)

        @pl.when(jnp.logical_not(flip))
        def _():
            for i, j in below + even:
                write(i, j, tile(i, j))

            @pl.when(halved)
            def _():
                for i, j in above:
                    write(i, j, tile(i, j).T)

            @pl.when(jnp.logical_not(halved))
            def _():
                for i, j in above:
                    write(i, j, tile(i, j))

    for k, buf in ((0, colbuf), (1, rowbuf), (2, totbuf)):
        others(buf, stat_send.at[k]).wait()
    sent = 0
    for r in range(R):
        for b in range(5):
            for h in range(H):
                own_to(b, r, h, to_zp).wait_send()
    for r in range(NB):
        core_copy(r).wait_send()
        for k in ("ep", "em", "dp", "dm", "fp", "fm"):
            x_copy(r, k).wait_send()
        zl_copy(r).wait_send()
        k = 0
        for src, ti, tj, row, col, maybe in final_sends(r):
            if maybe:

                @pl.when(col // 8 != zl)
                def _():
                    first_leg(r, src, ti, tj, row, col, fin_own.at[r, k]).wait_send()

                k += 1
            else:
                sent += src.shape[0]
    for d in range(1, 8):
        for k in range(3):
            second_leg((c % 8 + d) % 8, k).wait_send()
    assert sent % 16 == 0
    pltpu.make_async_copy(prods[2].at[0 : sent // 16], prods[2].at[0 : sent // 16], fin_send).wait()


def body(counts):
    cells, genes = counts.shape
    S = genes // R
    ns = [n for n, _ in ROUNDS]
    f32 = jnp.float32
    dma = pltpu.SemaphoreType.DMA
    own_groups = max(sum(PAIRS[gr[0]][0] == OWN for gr in groups) for _, groups in ROUNDS)
    scratch = [
        pltpu.VMEM((cells // 128, genes, 128), f32),
        pltpu.VMEM((NC, 8, 128), f32),
        pltpu.VMEM((NC, 8, 128), f32),
        pltpu.VMEM((NC, 8, 128), f32),
        pltpu.VMEM((R, S, cells), jnp.bfloat16),
        pltpu.VMEM((R, 5, S, cells), jnp.bfloat16),
        pltpu.VMEM((8, R, R, 2, S // 16, S), f32),
        pltpu.VMEM((R, R, 16, S // 16, S), f32),
        *[pltpu.VMEM((n, 8, S // 8, S), f32) for n in ns],
        *[pltpu.VMEM((n, 4, S // 8, S), f32) for n in ns],
        *[pltpu.VMEM((n, S // 8, S), f32) for n in ns],
        *[pltpu.VMEM((2, n, S // 8, S), f32) for n in ns],
        *[pltpu.VMEM((n, S // 16, S), f32) for n in ns],
        dma((3,)),
        dma((3,)),
        dma((5, R, H)),
        dma((5, R, H)),
        dma((NB, 8)),
        dma((NB, 8)),
        dma(()),
        dma((NB, own_groups)),
        dma((2, 8)),
        dma((3, 8)),
        dma(()),
    ]
    return pl.pallas_call(
        kernel,
        out_shape=jax.ShapeDtypeStruct((genes, genes), f32),
        in_specs=[pl.BlockSpec(memory_space=pltpu.VMEM)],
        out_specs=pl.BlockSpec(memory_space=pltpu.VMEM),
        scratch_shapes=scratch,
        compiler_params=pltpu.CompilerParams(
            collective_id=0, has_side_effects=True, vmem_limit_bytes=60 * 1024 * 1024
        ),
    )(counts)


def solution(mesh):
    return jax.shard_map(
        body,
        mesh=mesh,
        in_specs=(P("cell", "gene"),),
        out_specs=P("gene", "cell"),
        check_vma=False,
    )
```

```python
import functools

import jax
import jax.numpy as jnp
from jax import lax
from jax.experimental import pallas as pl
from jax.experimental.pallas import tpu as pltpu
from jax.sharding import PartitionSpec as P

MESH = pl.DeviceIdType.MESH
R = 4
H = 2
NC = 16
YP, ZP, T, Y2, ZM = range(5)
OWN = -1
OFFSET = {OWN: (0, 0), YP: (1, 0), ZP: (0, 1), T: (3, 3), Y2: (2, 3), ZM: (0, 3)}
PAIRS = (
    (OWN, OWN, None),
    (OWN, YP, "all"),
    (OWN, ZP, "all"),
    (YP, ZM, "all"),
    (OWN, Y2, "all"),
    (YP, ZP, "all"),
    (ZM, Y2, "below"),
    (ZP, T, "all"),
    (ZP, Y2, "below"),
    (ZP, ZM, "below"),
)
HALVED = ((2, 0), (0, 2), (2, 2))
MIRRORED = ((3, 0), (0, 3), (1, 1), (2, 1), (1, 3), (1, 2))


def whole_at(step):
    found = []
    if step < 2:
        found += [(1, r) for r in range(2 * step, 2 * step + 2)]
    if step < R:
        found += [(2, step)]
    if 0 < step < R:
        found += [(pair, r) for r in range(0 if step == 1 else step, step + 1) for pair in (3, 5)]
    if step:
        found += [(4, step - 1)]
    return found


def plan():
    batches = []
    for step in range(-1, R + 1):
        groups, n = [], 0

        def add(pair, count, i, j, along):
            nonlocal n
            groups.append((pair, n, count, i, j, along))
            n += count

        if step < 0:
            for i in range(R):
                add(0, i + 1, i, 0, "j")
        if step >= 0:
            for pair, r in whole_at(step):
                add(pair, R, 0, r, "i")
            if step < R:
                add(9, step + 1, step, 0, "j")
            if step:
                for pair in (6, 7, 8):
                    add(pair, step, step - 1, 0, "j")
                if step > 1:
                    add(7, step - 1, 0, step - 1, "i")
        batches.append((n, groups))
    return batches


ROUNDS = plan()
NB = len(ROUNDS)


def gene_at(y, z, offset):
    return ((y + offset[0]) % 4) * 4 + (z + offset[1]) % 4


def kernel(counts_hbm, out, *scratch):
    (counts, counts_sem), scratch = scratch[:2], scratch[2:]
    (vt, colbuf, rowbuf, totbuf, own, got, mid, final), rest = scratch[:8], scratch[8:]
    prods, rest = rest[:NB], rest[NB:]
    halves, rest = rest[:NB], rest[NB:]
    early, rest = rest[:NB], rest[NB:]
    late, rest = rest[:NB], rest[NB:]
    pieces, rest = rest[:NB], rest[NB:]
    (stat_send, stat_recv, in_send, in_recv, rs_send, rs_recv, fin_send, fin_own, mid_recv, mid_send, fin_recv) = rest
    genes, cells = own.shape[0] * own.shape[1], own.shape[2]
    S = genes // R
    nj = cells // 128
    c, g = lax.axis_index("cell"), lax.axis_index("gene")
    zl, x, core = c // 8, (c // 2) % 4, c % 2
    y, z = g // 4, g % 4
    pos = 8 * core + 2 * x + zl

    def cell_of(zl_, x_, core_):
        return {"cell": zl_ * 8 + x_ * 2 + core_}

    xp, xm = (x + 1) % 4, (x + 3) % 4
    to_xp, to_xm = cell_of(zl, xp, core), cell_of(zl, xm, core)
    to_core, to_zl = cell_of(zl, x, 1 - core), cell_of(1 - zl, x, core)
    to_yp, to_ym = {"gene": gene_at(y, z, (1, 0))}, {"gene": gene_at(y, z, (3, 0))}
    to_y2 = {"gene": gene_at(y, z, (2, 0))}
    to_zp, to_zm = {"gene": gene_at(y, z, (0, 1))}, {"gene": gene_at(y, z, (0, 3))}

    def remote(src, dst, ssem, rsem, device):
        return pltpu.make_async_remote_copy(
            src_ref=src, dst_ref=dst, send_sem=ssem, recv_sem=rsem, device_id=device, device_id_type=MESH
        )

    load = pltpu.make_async_copy(counts_hbm, counts, counts_sem)
    load.start()
    barrier = pltpu.get_barrier_semaphore()
    for k in range(1, NC):
        pl.semaphore_signal(barrier, inc=1, device_id={"cell": (c + k) % NC}, device_id_type=MESH)
        pl.semaphore_signal(barrier, inc=1, device_id={"gene": (g + k) % NC}, device_id_type=MESH)

    load.wait()
    def local(j, acc):
        v = counts[pl.ds(j * 128, 128), :].astype(jnp.float32)
        t = v.T
        vt[j] = t
        rowbuf[g, pl.ds(j, 1), :] = jnp.sum(t, axis=0, keepdims=True)
        return acc + jnp.sum(v, axis=0, keepdims=True)

    nq = genes // 128
    colsum = lax.fori_loop(0, nj, local, jnp.zeros((1, genes), jnp.float32))
    colbuf[c] = jnp.zeros((8, 128), jnp.float32)
    for q in range(nq):
        colbuf[c, q : q + 1, :] = colsum[:, q * 128 : (q + 1) * 128]
    pl.semaphore_wait(barrier, 2 * (NC - 1))

    def spread(buf, axis, me, k):
        for d in range(1, NC):
            remote(buf.at[me], buf.at[me], stat_send.at[k], stat_recv.at[k], {axis: (me + d) % NC}).start()

    def others(buf, sem):
        return pltpu.make_async_copy(buf.at[0 : NC - 1], buf.at[0 : NC - 1], sem)

    spread(colbuf, "cell", c, 0)
    spread(rowbuf, "gene", g, 1)
    others(colbuf, stat_recv.at[0]).wait()
    totals = jnp.sum(colbuf[...], axis=0)
    totbuf[g] = jnp.broadcast_to(jnp.sum(totals, axis=0, keepdims=True), (8, 128))
    spread(totbuf, "gene", g, 2)
    gcol = [jnp.broadcast_to(totals[q : q + 1, :], (128, 128)).T for q in range(nq)]
    others(rowbuf, stat_recv.at[1]).wait()
    depths = jnp.sum(rowbuf[...], axis=0)
    others(totbuf, stat_recv.at[2]).wait()
    grand = jnp.sum(jnp.sum(totbuf[...], axis=0)[0:1, :])
    share = depths / grand
    ceiling = float(NC * cells) ** 0.5
    def part(h):
        return slice(h * (S // H), (h + 1) * (S // H))

    def own_to(b, r, h, device):
        return remote(own.at[r, part(h)], got.at[r, b, part(h)], in_send.at[b, r, h], in_recv.at[b, r, h], device)

    def arrived(b, r, h):
        own_to(b, r, h, to_zp).wait_recv()

    def pass_on(k, h):
        arrived(ZM, k, h)
        src = got.at[k, ZM, part(h)]
        for b, device in ((T, to_yp), (Y2, to_y2)):
            remote(src, got.at[k, b, part(h)], in_send.at[b, k, h], in_recv.at[b, k, h], device).start()

    def have(b, r):
        for h in range(H):
            arrived(b, r, h)

    assert S == 128
    for r in range(R):
        for j in range(nj):
            v = vt[j, r * S : (r + 1) * S, :]
            e = gcol[r] * share[j : j + 1, :]
            t = (v - e) * lax.rsqrt(e + e * e / 100.0)
            own[r, :, j * 128 : (j + 1) * 128] = jnp.clip(t, -ceiling, ceiling).astype(jnp.bfloat16)
        for h in range(H):
            own_to(ZM, r, h, to_zp).start()
            own_to(ZP, r, h, to_zm).start()
        if r < 2:
            for h in range(H):
                own_to(YP, r, h, to_ym).start()

    def nt(a, b):
        return lax.dot_general(a, b, (((1,), (1,)), ((), ())), preferred_element_type=jnp.float32)

    def put(r, t, tile):
        prods[r][t] = tile.reshape(8, S // 8, S)

    def base_of(m):
        base = {}
        for pair, t0, n, i, j, along in ROUNDS[m][1]:
            base.setdefault((pair, along), t0)
        return base

    def compute_diagonal():
        for i in range(R):
            d = nt(own[i], own[0 : i + 1].reshape((i + 1) * S, cells))
            for j in range(i + 1):
                put(0, i * (i + 1) // 2 + j, d[:, j * S : (j + 1) * S])

    def whole(m, pairs):
        for a in (OWN, YP):
            cols = [(gr[1], gr[4], PAIRS[gr[0]][1]) for gr in ROUNDS[m][1] if gr[0] in pairs and PAIRS[gr[0]][0] == a]
            for two in (cols[k : k + 2] for k in range(0, len(cols), 2)):

                @pl.loop(0, R // 2)
                def _(i):
                    rows = pl.ds(2 * i, 2)
                    left = (own[rows] if a == OWN else got[rows, a]).reshape(2 * S, cells)
                    right = [got[j, b] for _, j, b in two]
                    d = nt(left, jnp.concatenate(right, axis=0) if len(two) > 1 else right[0])
                    for u in range(2):
                        for k, (t0, _, _) in enumerate(two):
                            put(m, t0 + 2 * i + u, d[u * S : (u + 1) * S, k * S : (k + 1) * S])

    def corner(m, pair, r):
        (a, b, _), t0 = PAIRS[pair], base_of(m)[pair, "j"]
        d = nt(got[r, a], got[0 : r + 1, b].reshape((r + 1) * S, cells))
        for j in range(r + 1):
            put(m, t0 + j, d[:, j * S : (j + 1) * S])

    def compute_early(m):
        whole(m, (1, 2, 3, 5))
        corner(m, 9, m - 1)

    def compute_late(m):
        base, l = base_of(m), m - 2
        whole(m, (4,))
        for pair in (6, 7, 8):
            corner(m, pair, l)
        if l:
            d = nt(got[0:l, ZP].reshape(l * S, cells), got[l, T])
            for i in range(l):
                put(m, base[7, "i"] + i, d[i * S : (i + 1) * S])

    def rs(r, k, src, dst, device):
        return remote(src, dst, rs_send.at[r, k], rs_recv.at[r, k], device)

    def core_copy(r):
        return rs(r, 0, prods[r].at[:, pl.ds(4 * (1 - core), 4)], halves[r], to_core)

    def x_copy(r, k):
        n = ROUNDS[r][0]
        a, b, p, h = slice(0, n // 2), slice(n // 2, n), prods[r], 4 * core
        if k == "ep":
            return rs(r, 1, p.at[a, h + (x + 2) % 4], early[r].at[a], to_xp)
        if k == "em":
            return rs(r, 2, p.at[b, h + (x + 2) % 4], early[r].at[b], to_xm)
        if k == "dp":
            return rs(r, 3, p.at[b, h + xp], late[r].at[0, b], to_xp)
        if k == "dm":
            return rs(r, 4, p.at[a, h + xm], late[r].at[1, a], to_xm)
        if k == "fp":
            return rs(r, 5, p.at[a, h + xp], late[r].at[0, a], to_xp)
        return rs(r, 6, p.at[b, h + xm], late[r].at[1, b], to_xm)

    def zl_copy(r):
        s = S // 16
        return rs(r, 7, prods[r].at[:, 4 * core + x, pl.ds((1 - zl) * s, s)], pieces[r], to_zl)

    def s0(r):
        core_copy(r).start()

    def s1(r):
        n = ROUNDS[r][0]
        core_copy(r).wait_recv()

        @pl.loop(0, n)
        def _(t):
            prods[r][t, pl.ds(4 * core, 4)] = prods[r][t, pl.ds(4 * core, 4)] + halves[r][t]

        for k in ("ep", "em", "dp", "dm"):
            x_copy(r, k).start()

    def s2(r):
        n = ROUNDS[r][0]
        a, b = slice(0, n // 2), slice(n // 2, n)
        x_copy(r, "ep").wait_recv()
        prods[r][a, 4 * core + xp] = prods[r][a, 4 * core + xp] + early[r][a]
        x_copy(r, "fp").start()
        x_copy(r, "em").wait_recv()
        prods[r][b, 4 * core + xm] = prods[r][b, 4 * core + xm] + early[r][b]
        x_copy(r, "fm").start()

    def s3(r):
        for k in ("dp", "dm", "fp", "fm"):
            x_copy(r, k).wait_recv()
        prods[r][:, 4 * core + x] = prods[r][:, 4 * core + x] + late[r][0] + late[r][1]
        zl_copy(r).start()

    def final_sends(r):
        for pair, t0, n, i, j, along in ROUNDS[r][1]:
            a, b, both = PAIRS[pair]
            ga, gb = gene_at(y, z, OFFSET[a]), gene_at(y, z, OFFSET[b])
            ti, tj = (i, slice(j, j + n)) if along == "j" else (slice(i, i + n), j)
            yield pieces[r].at[t0 : t0 + n], ti, tj, ga, gb, a == OWN
            if both == "all":
                yield pieces[r].at[t0 : t0 + n], ti, tj, gb, ga, False
            if both == "below" and i:
                yield pieces[r].at[t0 : t0 + i], slice(0, i), i, gb, ga, False

    def first_leg(r, src, ti, tj, row, col, sem):
        to = {"cell": (col // 8) * 8 + c % 8, "gene": row}
        return remote(src, mid.at[col % 8, ti, tj, zl], sem, mid_recv.at[r // (NB - 1), col % 8], to)

    def s4(r):
        s = S // 16
        zl_copy(r).wait_recv()
        pieces[r][...] = pieces[r][...] + prods[r][:, 4 * core + x, pl.ds(zl * s, s)]
        k = 0
        for src, ti, tj, row, col, maybe in final_sends(r):
            if maybe:

                @pl.when(col // 8 == zl)
                def _():
                    pltpu.make_async_copy(src, mid.at[col % 8, ti, tj, zl], mid_recv.at[r // (NB - 1), col % 8]).start()

                @pl.when(col // 8 != zl)
                def _():
                    first_leg(r, src, ti, tj, row, col, fin_own.at[r, k]).start()

                k += 1
            else:
                first_leg(r, src, ti, tj, row, col, fin_send).start()

    regions = ((slice(0, R - 1), slice(0, R - 1)), (R - 1, slice(0, R)), (slice(0, R - 1), R - 1))

    def second_leg(s, k):
        ti, tj = regions[k]
        dst = final.at[ti, tj, pl.ds(pos - zl, 2)]
        return remote(mid.at[s, ti, tj], dst, mid_send.at[k, s], fin_recv, {"cell": zl * 8 + s})

    def pass_final(phase):
        inner, rows = (R - 1) * (R - 1), R * (R - 1)
        for d in range(8):
            s = (c % 8 + d) % 8
            col = zl * 8 + s
            dy, dz = (col // 4 - y + 4) % 4, (col % 4 - z + 4) % 4
            diagonal = col == g
            lagging = (dy == 2) & ((dz == 1) | (dz == 3))
            inward = ((dz == 2) & (dy != 0)) | ((dz == 0) & (dy == 2))

            def await_tiles(n):
                like = late[2].at[0, 0:n]
                pltpu.make_async_copy(like, like, mid_recv.at[phase, s]).wait()

            @pl.when(lagging)
            def _():
                await_tiles(R if phase else rows)

            @pl.when(inward)
            def _():
                await_tiles(R * R - inner if phase else inner)

            if phase == 0:

                @pl.when(diagonal)
                def _():
                    await_tiles(R * (R + 1) // 2)

                @pl.when(jnp.logical_not(diagonal | lagging | inward))
                def _():
                    await_tiles(R * R)

            for k in (1, 2) if phase else (0,):
                if d:
                    second_leg(s, k).start()
                else:
                    ti, tj = regions[k]
                    pltpu.make_async_copy(mid.at[s, ti, tj], final.at[ti, tj, pl.ds(pos - zl, 2)], fin_recv).start()

    compute_diagonal()
    s0(0)
    s1(0)
    pass_on(0, 0)
    for k in range(R + 1):
        m = k + 1
        if k < R:
            for h in range(1, H):
                pass_on(k, h)
            if k == 0:
                for r in range(2, R):
                    for h in range(H):
                        own_to(YP, r, h, to_ym).start()
        if k < R:
            have(ZP, k)
            for r in range(2 * k, 2 * k + 2 if k < 2 else 0):
                have(YP, r)
            compute_early(m)
        if k:
            have(T, k - 1)
            have(Y2, k - 1)
            compute_late(m)
        s0(m)
        if k == R:
            s1(m)
            s3(m - 1)
            s2(m)
            continue
        s2(m - 1)
        if k:
            s3(m - 2)
        s1(m)
        if k + 1 < R:
            pass_on(k + 1, 0)
            continue
        for done in range(m - 1):
            s4(done)
        s2(m)
        s3(m - 1)
        s4(m - 1)
    s4(NB - 2)
    s3(NB - 1)
    s4(NB - 1)
    pass_final(0)
    pass_final(1)

    pltpu.make_async_copy(final, final, fin_recv).wait()
    dy, dz = (c // 4 - y + 4) % 4, (c % 4 - z + 4) % 4

    def among(offsets):
        return functools.reduce(jnp.logical_or, [(dy == a) & (dz == b) for a, b in offsets])

    diagonal, halved, flip = among(((0, 0),)), among(HALVED), among(MIRRORED)

    def write(i, j, tile):
        out[i * S : (i + 1) * S, j * S : (j + 1) * S] = tile

    def tile(i, j):
        return final[i, j].reshape(S, S)

    below = [(i, j) for i in range(R) for j in range(i)]
    above = [(i, j) for j, i in below]
    even = [(i, i) for i in range(R)]

    @pl.when(diagonal)
    def _():
        for i, j in below:
            write(i, j, tile(i, j))
            write(j, i, tile(i, j).T)
        for i, j in even:
            write(i, j, tile(i, j))

    @pl.when(jnp.logical_not(diagonal))
    def _():

        @pl.when(flip)
        def _():
            for i, j in below + even + above:
                write(j, i, tile(i, j).T)

        @pl.when(jnp.logical_not(flip))
        def _():
            for i, j in below + even:
                write(i, j, tile(i, j))

            @pl.when(halved)
            def _():
                for i, j in above:
                    write(i, j, tile(i, j).T)

            @pl.when(jnp.logical_not(halved))
            def _():
                for i, j in above:
                    write(i, j, tile(i, j))

    for k, buf in ((0, colbuf), (1, rowbuf), (2, totbuf)):
        others(buf, stat_send.at[k]).wait()
    sent = 0
    for r in range(R):
        for b in range(5):
            for h in range(H):
                own_to(b, r, h, to_zp).wait_send()
    for r in range(NB):
        core_copy(r).wait_send()
        for k in ("ep", "em", "dp", "dm", "fp", "fm"):
            x_copy(r, k).wait_send()
        zl_copy(r).wait_send()
        k = 0
        for src, ti, tj, row, col, maybe in final_sends(r):
            if maybe:

                @pl.when(col // 8 != zl)
                def _():
                    first_leg(r, src, ti, tj, row, col, fin_own.at[r, k]).wait_send()

                k += 1
            else:
                sent += src.shape[0]
    for d in range(1, 8):
        for k in range(3):
            second_leg((c % 8 + d) % 8, k).wait_send()
    assert sent % 16 == 0
    pltpu.make_async_copy(prods[2].at[0 : sent // 16], prods[2].at[0 : sent // 16], fin_send).wait()


def body(counts):
    cells, genes = counts.shape
    S = genes // R
    ns = [n for n, _ in ROUNDS]
    f32 = jnp.float32
    dma = pltpu.SemaphoreType.DMA
    own_groups = max(sum(PAIRS[gr[0]][0] == OWN for gr in groups) for _, groups in ROUNDS)
    scratch = [
        pltpu.VMEM((cells, genes), jnp.int32),
        dma(()),
        pltpu.VMEM((cells // 128, genes, 128), f32),
        pltpu.VMEM((NC, 8, 128), f32),
        pltpu.VMEM((NC, 8, 128), f32),
        pltpu.VMEM((NC, 8, 128), f32),
        pltpu.VMEM((R, S, cells), jnp.bfloat16),
        pltpu.VMEM((R, 5, S, cells), jnp.bfloat16),
        pltpu.VMEM((8, R, R, 2, S // 16, S), f32),
        pltpu.VMEM((R, R, 16, S // 16, S), f32),
        *[pltpu.VMEM((n, 8, S // 8, S), f32) for n in ns],
        *[pltpu.VMEM((n, 4, S // 8, S), f32) for n in ns],
        *[pltpu.VMEM((n, S // 8, S), f32) for n in ns],
        *[pltpu.VMEM((2, n, S // 8, S), f32) for n in ns],
        *[pltpu.VMEM((n, S // 16, S), f32) for n in ns],
        dma((3,)),
        dma((3,)),
        dma((5, R, H)),
        dma((5, R, H)),
        dma((NB, 8)),
        dma((NB, 8)),
        dma(()),
        dma((NB, own_groups)),
        dma((2, 8)),
        dma((3, 8)),
        dma(()),
    ]
    total = pl.pallas_call(
        kernel,
        out_shape=jax.ShapeDtypeStruct((genes, genes), f32),
        in_specs=[pl.BlockSpec(memory_space=pl.ANY)],
        out_specs=pl.BlockSpec(memory_space=pltpu.VMEM),
        scratch_shapes=scratch,
        compiler_params=pltpu.CompilerParams(
            collective_id=0, has_side_effects=True, vmem_limit_bytes=60 * 1024 * 1024
        ),
    )(counts)
    return total / jnp.float32(NC * cells)


def solution(mesh):
    return jax.shard_map(
        body,
        mesh=mesh,
        in_specs=(P("cell", "gene"),),
        out_specs=P("gene", "cell"),
        check_vma=False,
    )
```

```python
import functools

import jax
import jax.numpy as jnp
from jax import lax
from jax.experimental import pallas as pl
from jax.experimental.pallas import tpu as pltpu
from jax.sharding import PartitionSpec as P

MESH = pl.DeviceIdType.MESH
R = 4
H = 2
NC = 16
YP, ZP, T, Y2, ZM = range(5)
OWN = -1
OFFSET = {OWN: (0, 0), YP: (1, 0), ZP: (0, 1), T: (3, 3), Y2: (2, 3), ZM: (0, 3)}
PAIRS = (
    (OWN, OWN, None),
    (OWN, YP, "all"),
    (OWN, ZP, "all"),
    (YP, ZM, "all"),
    (OWN, Y2, "all"),
    (YP, ZP, "all"),
    (ZM, Y2, "below"),
    (ZP, T, "all"),
    (ZP, Y2, "below"),
    (ZP, ZM, "below"),
)
HALVED = ((2, 0), (0, 2), (2, 2))
MIRRORED = ((3, 0), (0, 3), (1, 1), (2, 1), (1, 3), (1, 2))


def whole_at(step):
    found = []
    if step < 2:
        found += [(1, r) for r in range(2 * step, 2 * step + 2)]
    if step < R:
        found += [(2, step)]
    if 0 < step < R:
        found += [(pair, r) for r in range(0 if step == 1 else step, step + 1) for pair in (3, 5)]
    if step:
        found += [(4, step - 1)]
    return found


def plan():
    batches = []
    for step in range(-1, R + 1):
        groups, n = [], 0

        def add(pair, count, i, j, along):
            nonlocal n
            groups.append((pair, n, count, i, j, along))
            n += count

        if step < 0:
            for i in range(R):
                add(0, i + 1, i, 0, "j")
        if step >= 0:
            for pair, r in whole_at(step):
                add(pair, R, 0, r, "i")
            if step < R:
                add(9, step + 1, step, 0, "j")
            if step:
                for pair in (6, 7, 8):
                    add(pair, step, step - 1, 0, "j")
                if step > 1:
                    add(7, step - 1, 0, step - 1, "i")
        batches.append((n, groups))
    return batches


ROUNDS = plan()
NB = len(ROUNDS)


def gene_at(y, z, offset):
    return ((y + offset[0]) % 4) * 4 + (z + offset[1]) % 4


def kernel(counts_hbm, out, *scratch):
    (counts, counts_sem), scratch = scratch[:2], scratch[2:]
    (vt, colbuf, rowbuf, totbuf, own, got, mid, final), rest = scratch[:8], scratch[8:]
    prods, rest = rest[:NB], rest[NB:]
    halves, rest = rest[:NB], rest[NB:]
    early, rest = rest[:NB], rest[NB:]
    late, rest = rest[:NB], rest[NB:]
    pieces, rest = rest[:NB], rest[NB:]
    (stat_send, stat_recv, in_send, in_recv, rs_send, rs_recv, fin_send, fin_own, mid_recv, mid_send, fin_recv) = rest
    genes, cells = own.shape[0] * own.shape[1], own.shape[2]
    S = genes // R
    nj = cells // 128
    c, g = lax.axis_index("cell"), lax.axis_index("gene")
    zl, x, core = c // 8, (c // 2) % 4, c % 2
    y, z = g // 4, g % 4
    pos = 8 * core + 2 * x + zl

    def cell_of(zl_, x_, core_):
        return {"cell": zl_ * 8 + x_ * 2 + core_}

    xp, xm = (x + 1) % 4, (x + 3) % 4
    to_xp, to_xm = cell_of(zl, xp, core), cell_of(zl, xm, core)
    to_core, to_zl = cell_of(zl, x, 1 - core), cell_of(1 - zl, x, core)
    to_yp, to_ym = {"gene": gene_at(y, z, (1, 0))}, {"gene": gene_at(y, z, (3, 0))}
    to_y2 = {"gene": gene_at(y, z, (2, 0))}
    to_zp, to_zm = {"gene": gene_at(y, z, (0, 1))}, {"gene": gene_at(y, z, (0, 3))}

    def remote(src, dst, ssem, rsem, device):
        return pltpu.make_async_remote_copy(
            src_ref=src, dst_ref=dst, send_sem=ssem, recv_sem=rsem, device_id=device, device_id_type=MESH
        )

    load = pltpu.make_async_copy(counts_hbm, counts, counts_sem)
    load.start()
    barrier = pltpu.get_barrier_semaphore()
    for k in range(1, NC):
        pl.semaphore_signal(barrier, inc=1, device_id={"cell": (c + k) % NC}, device_id_type=MESH)
        pl.semaphore_signal(barrier, inc=1, device_id={"gene": (g + k) % NC}, device_id_type=MESH)

    load.wait()
    def local(j, acc):
        v = counts[pl.ds(j * 128, 128), :].astype(jnp.float32)
        t = v.T
        vt[j] = t
        rowbuf[g, pl.ds(j, 1), :] = jnp.sum(t, axis=0, keepdims=True)
        return acc + jnp.sum(v, axis=0, keepdims=True)

    nq = genes // 128
    colsum = lax.fori_loop(0, nj, local, jnp.zeros((1, genes), jnp.float32))
    colbuf[c] = jnp.zeros((8, 128), jnp.float32)
    for q in range(nq):
        colbuf[c, q : q + 1, :] = colsum[:, q * 128 : (q + 1) * 128]
    pl.semaphore_wait(barrier, 2 * (NC - 1))

    def spread(buf, axis, me, k):
        for d in range(1, NC):
            remote(buf.at[me], buf.at[me], stat_send.at[k], stat_recv.at[k], {axis: (me + d) % NC}).start()

    def others(buf, sem):
        return pltpu.make_async_copy(buf.at[0 : NC - 1], buf.at[0 : NC - 1], sem)

    spread(colbuf, "cell", c, 0)
    spread(rowbuf, "gene", g, 1)
    others(colbuf, stat_recv.at[0]).wait()
    totals = jnp.sum(colbuf[...], axis=0)
    totbuf[g] = jnp.broadcast_to(jnp.sum(totals, axis=0, keepdims=True), (8, 128))
    spread(totbuf, "gene", g, 2)
    gcol = [jnp.broadcast_to(totals[q : q + 1, :], (128, 128)).T for q in range(nq)]
    others(rowbuf, stat_recv.at[1]).wait()
    depths = jnp.sum(rowbuf[...], axis=0)
    others(totbuf, stat_recv.at[2]).wait()
    grand = jnp.sum(jnp.sum(totbuf[...], axis=0)[0:1, :])
    share = depths / grand
    ceiling = float(NC * cells) ** 0.5
    def part(h):
        return slice(h * (S // H), (h + 1) * (S // H))

    def own_to(b, r, h, device):
        return remote(own.at[r, part(h)], got.at[r, b, part(h)], in_send.at[b, r, h], in_recv.at[b, r, h], device)

    def arrived(b, r, h):
        own_to(b, r, h, to_zp).wait_recv()

    def pass_on(k, h):
        arrived(ZM, k, h)
        src = got.at[k, ZM, part(h)]
        for b, device in ((T, to_yp), (Y2, to_y2)):
            remote(src, got.at[k, b, part(h)], in_send.at[b, k, h], in_recv.at[b, k, h], device).start()

    def have(b, r):
        for h in range(H):
            arrived(b, r, h)

    assert S == 128
    for r in range(R):
        for j in range(nj):
            v = vt[j, r * S : (r + 1) * S, :]
            e = gcol[r] * share[j : j + 1, :]
            t = (v - e) * lax.rsqrt(e + e * e / 100.0)
            own[r, :, j * 128 : (j + 1) * 128] = jnp.clip(t, -ceiling, ceiling).astype(jnp.bfloat16)
        for h in range(H):
            own_to(ZM, r, h, to_zp).start()
            own_to(ZP, r, h, to_zm).start()
        if r < 2:
            for h in range(H):
                own_to(YP, r, h, to_ym).start()

    def nt(a, b):
        return lax.dot_general(a, b, (((1,), (1,)), ((), ())), preferred_element_type=jnp.float32)

    def put(r, t, tile):
        prods[r][t] = tile.reshape(8, S // 8, S)

    def base_of(m):
        base = {}
        for pair, t0, n, i, j, along in ROUNDS[m][1]:
            base.setdefault((pair, along), t0)
        return base

    def compute_diagonal():
        for i in range(R):
            d = nt(own[i], own[0 : i + 1].reshape((i + 1) * S, cells))
            for j in range(i + 1):
                put(0, i * (i + 1) // 2 + j, d[:, j * S : (j + 1) * S])

    def whole(m, pairs):
        for a in (OWN, YP):
            cols = [(gr[1], gr[4], PAIRS[gr[0]][1]) for gr in ROUNDS[m][1] if gr[0] in pairs and PAIRS[gr[0]][0] == a]
            for two in (cols[k : k + 2] for k in range(0, len(cols), 2)):

                @pl.loop(0, R // 2)
                def _(i):
                    rows = pl.ds(2 * i, 2)
                    left = (own[rows] if a == OWN else got[rows, a]).reshape(2 * S, cells)
                    right = [got[j, b] for _, j, b in two]
                    d = nt(left, jnp.concatenate(right, axis=0) if len(two) > 1 else right[0])
                    for u in range(2):
                        for k, (t0, _, _) in enumerate(two):
                            put(m, t0 + 2 * i + u, d[u * S : (u + 1) * S, k * S : (k + 1) * S])

    def corner(m, pair, r):
        (a, b, _), t0 = PAIRS[pair], base_of(m)[pair, "j"]
        d = nt(got[r, a], got[0 : r + 1, b].reshape((r + 1) * S, cells))
        for j in range(r + 1):
            put(m, t0 + j, d[:, j * S : (j + 1) * S])

    def compute_early(m):
        whole(m, (1, 2, 3, 5))
        corner(m, 9, m - 1)

    def compute_late(m):
        base, l = base_of(m), m - 2
        whole(m, (4,))
        for pair in (6, 7, 8):
            corner(m, pair, l)
        if l:
            d = nt(got[0:l, ZP].reshape(l * S, cells), got[l, T])
            for i in range(l):
                put(m, base[7, "i"] + i, d[i * S : (i + 1) * S])

    def rs(r, k, src, dst, device):
        return remote(src, dst, rs_send.at[r, k], rs_recv.at[r, k], device)

    def core_copy(r):
        return rs(r, 0, prods[r].at[:, pl.ds(4 * (1 - core), 4)], halves[r], to_core)

    def x_copy(r, k):
        n = ROUNDS[r][0]
        a, b, p, h = slice(0, n // 2), slice(n // 2, n), prods[r], 4 * core
        if k == "ep":
            return rs(r, 1, p.at[a, h + (x + 2) % 4], early[r].at[a], to_xp)
        if k == "em":
            return rs(r, 2, p.at[b, h + (x + 2) % 4], early[r].at[b], to_xm)
        if k == "dp":
            return rs(r, 3, p.at[b, h + xp], late[r].at[0, b], to_xp)
        if k == "dm":
            return rs(r, 4, p.at[a, h + xm], late[r].at[1, a], to_xm)
        if k == "fp":
            return rs(r, 5, p.at[a, h + xp], late[r].at[0, a], to_xp)
        return rs(r, 6, p.at[b, h + xm], late[r].at[1, b], to_xm)

    def zl_copy(r):
        s = S // 16
        return rs(r, 7, prods[r].at[:, 4 * core + x, pl.ds((1 - zl) * s, s)], pieces[r], to_zl)

    def s0(r):
        core_copy(r).start()

    def s1(r):
        n = ROUNDS[r][0]
        core_copy(r).wait_recv()

        @pl.loop(0, n)
        def _(t):
            prods[r][t, pl.ds(4 * core, 4)] = prods[r][t, pl.ds(4 * core, 4)] + halves[r][t]

        for k in ("ep", "em", "dp", "dm"):
            x_copy(r, k).start()

    def s2(r):
        n = ROUNDS[r][0]
        a, b = slice(0, n // 2), slice(n // 2, n)
        x_copy(r, "ep").wait_recv()
        prods[r][a, 4 * core + xp] = prods[r][a, 4 * core + xp] + early[r][a]
        x_copy(r, "fp").start()
        x_copy(r, "em").wait_recv()
        prods[r][b, 4 * core + xm] = prods[r][b, 4 * core + xm] + early[r][b]
        x_copy(r, "fm").start()

    def s3(r):
        for k in ("dp", "dm", "fp", "fm"):
            x_copy(r, k).wait_recv()
        prods[r][:, 4 * core + x] = prods[r][:, 4 * core + x] + late[r][0] + late[r][1]
        zl_copy(r).start()

    def final_sends(r):
        for pair, t0, n, i, j, along in ROUNDS[r][1]:
            a, b, both = PAIRS[pair]
            ga, gb = gene_at(y, z, OFFSET[a]), gene_at(y, z, OFFSET[b])
            ti, tj = (i, slice(j, j + n)) if along == "j" else (slice(i, i + n), j)
            yield pieces[r].at[t0 : t0 + n], ti, tj, ga, gb, a == OWN
            if both == "all":
                yield pieces[r].at[t0 : t0 + n], ti, tj, gb, ga, False
            if both == "below" and i:
                yield pieces[r].at[t0 : t0 + i], slice(0, i), i, gb, ga, False

    def first_leg(r, src, ti, tj, row, col, sem):
        to = {"cell": (col // 8) * 8 + c % 8, "gene": row}
        return remote(src, mid.at[col % 8, ti, tj, zl], sem, mid_recv.at[r // (NB - 1), col % 8], to)

    def s4(r):
        s = S // 16
        zl_copy(r).wait_recv()
        pieces[r][...] = pieces[r][...] + prods[r][:, 4 * core + x, pl.ds(zl * s, s)]
        k = 0
        for src, ti, tj, row, col, maybe in final_sends(r):
            if maybe:

                @pl.when(col // 8 == zl)
                def _():
                    pltpu.make_async_copy(src, mid.at[col % 8, ti, tj, zl], mid_recv.at[r // (NB - 1), col % 8]).start()

                @pl.when(col // 8 != zl)
                def _():
                    first_leg(r, src, ti, tj, row, col, fin_own.at[r, k]).start()

                k += 1
            else:
                first_leg(r, src, ti, tj, row, col, fin_send).start()

    regions = ((slice(0, R - 1), slice(0, R - 1)), (R - 1, slice(0, R)), (slice(0, R - 1), R - 1))

    def second_leg(s, k):
        ti, tj = regions[k]
        dst = final.at[ti, tj, pl.ds(pos - zl, 2)]
        return remote(mid.at[s, ti, tj], dst, mid_send.at[k, s], fin_recv, {"cell": zl * 8 + s})

    def pass_final(phase):
        inner, rows = (R - 1) * (R - 1), R * (R - 1)
        for d in range(8):
            s = (c % 8 + d) % 8
            col = zl * 8 + s
            dy, dz = (col // 4 - y + 4) % 4, (col % 4 - z + 4) % 4
            diagonal = col == g
            lagging = (dy == 2) & ((dz == 1) | (dz == 3))
            inward = ((dz == 2) & (dy != 0)) | ((dz == 0) & (dy == 2))

            def await_tiles(n):
                like = late[2].at[0, 0:n]
                pltpu.make_async_copy(like, like, mid_recv.at[phase, s]).wait()

            @pl.when(lagging)
            def _():
                await_tiles(R if phase else rows)

            @pl.when(inward)
            def _():
                await_tiles(R * R - inner if phase else inner)

            if phase == 0:

                @pl.when(diagonal)
                def _():
                    await_tiles(R * (R + 1) // 2)

                @pl.when(jnp.logical_not(diagonal | lagging | inward))
                def _():
                    await_tiles(R * R)

            for k in (1, 2) if phase else (0,):
                if d:
                    second_leg(s, k).start()
                else:
                    ti, tj = regions[k]
                    pltpu.make_async_copy(mid.at[s, ti, tj], final.at[ti, tj, pl.ds(pos - zl, 2)], fin_recv).start()

    compute_diagonal()
    s0(0)
    s1(0)
    pass_on(0, 0)
    for k in range(R + 1):
        m = k + 1
        if k < R:
            for h in range(1, H):
                pass_on(k, h)
            if k == 0:
                for r in range(2, R):
                    for h in range(H):
                        own_to(YP, r, h, to_ym).start()
        if k < R:
            have(ZP, k)
            for r in range(2 * k, 2 * k + 2 if k < 2 else 0):
                have(YP, r)
            compute_early(m)
        if k:
            have(T, k - 1)
            have(Y2, k - 1)
            compute_late(m)
        s0(m)
        if k == R:
            s3(m - 1)
            s1(m)
            s4(m - 1)
            s2(m)
            continue
        s2(m - 1)
        if k:
            s3(m - 2)
        s1(m)
        if k + 1 < R:
            pass_on(k + 1, 0)
            continue
        for done in range(m - 1):
            s4(done)
        s2(m)
        s3(m - 1)
        s4(m - 1)
    s3(NB - 1)
    s4(NB - 1)
    pass_final(0)
    pass_final(1)

    pltpu.make_async_copy(final, final, fin_recv).wait()
    dy, dz = (c // 4 - y + 4) % 4, (c % 4 - z + 4) % 4

    def among(offsets):
        return functools.reduce(jnp.logical_or, [(dy == a) & (dz == b) for a, b in offsets])

    diagonal, halved, flip = among(((0, 0),)), among(HALVED), among(MIRRORED)

    def write(i, j, tile):
        out[i * S : (i + 1) * S, j * S : (j + 1) * S] = tile

    def tile(i, j):
        return final[i, j].reshape(S, S)

    below = [(i, j) for i in range(R) for j in range(i)]
    above = [(i, j) for j, i in below]
    even = [(i, i) for i in range(R)]

    @pl.when(diagonal)
    def _():
        for i, j in below:
            write(i, j, tile(i, j))
            write(j, i, tile(i, j).T)
        for i, j in even:
            write(i, j, tile(i, j))

    @pl.when(jnp.logical_not(diagonal))
    def _():

        @pl.when(flip)
        def _():
            for i, j in below + even + above:
                write(j, i, tile(i, j).T)

        @pl.when(jnp.logical_not(flip))
        def _():
            for i, j in below + even:
                write(i, j, tile(i, j))

            @pl.when(halved)
            def _():
                for i, j in above:
                    write(i, j, tile(i, j).T)

            @pl.when(jnp.logical_not(halved))
            def _():
                for i, j in above:
                    write(i, j, tile(i, j))

    for k, buf in ((0, colbuf), (1, rowbuf), (2, totbuf)):
        others(buf, stat_send.at[k]).wait()
    sent = 0
    for r in range(R):
        for b in range(5):
            for h in range(H):
                own_to(b, r, h, to_zp).wait_send()
    for r in range(NB):
        core_copy(r).wait_send()
        for k in ("ep", "em", "dp", "dm", "fp", "fm"):
            x_copy(r, k).wait_send()
        zl_copy(r).wait_send()
        k = 0
        for src, ti, tj, row, col, maybe in final_sends(r):
            if maybe:

                @pl.when(col // 8 != zl)
                def _():
                    first_leg(r, src, ti, tj, row, col, fin_own.at[r, k]).wait_send()

                k += 1
            else:
                sent += src.shape[0]
    for d in range(1, 8):
        for k in range(3):
            second_leg((c % 8 + d) % 8, k).wait_send()
    assert sent % 16 == 0
    pltpu.make_async_copy(prods[2].at[0 : sent // 16], prods[2].at[0 : sent // 16], fin_send).wait()


def body(counts):
    cells, genes = counts.shape
    S = genes // R
    ns = [n for n, _ in ROUNDS]
    f32 = jnp.float32
    dma = pltpu.SemaphoreType.DMA
    own_groups = max(sum(PAIRS[gr[0]][0] == OWN for gr in groups) for _, groups in ROUNDS)
    scratch = [
        pltpu.VMEM((cells, genes), jnp.int32),
        dma(()),
        pltpu.VMEM((cells // 128, genes, 128), f32),
        pltpu.VMEM((NC, 8, 128), f32),
        pltpu.VMEM((NC, 8, 128), f32),
        pltpu.VMEM((NC, 8, 128), f32),
        pltpu.VMEM((R, S, cells), jnp.bfloat16),
        pltpu.VMEM((R, 5, S, cells), jnp.bfloat16),
        pltpu.VMEM((8, R, R, 2, S // 16, S), f32),
        pltpu.VMEM((R, R, 16, S // 16, S), f32),
        *[pltpu.VMEM((n, 8, S // 8, S), f32) for n in ns],
        *[pltpu.VMEM((n, 4, S // 8, S), f32) for n in ns],
        *[pltpu.VMEM((n, S // 8, S), f32) for n in ns],
        *[pltpu.VMEM((2, n, S // 8, S), f32) for n in ns],
        *[pltpu.VMEM((n, S // 16, S), f32) for n in ns],
        dma((3,)),
        dma((3,)),
        dma((5, R, H)),
        dma((5, R, H)),
        dma((NB, 8)),
        dma((NB, 8)),
        dma(()),
        dma((NB, own_groups)),
        dma((2, 8)),
        dma((3, 8)),
        dma(()),
    ]
    total = pl.pallas_call(
        kernel,
        out_shape=jax.ShapeDtypeStruct((genes, genes), f32),
        in_specs=[pl.BlockSpec(memory_space=pl.ANY)],
        out_specs=pl.BlockSpec(memory_space=pltpu.VMEM),
        scratch_shapes=scratch,
        compiler_params=pltpu.CompilerParams(
            collective_id=0, has_side_effects=True, vmem_limit_bytes=60 * 1024 * 1024
        ),
    )(counts)
    return total / jnp.float32(NC * cells)


def solution(mesh):
    return jax.shard_map(
        body,
        mesh=mesh,
        in_specs=(P("cell", "gene"),),
        out_specs=P("gene", "cell"),
        check_vma=False,
    )
```
